128 devices in a mesh: src: 8 (over z_hi, y), obs: 16 (over x, z_lo, core).
Axes of the slice: x: 4, y: 4, z: 4 (z_hi: 2, z_lo: 2; z = z_hi * 2 + z_lo), core: 2. Of those that a mesh axis runs over, the one named last changes fastest.
Arguments:
- tiles: bfloat16 [8, 16, 512, 128, 128], P('src', 'obs'), may hold values from -0.25 to 0.25
- tile_index: int32 [8, 16, 3, 512], P('src', 'obs'), may hold values from 0 to 1023, as said below
- tile_count: int32 [8, 16], P('src', 'obs'), may hold values from 64 to 512, as said below
- history: bfloat16 [16, 4, 1048576], P(None, None, ('src', 'obs')), may hold values from -6 to 6
- incident: float32 [2, 4, 1048576], P(None, None, ('src', 'obs')), may hold values from -6 to 6
- near_inverse: bfloat16 [8192, 128, 128], P(('src', 'obs')), may hold values from -0.5 to 0.5
Outputs:
- densities: bfloat16 [2, 4, 1048576], P(None, None, ('src', 'obs'))
The draws below stay inside these ranges and needn't reach their ends.
Inputs may be any that keep to these rules, and one draw needn't show every extreme that they name: `tile_index`: row 0 is an observer block among the 512 of a device, row 1 a source block among its 1024, row 2 a delay slot below 16; slots at or past the device's count are padding; a tile may repeat. `tile_count`: live tile slots of each device, the first ones of its list.
All inputs are finite; a program needn't handle non-finite values.
Results may differ from the reference program's by a relative error of at most 0.005.
Values may be sent and summed in bfloat16 or wider, within the bound.
A program may use at most 128 MiB of HBM per device.

```python
import jax
import jax.numpy as jnp
from jax import lax

TB = 128
NC = 4
HISTORY = 16
BD = 64
TILES_DEV = 512
OBS_BLOCKS = 512
SRC_BLOCKS = 1024
NB = 8192
PATCHES = 1048576
N_SRC = 8
N_OBS = 16


def draw_tile_index(key, part):
    key_observer = jax.random.fold_in(key, 11)
    key_source = jax.random.fold_in(key, 12)
    key_delay = jax.random.fold_in(key, 13)
    grid_shape = (N_SRC, N_OBS, 1, TILES_DEV)
    observer = jax.random.randint(key_observer, grid_shape, 0, OBS_BLOCKS)
    source = jax.random.randint(key_source, grid_shape, 0, SRC_BLOCKS)
    delay_slot = jax.random.randint(key_delay, grid_shape, 0, HISTORY)
    return jnp.concatenate([observer, source, delay_slot], axis=2).astype(jnp.int32)


def draw_tile_count(key, part):
    key_level = jax.random.fold_in(key, 21)
    key_highest = jax.random.fold_in(key, 22)
    key_lowest = jax.random.fold_in(key, 23)
    devices_all = N_SRC * N_OBS
    levels = jax.random.randint(key_level, (devices_all,), 0, 4)
    counts = jnp.right_shift(jnp.full((devices_all,), TILES_DEV, jnp.int32), levels.astype(jnp.int32))
    highest = jax.random.randint(key_highest, (), 0, devices_all)
    lowest = (highest + 1 + jax.random.randint(key_lowest, (), 0, devices_all - 1)) % devices_all
    places = jnp.arange(devices_all, dtype=jnp.int32)
    counts = jnp.where(places == highest, TILES_DEV, counts)
    counts = jnp.where(places == lowest, TILES_DEV // 8, counts)
    return counts.reshape(N_SRC, N_OBS).astype(jnp.int32)


def steps_of(key, extent, pieces, least, high):
    def one(dim, blocks):
        draws = jax.random.uniform(jax.random.fold_in(jax.random.fold_in(key, 6), dim), (blocks,), jnp.float32, least / len(pieces), high / len(pieces))
        return jnp.repeat(jnp.exp(draws), extent[dim] // blocks).reshape((-1,) + (1,) * (len(extent) - dim - 1))

    factor_of = one(*pieces[0])
    for cut in pieces[1:]:
        factor_of = factor_of * one(*cut)
    return factor_of


def bell_draw(own_key, shape, width, most, cuts=(), kind=jnp.bfloat16):
    gain = steps_of(own_key, shape, cuts, -0.22, 0.18) if cuts else 1.0
    drawn = jax.random.normal(own_key, shape, jnp.float32) * width * gain
    return jnp.minimum(jnp.maximum(drawn, -most), most).astype(kind)


def setup_inputs(seed: int = 0) -> dict:
    arg_keys = jax.random.split(jax.random.key(seed), 7)
    return {
        "tiles": bell_draw(arg_keys[0], (N_SRC, N_OBS, TILES_DEV, TB, TB), (TB * max(1, TILES_DEV // (2 * BD))) ** -0.5, 0.25, ((0, 8), (1, 16))),
        "tile_index": draw_tile_index(jax.random.fold_in(arg_keys[6], 71), 0),
        "tile_count": draw_tile_count(jax.random.fold_in(arg_keys[6], 71), 0),
        "history": bell_draw(arg_keys[3], (HISTORY, NC, PATCHES), 1.0, 6.0, ((2, 128),)),
        "incident": bell_draw(arg_keys[4], (2, NC, PATCHES), 1.0, 6.0, ((2, 128),), jnp.float32),
        "near_inverse": bell_draw(arg_keys[5], (NB, TB, TB), TB ** -0.5, 0.5, ((0, 128),)),
    }


def scattered_field(slot_data, tiles, tile_index, tile_count):
    block_view = slot_data.reshape(slot_data.shape[0], NC, NB, TB)
    flat_tiles = tiles.reshape(N_SRC * N_OBS, TILES_DEV, TB, TB)
    flat_index = tile_index.reshape(N_SRC * N_OBS, 3, TILES_DEV)
    flat_count = tile_count.reshape(N_SRC * N_OBS)
    device_ids = jnp.arange(N_SRC * N_OBS, dtype=jnp.int32)

    def add_device(accumulated, carried):
        tiles_here, index_here, count_here, device = carried
        source_axis = device // N_OBS
        observer_axis = device % N_OBS
        observer_local = index_here[0]
        observer_global = (observer_local // BD) * SRC_BLOCKS + observer_axis * BD + observer_local % BD
        source_global = source_axis * SRC_BLOCKS + index_here[1]
        picked = block_view[index_here[2], :, source_global]
        products = jnp.einsum("tck,tki->tci", picked.astype(jnp.float32), tiles_here.astype(jnp.float32))
        alive_mask = (jnp.arange(TILES_DEV, dtype=jnp.int32) < count_here).astype(jnp.float32)
        products = products * alive_mask[:, None, None]
        return accumulated.at[observer_global].add(products), None

    accumulated = jnp.zeros((NB, NC, TB), jnp.float32)
    accumulated, _ = lax.scan(add_device, accumulated, (flat_tiles, flat_index, flat_count, device_ids))
    return jnp.transpose(accumulated, (1, 0, 2)).reshape(NC, NB * TB)


def near_solve(drive, near_inverse):
    drive_rows = lax.optimization_barrier(drive.astype(jnp.bfloat16)).reshape(NC, NB, TB)
    solved = jnp.einsum("cbk,bki->cbi", drive_rows.astype(jnp.float32), near_inverse.astype(jnp.float32))
    return solved.reshape(NC, NB * TB).astype(jnp.bfloat16)


def reference(tiles, tile_index, tile_count, history, incident, near_inverse):
    field_one = scattered_field(history, tiles, tile_index, tile_count)
    first_new = lax.optimization_barrier(near_solve(incident[0] - field_one, near_inverse))
    shifted = jnp.concatenate([first_new[None], history[:HISTORY - 1]], axis=0)
    field_two = scattered_field(shifted, tiles, tile_index, tile_count)
    second_new = near_solve(incident[1] - field_two, near_inverse)
    return jnp.stack([first_new, second_new])
```

```python
import functools

import jax
import jax.numpy as jnp
from jax import lax
from jax.experimental import pallas as pl
from jax.experimental.pallas import tpu as pltpu
from jax.sharding import PartitionSpec as P

MESH = pl.DeviceIdType.MESH
CAP = 64
CAP0 = 16
FAR = -(1 << 20)


def greet(src_peers, obs_peers, n_src, n_obs):
    me_s, me_o = lax.axis_index("src"), lax.axis_index("obs")
    barrier = pltpu.get_barrier_semaphore()
    if src_peers:
        for k in range(1, n_src):
            pl.semaphore_signal(
                barrier, inc=1, device_id=(lax.rem(me_s + k, n_src), me_o), device_id_type=MESH
            )
    if obs_peers:
        for k in range(1, n_obs):
            pl.semaphore_signal(
                barrier, inc=1, device_id=(me_s, lax.rem(me_o + k, n_obs)), device_id_type=MESH
            )
    total = (n_src - 1) * src_peers + (n_obs - 1) * obs_peers
    return lambda: pl.semaphore_wait(barrier, total)


def to_obs(k, n_obs, src_ref, dst_ref, send_sem, recv_sem):
    me_s, me_o = lax.axis_index("src"), lax.axis_index("obs")
    return pltpu.make_async_remote_copy(
        src_ref=src_ref, dst_ref=dst_ref, send_sem=send_sem.at[k], recv_sem=recv_sem.at[k],
        device_id=(me_s, lax.rem(me_o + k, n_obs)), device_id_type=MESH,
    )


def to_src(k, n_src, src_ref, dst_ref, send_sem, recv_sem):
    me_s, me_o = lax.axis_index("src"), lax.axis_index("obs")
    return pltpu.make_async_remote_copy(
        src_ref=src_ref, dst_ref=dst_ref, send_sem=send_sem.at[k], recv_sem=recv_sem.at[k],
        device_id=(lax.rem(me_s + k, n_src), me_o), device_id_type=MESH,
    )


def request_kernel(n_src, n_obs, bd, idx_ref, cnt_ref, recv_ref, info_ref, send_ref, send_sem, recv_sem):
    me = lax.axis_index("obs")
    entered = greet(0, 1, n_src, n_obs)
    n_tiles = idx_ref.shape[1]
    shift = bd.bit_length() - 1
    lane = lax.broadcasted_iota(jnp.int32, (1, n_tiles), 1)
    live = lane < cnt_ref[0, 0]
    obs_block = idx_ref[0:1, :]
    source = idx_ref[1:2, :]
    delay = idx_ref[2:3, :]
    owner = lax.shift_right_logical(source, shift)
    place = jnp.bitwise_and(source, bd - 1)
    owner_row = lax.broadcasted_iota(jnp.int32, (n_obs, n_tiles), 0)
    mine = jnp.where(jnp.logical_and(owner == owner_row, live), 1.0, 0.0)
    mine0 = jnp.where(delay == 0, mine, 0.0)
    before = jnp.where(
        lax.broadcasted_iota(jnp.int32, (n_tiles, n_tiles), 0)
        < lax.broadcasted_iota(jnp.int32, (n_tiles, n_tiles), 1),
        1.0, 0.0,
    ).astype(jnp.bfloat16)
    order = jnp.dot(mine.astype(jnp.bfloat16), before, preferred_element_type=jnp.float32)
    order0 = jnp.dot(mine0.astype(jnp.bfloat16), before, preferred_element_type=jnp.float32)
    rank = jnp.sum(order * mine, axis=0, keepdims=True)
    rank0 = jnp.sum(order0 * mine0, axis=0, keepdims=True)
    newest = jnp.logical_and(live, delay == 0)
    over = jnp.where(live, jnp.where(rank >= CAP, 1.0, 0.0), 0.0) + jnp.where(
        newest, jnp.where(rank0 >= CAP0, 1.0, 0.0), 0.0
    )
    flag = jnp.max(over, axis=1, keepdims=True)
    rank = rank.astype(jnp.int32)
    rank0 = rank0.astype(jnp.int32)
    fits = jnp.logical_and(live, rank < CAP)
    fits0 = jnp.logical_and(newest, rank0 < CAP0)
    slot = jnp.where(fits, owner * CAP + rank, 0)
    slot0 = jnp.where(fits0, n_obs * CAP + owner * CAP0 + rank0, 0)
    info_ref[0:1, :] = slot
    info_ref[1:2, :] = jnp.where(fits, obs_block, n_src * bd)
    info_ref[2:3, :] = jnp.where(newest, slot0, slot)
    info_ref[3:8, :] = jnp.zeros((5, n_tiles), jnp.int32)
    key = jnp.where(fits, owner * 128 + rank, FAR)
    key0 = jnp.where(fits0, owner * 128 + CAP + rank0, FAR)
    code_row = lax.broadcasted_iota(jnp.int32, (16, n_tiles), 0)
    codes = jnp.where(code_row == 0, place, jnp.where(code_row == 1, delay, 0))
    codes = codes.astype(jnp.float32).astype(jnp.bfloat16)
    row = lax.broadcasted_iota(jnp.int32, (128, n_tiles), 0)
    out_lane = lax.broadcasted_iota(jnp.int32, (1, 128), 1)

    def one_owner(o, carry):
        hit = jnp.logical_or(key - o * 128 == row, key0 - o * 128 == row)
        pick = jnp.where(hit, 1.0, 0.0).astype(jnp.bfloat16)
        found = lax.dot_general(
            codes, pick, (((1,), (1,)), ((), ())), preferred_element_type=jnp.float32
        )
        code = found[0:1, :] + found[1:2, :] * bd
        code = jnp.where(out_lane == 127, flag, code)
        send_ref[o] = code.astype(jnp.int32)
        return carry

    lax.fori_loop(0, n_obs, one_owner, 0)
    recv_ref[me] = send_ref[me]
    entered()
    copies = []
    for k in range(1, n_obs):
        copy = to_obs(k, n_obs, send_ref.at[lax.rem(me + k, n_obs)], recv_ref.at[me], send_sem, recv_sem)
        copy.start()
        copies.append(copy)
    for copy in copies:
        copy.wait()


def gather_rows(req_ref, table_ref, out_ref, dest, slots, first, code_to_row):
    step = 8

    def one(turn, carry):
        for i in range(step):
            r = turn * step + i
            out_ref[r] = table_ref[code_to_row(req_ref[dest, 0, first + r])]
        return carry

    lax.fori_loop(0, slots // step, one, 0)


def rows_kernel(n_src, n_obs, bd, req_ref, hist_ref, rows_ref, flags_ref, send, mark, own_sem, send_sem, recv_sem, fsend, frecv):
    me_s, me_o = lax.axis_index("src"), lax.axis_index("obs")
    entered = greet(1, 1, n_src, n_obs)
    flag = req_ref[0, 0, 127]
    for o in range(1, n_obs):
        flag = jnp.maximum(flag, req_ref[o, 0, 127])
    mark[...] = jnp.full(mark.shape, flag, jnp.int32)
    flags_ref[me_s] = mark[...]
    copies = []
    for k in range(1, n_obs):
        gather_rows(req_ref, hist_ref, send.at[k], lax.rem(me_o + k, n_obs), CAP, 0, lambda c: c)
        if k == 1:
            entered()
        copy = to_obs(k, n_obs, send.at[k], rows_ref.at[pl.ds(me_o * CAP, CAP)], send_sem, recv_sem)
        copy.start()
        copies.append(copy)
        if k == 1:
            for j in range(1, n_src):
                copy = to_src(j, n_src, mark, flags_ref.at[me_s], fsend, frecv)
                copy.start()
                copies.append(copy)
    gather_rows(req_ref, hist_ref, send.at[0], me_o, CAP, 0, lambda c: c)
    own = pltpu.make_async_copy(send.at[0], rows_ref.at[pl.ds(me_o * CAP, CAP)], own_sem)
    own.start()
    own.wait()
    for copy in copies:
        copy.wait()


def products_kernel(which, chunk, depth, info_ref, cnt_ref, tiles_ref, rows_ref, acc_ref, buf, sem):
    live = cnt_ref[0, 0]
    chunks = (live + chunk - 1) // chunk

    def fetch(c, slot):
        return pltpu.make_async_copy(tiles_ref.at[pl.ds(c * chunk, chunk)], buf.at[slot], sem.at[slot])

    for c in range(min(depth - 1, tiles_ref.shape[0] // chunk)):
        @pl.when(c < chunks)
        def _():
            fetch(c, c).start()

    acc_ref[...] = jnp.zeros_like(acc_ref)

    def one_chunk(c, carry):
        slot = lax.rem(c, depth)

        @pl.when(c + depth - 1 < chunks)
        def _():
            fetch(c + depth - 1, lax.rem(c + depth - 1, depth)).start()

        fetch(c, slot).wait()
        for i in range(chunk):
            t = c * chunk + i
            y = jnp.dot(rows_ref[info_ref[which, t]], buf[slot, i], preferred_element_type=jnp.float32)
            l = info_ref[1, t]
            acc_ref[l] = acc_ref[l] + y
        return carry

    lax.fori_loop(0, chunks, one_chunk, 0)


def scatter_start(n_src, bd, part_ref, recv, send_sem, recv_sem):
    me_s = lax.axis_index("src")
    copies = []
    for k in range(1, n_src):
        peer = lax.rem(me_s + k, n_src)
        copy = to_src(k, n_src, part_ref.at[pl.ds(peer * bd, bd)], recv.at[k], send_sem, recv_sem)
        copy.start()
        copies.append(copy)
    return copies


def reduce_solve(n_src, bd, part_ref, recv, inc_ref, near, new_ref):
    me_s = lax.axis_index("src")
    step = 8

    def one(turn, carry):
        at = pl.ds(turn * step, step)
        total = part_ref[pl.ds(me_s * bd + turn * step, step)]
        for k in range(1, n_src):
            total = total + recv[k, at]
        drive = (inc_ref[at] - total).astype(jnp.bfloat16)
        for i in range(step):
            b = turn * step + i
            new_ref[b] = jnp.dot(drive[i], near[b], preferred_element_type=jnp.float32).astype(jnp.bfloat16)
        return carry

    lax.fori_loop(0, bd // step, one, 0)


def first_kernel(
    n_src, n_obs, bd, req_ref, part_ref, inc_ref, near_ref, hist_ref, new_ref, rows_ref,
    recv, near, send, send0, near_sem, own_sem, rsend, rrecv, send_sem, recv_sem, send_sem0, recv_sem0,
):
    me_s, me_o = lax.axis_index("src"), lax.axis_index("obs")
    entered = greet(1, 1, n_src, n_obs)
    load = pltpu.make_async_copy(near_ref, near, near_sem)
    load.start()
    entered()
    reduce = scatter_start(n_src, bd, part_ref, recv, rsend, rrecv)
    older = lambda c: jnp.maximum(c - bd, 0)
    copies = []
    for k in range(1, n_obs):
        gather_rows(req_ref, hist_ref, send.at[k], lax.rem(me_o + k, n_obs), CAP, 0, older)
        copy = to_obs(k, n_obs, send.at[k], rows_ref.at[pl.ds(me_o * CAP, CAP)], send_sem, recv_sem)
        copy.start()
        copies.append(copy)
    gather_rows(req_ref, hist_ref, send.at[0], me_o, CAP, 0, older)
    own = pltpu.make_async_copy(send.at[0], rows_ref.at[pl.ds(me_o * CAP, CAP)], own_sem.at[0])
    own.start()
    load.wait()
    for copy in reduce:
        copy.wait()
    reduce_solve(n_src, bd, part_ref, recv, inc_ref, near, new_ref)
    base = n_obs * CAP
    place = lambda c: jnp.bitwise_and(c, bd - 1)
    for k in range(1, n_obs):
        gather_rows(req_ref, new_ref, send0.at[k], lax.rem(me_o + k, n_obs), CAP0, CAP, place)
        copy = to_obs(k, n_obs, send0.at[k], rows_ref.at[pl.ds(base + me_o * CAP0, CAP0)], send_sem0, recv_sem0)
        copy.start()
        copies.append(copy)
    gather_rows(req_ref, new_ref, send0.at[0], me_o, CAP0, CAP, place)
    own0 = pltpu.make_async_copy(send0.at[0], rows_ref.at[pl.ds(base + me_o * CAP0, CAP0)], own_sem.at[1])
    own0.start()
    own.wait()
    own0.wait()
    for copy in copies:
        copy.wait()


def second_kernel(n_src, n_obs, bd, part_ref, inc_ref, near_ref, new_ref, recv, near, near_sem, rsend, rrecv):
    entered = greet(1, 0, n_src, n_obs)
    load = pltpu.make_async_copy(near_ref, near, near_sem)
    load.start()
    entered()
    reduce = scatter_start(n_src, bd, part_ref, recv, rsend, rrecv)
    load.wait()
    for copy in reduce:
        copy.wait()
    reduce_solve(n_src, bd, part_ref, recv, inc_ref, near, new_ref)


def dense_path(tile_rows, index_rows, live_count, history, incident, near_inverse, n_src, n_obs):
    bd, width = near_inverse.shape[:2]
    slots, coefs = history.shape[:2]
    n_tiles = tile_rows.shape[0]
    group = min(64, n_tiles)

    def gather_obs(block):
        ring = [(i, (i + 1) % n_obs) for i in range(n_obs)]
        me = lax.axis_index("obs")
        whole = jnp.zeros((n_obs,) + block.shape, block.dtype)

        def hop(k, carry):
            whole, moving = carry
            whole = lax.dynamic_update_index_in_dim(whole, moving, lax.rem(me - k + n_obs, n_obs), 0)
            return whole, lax.ppermute(moving, "obs", ring)

        return lax.fori_loop(0, n_obs, hop, (whole, block))[0]

    def sum_src(value):
        ring = [(i, (i + 1) % n_src) for i in range(n_src)]

        def hop(k, carry):
            total, moving = carry
            moving = lax.ppermute(moving, "src", ring)
            return total + moving, moving

        return lax.fori_loop(0, n_src - 1, hop, (value, value))[0]

    def accumulate(chooser):
        def one_group(turn, partial):
            start = turn * group
            tile_part = lax.dynamic_slice_in_dim(tile_rows, start, group, 0)
            index_part = lax.dynamic_slice_in_dim(index_rows, start, group, 1)
            products = jnp.einsum(
                "gck,gki->gci", chooser(index_part), tile_part, preferred_element_type=jnp.float32
            )
            alive = start + jnp.arange(group, dtype=jnp.int32) < live_count
            products = jnp.where(alive[:, None, None], products, 0.0)
            return partial.at[index_part[0]].add(products)

        initial = jnp.zeros((bd * n_src, coefs, width), jnp.float32)
        return lax.fori_loop(0, n_tiles // group, one_group, initial)

    def settle(partial, drive):
        own = lax.dynamic_slice_in_dim(sum_src(partial), lax.axis_index("src") * bd, bd, 0)
        right = (drive - own).astype(jnp.bfloat16)
        solved = jnp.einsum("bck,bki->bci", right, near_inverse, preferred_element_type=jnp.float32)
        return solved.astype(jnp.bfloat16)

    past = gather_obs(history)

    def pick(block, index_part, slot):
        return past[index_part[1] // bd, slot, index_part[1] % bd]

    past = past.reshape(n_obs, slots, coefs, bd, width).transpose(0, 1, 3, 2, 4)
    first = settle(accumulate(lambda ip: pick(past, ip, ip[2])), incident[0])
    newest = gather_obs(first)

    def second_rows(ip):
        older = pick(past, ip, jnp.maximum(ip[2] - 1, 0))
        newer = newest[ip[1] // bd, ip[1] % bd]
        return jnp.where((ip[2] == 0)[:, None, None], newer, older)

    second = settle(accumulate(second_rows), incident[1])
    return jnp.stack([first, second])


def solution(mesh):
    n_src, n_obs = mesh.shape["src"], mesh.shape["obs"]
    vmem = pl.BlockSpec(memory_space=pltpu.VMEM)
    smem = pl.BlockSpec(memory_space=pltpu.SMEM)
    anywhere = pl.BlockSpec(memory_space=pl.ANY)
    dma = pltpu.SemaphoreType.DMA

    def params(i):
        return pltpu.CompilerParams(collective_id=i, has_side_effects=True)

    def on_device(tiles, tile_index, tile_count, history, incident, near_inverse):
        n_tiles, width = tiles.shape[2], tiles.shape[4]
        bd = near_inverse.shape[0]
        slots, coefs = history.shape[:2]
        tile_rows = tiles.reshape(n_tiles, width, width)
        index_rows = tile_index.reshape(3, n_tiles)
        hist = history.reshape(slots, coefs, bd, width).transpose(0, 2, 1, 3).reshape(slots * bd, coefs, width)
        drive = incident.reshape(2, coefs, bd, width).transpose(0, 2, 1, 3)
        row_slots = n_obs * CAP

        requests, info = pl.pallas_call(
            functools.partial(request_kernel, n_src, n_obs, bd),
            name="requests",
            out_shape=(
                jax.ShapeDtypeStruct((n_obs, 1, 128), jnp.int32),
                jax.ShapeDtypeStruct((8, n_tiles), jnp.int32),
            ),
            in_specs=[vmem, smem],
            out_specs=(vmem, vmem),
            scratch_shapes=[pltpu.VMEM((n_obs, 1, 128), jnp.int32), dma((n_obs,)), dma((n_obs,))],
            compiler_params=params(0),
        )(index_rows, tile_count)

        rows, flags = pl.pallas_call(
            functools.partial(rows_kernel, n_src, n_obs, bd),
            name="rows",
            out_shape=(
                jax.ShapeDtypeStruct((row_slots, coefs, width), jnp.bfloat16),
                jax.ShapeDtypeStruct((n_src, 1, 128), jnp.int32),
            ),
            in_specs=[smem, vmem],
            out_specs=(anywhere, vmem),
            scratch_shapes=[
                pltpu.VMEM((n_obs, CAP, coefs, width), jnp.bfloat16), pltpu.VMEM((1, 128), jnp.int32),
                dma, dma((n_obs,)), dma((n_obs,)), dma((n_src,)), dma((n_src,)),
            ],
            compiler_params=params(1),
        )(requests, hist)

        chunk, depth = min(32, n_tiles), 4

        def products(which, row_array):
            return pl.pallas_call(
                functools.partial(products_kernel, which, chunk, depth),
                name="products",
                out_shape=jax.ShapeDtypeStruct((n_src * bd + 8, coefs, width), jnp.float32),
                in_specs=[smem, smem, anywhere, vmem],
                out_specs=vmem,
                scratch_shapes=[pltpu.VMEM((depth, chunk, width, width), jnp.bfloat16), dma((depth,))],
            )(info, tile_count, tile_rows, row_array)

        part = products(0, rows)
        first, rows2 = pl.pallas_call(
            functools.partial(first_kernel, n_src, n_obs, bd),
            name="first",
            out_shape=(
                jax.ShapeDtypeStruct((bd, coefs, width), jnp.bfloat16),
                jax.ShapeDtypeStruct((row_slots + n_obs * CAP0, coefs, width), jnp.bfloat16),
            ),
            in_specs=[smem, vmem, vmem, anywhere, vmem],
            out_specs=(vmem, anywhere),
            scratch_shapes=[
                pltpu.VMEM((n_src, bd, coefs, width), jnp.float32),
                pltpu.VMEM((bd, width, width), jnp.bfloat16),
                pltpu.VMEM((n_obs, CAP, coefs, width), jnp.bfloat16),
                pltpu.VMEM((n_obs, CAP0, coefs, width), jnp.bfloat16),
                dma, dma((2,)), dma((n_src,)), dma((n_src,)),
                dma((n_obs,)), dma((n_obs,)), dma((n_obs,)), dma((n_obs,)),
            ],
            compiler_params=params(2),
        )(requests, part, drive[0], near_inverse, hist)
        part = products(2, rows2)
        second = pl.pallas_call(
            functools.partial(second_kernel, n_src, n_obs, bd),
            name="second",
            out_shape=jax.ShapeDtypeStruct((bd, coefs, width), jnp.bfloat16),
            in_specs=[vmem, vmem, anywhere],
            out_specs=vmem,
            scratch_shapes=[
                pltpu.VMEM((n_src, bd, coefs, width), jnp.float32),
                pltpu.VMEM((bd, width, width), jnp.bfloat16),
                dma, dma((n_src,)), dma((n_src,)),
            ],
            compiler_params=params(3),
        )(part, drive[1], near_inverse)
        both = jnp.stack([first, second])
        crowded = jnp.max(flags) > 0

        both = lax.cond(
            crowded,
            lambda kept: dense_path(
                tile_rows, index_rows, tile_count.reshape(()), history, drive, near_inverse, n_src, n_obs
            ),
            lambda kept: kept,
            both,
        )
        return both.transpose(0, 2, 1, 3).reshape(2, coefs, bd * width)

    in_specs = (
        P("src", "obs", None, None, None),
        P("src", "obs", None, None),
        P("src", "obs"),
        P(None, None, ("src", "obs")),
        P(None, None, ("src", "obs")),
        P(("src", "obs"), None, None),
    )
    out_specs = P(None, None, ("src", "obs"))
    return jax.shard_map(on_device, mesh=mesh, in_specs=in_specs, out_specs=out_specs, check_vma=False)
```

```python
import functools

import jax
import jax.numpy as jnp
from jax import lax
from jax.experimental import pallas as pl
from jax.experimental.pallas import tpu as pltpu
from jax.sharding import PartitionSpec as P

MESH = pl.DeviceIdType.MESH
CAP = 64
CAP0 = 16
FAR = -(1 << 20)


def greet(src_peers, obs_peers, n_src, n_obs):
    me_s, me_o = lax.axis_index("src"), lax.axis_index("obs")
    barrier = pltpu.get_barrier_semaphore()
    if src_peers:
        for k in range(1, n_src):
            pl.semaphore_signal(
                barrier, inc=1, device_id=(lax.rem(me_s + k, n_src), me_o), device_id_type=MESH
            )
    if obs_peers:
        for k in range(1, n_obs):
            pl.semaphore_signal(
                barrier, inc=1, device_id=(me_s, lax.rem(me_o + k, n_obs)), device_id_type=MESH
            )
    total = (n_src - 1) * src_peers + (n_obs - 1) * obs_peers
    return lambda: pl.semaphore_wait(barrier, total)


def to_obs(k, n_obs, src_ref, dst_ref, send_sem, recv_sem):
    me_s, me_o = lax.axis_index("src"), lax.axis_index("obs")
    return pltpu.make_async_remote_copy(
        src_ref=src_ref, dst_ref=dst_ref, send_sem=send_sem.at[k], recv_sem=recv_sem.at[k],
        device_id=(me_s, lax.rem(me_o + k, n_obs)), device_id_type=MESH,
    )


def to_src(k, n_src, src_ref, dst_ref, send_sem, recv_sem):
    me_s, me_o = lax.axis_index("src"), lax.axis_index("obs")
    return pltpu.make_async_remote_copy(
        src_ref=src_ref, dst_ref=dst_ref, send_sem=send_sem.at[k], recv_sem=recv_sem.at[k],
        device_id=(lax.rem(me_s + k, n_src), me_o), device_id_type=MESH,
    )


def request_kernel(n_src, n_obs, bd, idx_ref, cnt_ref, recv_ref, info_ref, send_ref, send_sem, recv_sem):
    me = lax.axis_index("obs")
    entered = greet(0, 1, n_src, n_obs)
    n_tiles = idx_ref.shape[1]
    shift = bd.bit_length() - 1
    lane = lax.broadcasted_iota(jnp.int32, (1, n_tiles), 1)
    live = lane < cnt_ref[0, 0]
    obs_block = idx_ref[0:1, :]
    source = idx_ref[1:2, :]
    delay = idx_ref[2:3, :]
    owner = lax.shift_right_logical(source, shift)
    place = jnp.bitwise_and(source, bd - 1)
    owner_row = lax.broadcasted_iota(jnp.int32, (n_obs, n_tiles), 0)
    mine = jnp.where(jnp.logical_and(owner == owner_row, live), 1.0, 0.0)
    mine0 = jnp.where(delay == 0, mine, 0.0)
    before = jnp.where(
        lax.broadcasted_iota(jnp.int32, (n_tiles, n_tiles), 0)
        < lax.broadcasted_iota(jnp.int32, (n_tiles, n_tiles), 1),
        1.0, 0.0,
    ).astype(jnp.bfloat16)
    order = jnp.dot(mine.astype(jnp.bfloat16), before, preferred_element_type=jnp.float32)
    order0 = jnp.dot(mine0.astype(jnp.bfloat16), before, preferred_element_type=jnp.float32)
    rank = jnp.sum(order * mine, axis=0, keepdims=True)
    rank0 = jnp.sum(order0 * mine0, axis=0, keepdims=True)
    newest = jnp.logical_and(live, delay == 0)
    over = jnp.where(live, jnp.where(rank >= CAP, 1.0, 0.0), 0.0) + jnp.where(
        newest, jnp.where(rank0 >= CAP0, 1.0, 0.0), 0.0
    )
    flag = jnp.max(over, axis=1, keepdims=True)
    rank = rank.astype(jnp.int32)
    rank0 = rank0.astype(jnp.int32)
    fits = jnp.logical_and(live, rank < CAP)
    fits0 = jnp.logical_and(newest, rank0 < CAP0)
    slot = jnp.where(fits, owner * CAP + rank, 0)
    slot0 = jnp.where(fits0, n_obs * CAP + owner * CAP0 + rank0, 0)
    info_ref[0:1, :] = slot
    info_ref[1:2, :] = jnp.where(fits, obs_block, n_src * bd)
    info_ref[2:3, :] = jnp.where(newest, slot0, slot)
    info_ref[3:8, :] = jnp.zeros((5, n_tiles), jnp.int32)
    key = jnp.where(fits, owner * 128 + rank, FAR)
    key0 = jnp.where(fits0, owner * 128 + CAP + rank0, FAR)
    code_row = lax.broadcasted_iota(jnp.int32, (16, n_tiles), 0)
    codes = jnp.where(code_row == 0, place, jnp.where(code_row == 1, delay, 0))
    codes = codes.astype(jnp.float32).astype(jnp.bfloat16)
    row = lax.broadcasted_iota(jnp.int32, (128, n_tiles), 0)
    out_lane = lax.broadcasted_iota(jnp.int32, (1, 128), 1)

    def one_owner(o, carry):
        hit = jnp.logical_or(key - o * 128 == row, key0 - o * 128 == row)
        pick = jnp.where(hit, 1.0, 0.0).astype(jnp.bfloat16)
        found = lax.dot_general(
            codes, pick, (((1,), (1,)), ((), ())), preferred_element_type=jnp.float32
        )
        code = found[0:1, :] + found[1:2, :] * bd
        code = jnp.where(out_lane == 127, flag, code)
        send_ref[o] = code.astype(jnp.int32)
        return carry

    lax.fori_loop(0, n_obs, one_owner, 0)
    recv_ref[me] = send_ref[me]
    entered()
    copies = []
    for k in range(1, n_obs):
        copy = to_obs(k, n_obs, send_ref.at[lax.rem(me + k, n_obs)], recv_ref.at[me], send_sem, recv_sem)
        copy.start()
        copies.append(copy)
    for copy in copies:
        copy.wait()


def gather_rows(req_ref, table_ref, out_ref, dest, slots, first, code_to_row):
    step = 8

    def one(turn, carry):
        for i in range(step):
            r = turn * step + i
            out_ref[r] = table_ref[code_to_row(req_ref[dest, 0, first + r])]
        return carry

    lax.fori_loop(0, slots // step, one, 0)


def rows_kernel(n_src, n_obs, bd, req_ref, hist_ref, rows_ref, flags_ref, send, mark, own_sem, send_sem, recv_sem, fsend, frecv):
    me_s, me_o = lax.axis_index("src"), lax.axis_index("obs")
    entered = greet(1, 1, n_src, n_obs)
    flag = req_ref[0, 0, 127]
    for o in range(1, n_obs):
        flag = jnp.maximum(flag, req_ref[o, 0, 127])
    mark[...] = jnp.full(mark.shape, flag, jnp.int32)
    flags_ref[me_s] = mark[...]
    copies = []
    for k in range(1, n_obs):
        gather_rows(req_ref, hist_ref, send.at[k], lax.rem(me_o + k, n_obs), CAP, 0, lambda c: c)
        if k == 1:
            entered()
        copy = to_obs(k, n_obs, send.at[k], rows_ref.at[pl.ds(me_o * CAP, CAP)], send_sem, recv_sem)
        copy.start()
        copies.append(copy)
        if k == 1:
            for j in range(1, n_src):
                copy = to_src(j, n_src, mark, flags_ref.at[me_s], fsend, frecv)
                copy.start()
                copies.append(copy)
    gather_rows(req_ref, hist_ref, send.at[0], me_o, CAP, 0, lambda c: c)
    own = pltpu.make_async_copy(send.at[0], rows_ref.at[pl.ds(me_o * CAP, CAP)], own_sem)
    own.start()
    own.wait()
    for copy in copies:
        copy.wait()


def products_kernel(which, chunk, depth, info_ref, cnt_ref, tiles_ref, rows_ref, out_ref, acc_ref, buf, sem):
    live = cnt_ref[0, 0]
    chunks = (live + chunk - 1) // chunk

    def fetch(c, slot):
        return pltpu.make_async_copy(tiles_ref.at[pl.ds(c * chunk, chunk)], buf.at[slot], sem.at[slot])

    for c in range(min(depth - 1, tiles_ref.shape[0] // chunk)):
        @pl.when(c < chunks)
        def _():
            fetch(c, c).start()

    acc_ref[...] = jnp.zeros_like(acc_ref)

    def one_chunk(c, carry):
        slot = lax.rem(c, depth)

        @pl.when(c + depth - 1 < chunks)
        def _():
            fetch(c + depth - 1, lax.rem(c + depth - 1, depth)).start()

        fetch(c, slot).wait()
        for i in range(chunk):
            t = c * chunk + i
            y = jnp.dot(rows_ref[info_ref[which, t]], buf[slot, i], preferred_element_type=jnp.float32)
            l = info_ref[1, t]
            acc_ref[l] = acc_ref[l] + y
        return carry

    lax.fori_loop(0, chunks, one_chunk, 0)
    out_ref[...] = acc_ref[0 : out_ref.shape[0]].astype(jnp.bfloat16)


def scatter_start(n_src, bd, part_ref, recv, send_sem, recv_sem):
    me_s = lax.axis_index("src")
    copies = []
    for k in range(1, n_src):
        peer = lax.rem(me_s + k, n_src)
        copy = to_src(k, n_src, part_ref.at[pl.ds(peer * bd, bd)], recv.at[k], send_sem, recv_sem)
        copy.start()
        copies.append(copy)
    return copies


def reduce_solve(n_src, bd, part_ref, recv, inc_ref, near, new_ref):
    me_s = lax.axis_index("src")
    step = 8

    def one(turn, carry):
        at = pl.ds(turn * step, step)
        total = part_ref[pl.ds(me_s * bd + turn * step, step)].astype(jnp.float32)
        for k in range(1, n_src):
            total = total + recv[k, at].astype(jnp.float32)
        drive = (inc_ref[at] - total).astype(jnp.bfloat16)
        for i in range(step):
            b = turn * step + i
            new_ref[b] = jnp.dot(drive[i], near[b], preferred_element_type=jnp.float32).astype(jnp.bfloat16)
        return carry

    lax.fori_loop(0, bd // step, one, 0)


def first_kernel(
    n_src, n_obs, bd, req_ref, part_ref, inc_ref, near_ref, hist_ref, new_ref, rows_ref,
    recv, near, send, send0, near_sem, own_sem, rsend, rrecv, send_sem, recv_sem, send_sem0, recv_sem0,
):
    me_s, me_o = lax.axis_index("src"), lax.axis_index("obs")
    entered = greet(1, 1, n_src, n_obs)
    load = pltpu.make_async_copy(near_ref, near, near_sem)
    load.start()
    entered()
    reduce = scatter_start(n_src, bd, part_ref, recv, rsend, rrecv)
    older = lambda c: jnp.maximum(c - bd, 0)
    copies = []
    for k in range(1, n_obs):
        gather_rows(req_ref, hist_ref, send.at[k], lax.rem(me_o + k, n_obs), CAP, 0, older)
        copy = to_obs(k, n_obs, send.at[k], rows_ref.at[pl.ds(me_o * CAP, CAP)], send_sem, recv_sem)
        copy.start()
        copies.append(copy)
    gather_rows(req_ref, hist_ref, send.at[0], me_o, CAP, 0, older)
    own = pltpu.make_async_copy(send.at[0], rows_ref.at[pl.ds(me_o * CAP, CAP)], own_sem.at[0])
    own.start()
    load.wait()
    for copy in reduce:
        copy.wait()
    reduce_solve(n_src, bd, part_ref, recv, inc_ref, near, new_ref)
    base = n_obs * CAP
    place = lambda c: jnp.bitwise_and(c, bd - 1)
    for k in range(1, n_obs):
        gather_rows(req_ref, new_ref, send0.at[k], lax.rem(me_o + k, n_obs), CAP0, CAP, place)
        copy = to_obs(k, n_obs, send0.at[k], rows_ref.at[pl.ds(base + me_o * CAP0, CAP0)], send_sem0, recv_sem0)
        copy.start()
        copies.append(copy)
    gather_rows(req_ref, new_ref, send0.at[0], me_o, CAP0, CAP, place)
    own0 = pltpu.make_async_copy(send0.at[0], rows_ref.at[pl.ds(base + me_o * CAP0, CAP0)], own_sem.at[1])
    own0.start()
    own.wait()
    own0.wait()
    for copy in copies:
        copy.wait()


def second_kernel(n_src, n_obs, bd, part_ref, inc_ref, near_ref, new_ref, recv, near, near_sem, rsend, rrecv):
    entered = greet(1, 0, n_src, n_obs)
    load = pltpu.make_async_copy(near_ref, near, near_sem)
    load.start()
    entered()
    reduce = scatter_start(n_src, bd, part_ref, recv, rsend, rrecv)
    load.wait()
    for copy in reduce:
        copy.wait()
    reduce_solve(n_src, bd, part_ref, recv, inc_ref, near, new_ref)


def dense_path(tile_rows, index_rows, live_count, history, incident, near_inverse, n_src, n_obs):
    bd, width = near_inverse.shape[:2]
    slots, coefs = history.shape[:2]
    n_tiles = tile_rows.shape[0]
    group = min(64, n_tiles)

    def gather_obs(block):
        ring = [(i, (i + 1) % n_obs) for i in range(n_obs)]
        me = lax.axis_index("obs")
        whole = jnp.zeros((n_obs,) + block.shape, block.dtype)

        def hop(k, carry):
            whole, moving = carry
            whole = lax.dynamic_update_index_in_dim(whole, moving, lax.rem(me - k + n_obs, n_obs), 0)
            return whole, lax.ppermute(moving, "obs", ring)

        return lax.fori_loop(0, n_obs, hop, (whole, block))[0]

    def sum_src(value):
        ring = [(i, (i + 1) % n_src) for i in range(n_src)]

        def hop(k, carry):
            total, moving = carry
            moving = lax.ppermute(moving, "src", ring)
            return total + moving, moving

        return lax.fori_loop(0, n_src - 1, hop, (value, value))[0]

    def accumulate(chooser):
        def one_group(turn, partial):
            start = turn * group
            tile_part = lax.dynamic_slice_in_dim(tile_rows, start, group, 0)
            index_part = lax.dynamic_slice_in_dim(index_rows, start, group, 1)
            products = jnp.einsum(
                "gck,gki->gci", chooser(index_part), tile_part, preferred_element_type=jnp.float32
            )
            alive = start + jnp.arange(group, dtype=jnp.int32) < live_count
            products = jnp.where(alive[:, None, None], products, 0.0)
            return partial.at[index_part[0]].add(products)

        initial = jnp.zeros((bd * n_src, coefs, width), jnp.float32)
        return lax.fori_loop(0, n_tiles // group, one_group, initial)

    def settle(partial, drive):
        own = lax.dynamic_slice_in_dim(sum_src(partial), lax.axis_index("src") * bd, bd, 0)
        right = (drive - own).astype(jnp.bfloat16)
        solved = jnp.einsum("bck,bki->bci", right, near_inverse, preferred_element_type=jnp.float32)
        return solved.astype(jnp.bfloat16)

    past = gather_obs(history)

    def pick(block, index_part, slot):
        return past[index_part[1] // bd, slot, index_part[1] % bd]

    past = past.reshape(n_obs, slots, coefs, bd, width).transpose(0, 1, 3, 2, 4)
    first = settle(accumulate(lambda ip: pick(past, ip, ip[2])), incident[0])
    newest = gather_obs(first)

    def second_rows(ip):
        older = pick(past, ip, jnp.maximum(ip[2] - 1, 0))
        newer = newest[ip[1] // bd, ip[1] % bd]
        return jnp.where((ip[2] == 0)[:, None, None], newer, older)

    second = settle(accumulate(second_rows), incident[1])
    return jnp.stack([first, second])


def solution(mesh):
    n_src, n_obs = mesh.shape["src"], mesh.shape["obs"]
    vmem = pl.BlockSpec(memory_space=pltpu.VMEM)
    smem = pl.BlockSpec(memory_space=pltpu.SMEM)
    anywhere = pl.BlockSpec(memory_space=pl.ANY)
    dma = pltpu.SemaphoreType.DMA

    def params(i):
        return pltpu.CompilerParams(collective_id=i, has_side_effects=True)

    def on_device(tiles, tile_index, tile_count, history, incident, near_inverse):
        n_tiles, width = tiles.shape[2], tiles.shape[4]
        bd = near_inverse.shape[0]
        slots, coefs = history.shape[:2]
        tile_rows = tiles.reshape(n_tiles, width, width)
        index_rows = tile_index.reshape(3, n_tiles)
        hist = history.reshape(slots, coefs, bd, width).transpose(0, 2, 1, 3).reshape(slots * bd, coefs, width)
        drive = incident.reshape(2, coefs, bd, width).transpose(0, 2, 1, 3)
        row_slots = n_obs * CAP

        requests, info = pl.pallas_call(
            functools.partial(request_kernel, n_src, n_obs, bd),
            name="requests",
            out_shape=(
                jax.ShapeDtypeStruct((n_obs, 1, 128), jnp.int32),
                jax.ShapeDtypeStruct((8, n_tiles), jnp.int32),
            ),
            in_specs=[vmem, smem],
            out_specs=(vmem, vmem),
            scratch_shapes=[pltpu.VMEM((n_obs, 1, 128), jnp.int32), dma((n_obs,)), dma((n_obs,))],
            compiler_params=params(0),
        )(index_rows, tile_count)

        rows, flags = pl.pallas_call(
            functools.partial(rows_kernel, n_src, n_obs, bd),
            name="rows",
            out_shape=(
                jax.ShapeDtypeStruct((row_slots, coefs, width), jnp.bfloat16),
                jax.ShapeDtypeStruct((n_src, 1, 128), jnp.int32),
            ),
            in_specs=[smem, vmem],
            out_specs=(anywhere, vmem),
            scratch_shapes=[
                pltpu.VMEM((n_obs, CAP, coefs, width), jnp.bfloat16), pltpu.VMEM((1, 128), jnp.int32),
                dma, dma((n_obs,)), dma((n_obs,)), dma((n_src,)), dma((n_src,)),
            ],
            compiler_params=params(1),
        )(requests, hist)

        chunk, depth = min(32, n_tiles), 4

        def products(which, row_array):
            return pl.pallas_call(
                functools.partial(products_kernel, which, chunk, depth),
                name="products",
                out_shape=jax.ShapeDtypeStruct((n_src * bd, coefs, width), jnp.bfloat16),
                in_specs=[smem, smem, anywhere, vmem],
                out_specs=vmem,
                scratch_shapes=[
                    pltpu.VMEM((n_src * bd + 8, coefs, width), jnp.float32),
                    pltpu.VMEM((depth, chunk, width, width), jnp.bfloat16), dma((depth,)),
                ],
            )(info, tile_count, tile_rows, row_array)

        part = products(0, rows)
        first, rows2 = pl.pallas_call(
            functools.partial(first_kernel, n_src, n_obs, bd),
            name="first",
            out_shape=(
                jax.ShapeDtypeStruct((bd, coefs, width), jnp.bfloat16),
                jax.ShapeDtypeStruct((row_slots + n_obs * CAP0, coefs, width), jnp.bfloat16),
            ),
            in_specs=[smem, vmem, vmem, anywhere, vmem],
            out_specs=(vmem, anywhere),
            scratch_shapes=[
                pltpu.VMEM((n_src, bd, coefs, width), jnp.bfloat16),
                pltpu.VMEM((bd, width, width), jnp.bfloat16),
                pltpu.VMEM((n_obs, CAP, coefs, width), jnp.bfloat16),
                pltpu.VMEM((n_obs, CAP0, coefs, width), jnp.bfloat16),
                dma, dma((2,)), dma((n_src,)), dma((n_src,)),
                dma((n_obs,)), dma((n_obs,)), dma((n_obs,)), dma((n_obs,)),
            ],
            compiler_params=params(2),
        )(requests, part, drive[0], near_inverse, hist)
        part = products(2, rows2)
        second = pl.pallas_call(
            functools.partial(second_kernel, n_src, n_obs, bd),
            name="second",
            out_shape=jax.ShapeDtypeStruct((bd, coefs, width), jnp.bfloat16),
            in_specs=[vmem, vmem, anywhere],
            out_specs=vmem,
            scratch_shapes=[
                pltpu.VMEM((n_src, bd, coefs, width), jnp.bfloat16),
                pltpu.VMEM((bd, width, width), jnp.bfloat16),
                dma, dma((n_src,)), dma((n_src,)),
            ],
            compiler_params=params(3),
        )(part, drive[1], near_inverse)
        both = jnp.stack([first, second])
        crowded = jnp.max(flags) > 0

        both = lax.cond(
            crowded,
            lambda kept: dense_path(
                tile_rows, index_rows, tile_count.reshape(()), history, drive, near_inverse, n_src, n_obs
            ),
            lambda kept: kept,
            both,
        )
        return both.transpose(0, 2, 1, 3).reshape(2, coefs, bd * width)

    in_specs = (
        P("src", "obs", None, None, None),
        P("src", "obs", None, None),
        P("src", "obs"),
        P(None, None, ("src", "obs")),
        P(None, None, ("src", "obs")),
        P(("src", "obs"), None, None),
    )
    out_specs = P(None, None, ("src", "obs"))
    return jax.shard_map(on_device, mesh=mesh, in_specs=in_specs, out_specs=out_specs, check_vma=False)
```

```python
import functools

import jax
import jax.numpy as jnp
from jax import lax
from jax.experimental import pallas as pl
from jax.experimental.pallas import tpu as pltpu
from jax.sharding import PartitionSpec as P

MESH = pl.DeviceIdType.MESH
CAP = 64
CAP0 = 16
CAPD = 64
FAR = -(1 << 20)


def greet(src_peers, obs_peers, n_src, n_obs):
    me_s, me_o = lax.axis_index("src"), lax.axis_index("obs")
    barrier = pltpu.get_barrier_semaphore()
    if src_peers:
        for k in range(1, n_src):
            pl.semaphore_signal(
                barrier, inc=1, device_id=(lax.rem(me_s + k, n_src), me_o), device_id_type=MESH
            )
    if obs_peers:
        for k in range(1, n_obs):
            pl.semaphore_signal(
                barrier, inc=1, device_id=(me_s, lax.rem(me_o + k, n_obs)), device_id_type=MESH
            )
    total = (n_src - 1) * src_peers + (n_obs - 1) * obs_peers
    return lambda: pl.semaphore_wait(barrier, total)


def to_obs(k, n_obs, src_ref, dst_ref, send_sem, recv_sem):
    me_s, me_o = lax.axis_index("src"), lax.axis_index("obs")
    return pltpu.make_async_remote_copy(
        src_ref=src_ref, dst_ref=dst_ref, send_sem=send_sem.at[k], recv_sem=recv_sem.at[k],
        device_id=(me_s, lax.rem(me_o + k, n_obs)), device_id_type=MESH,
    )


def to_src(k, n_src, src_ref, dst_ref, send_sem, recv_sem):
    me_s, me_o = lax.axis_index("src"), lax.axis_index("obs")
    return pltpu.make_async_remote_copy(
        src_ref=src_ref, dst_ref=dst_ref, send_sem=send_sem.at[k], recv_sem=recv_sem.at[k],
        device_id=(lax.rem(me_s + k, n_src), me_o), device_id_type=MESH,
    )


def each(count, body, start=0):
    lax.fori_loop(start, count, lambda i, carry: (body(i), carry)[1], 0)


def request_kernel(n_src, n_obs, bd, idx_ref, cnt_ref, recv_ref, info_ref, list_ref, send_ref, send_sem, recv_sem):
    me = lax.axis_index("obs")
    entered = greet(0, 1, n_src, n_obs)
    n_tiles = idx_ref.shape[2]
    shift = bd.bit_length() - 1
    lane = lax.broadcasted_iota(jnp.int32, (1, n_tiles), 1)
    live = lane < cnt_ref[0, 0]
    obs_block, source, delay = idx_ref[0], idx_ref[1], idx_ref[2]
    owner = lax.shift_right_logical(source, shift)
    place = jnp.bitwise_and(source, bd - 1)
    owner_row = lax.broadcasted_iota(jnp.int32, (n_obs, n_tiles), 0)
    mine = jnp.where(jnp.logical_and(owner == owner_row, live), 1.0, 0.0)
    mine0 = jnp.where(delay == 0, mine, 0.0)
    before = jnp.where(
        lax.broadcasted_iota(jnp.int32, (n_tiles, n_tiles), 0)
        < lax.broadcasted_iota(jnp.int32, (n_tiles, n_tiles), 1),
        1.0, 0.0,
    ).astype(jnp.bfloat16)
    both = jnp.concatenate([mine, mine0], axis=0).astype(jnp.bfloat16)
    order = jnp.dot(both, before, preferred_element_type=jnp.float32)
    rank = jnp.sum(order[:n_obs] * mine, axis=0, keepdims=True)
    rank0 = jnp.sum(order[n_obs:] * mine0, axis=0, keepdims=True)
    rank_d = jnp.sum(order[n_obs:], axis=0, keepdims=True)
    newest = jnp.logical_and(live, delay == 0)
    over = jnp.where(live, jnp.where(rank >= CAP, 1.0, 0.0), 0.0) + jnp.where(
        newest, jnp.where(rank0 >= CAP0, 1.0, 0.0) + jnp.where(rank_d >= CAPD, 1.0, 0.0), 0.0
    )
    flag = jnp.max(over, axis=1, keepdims=True)
    rank = rank.astype(jnp.int32)
    rank0 = rank0.astype(jnp.int32)
    fits = jnp.logical_and(live, rank < CAP)
    fits0 = jnp.logical_and(newest, rank0 < CAP0)
    nowhere = n_src * bd
    info_ref[0:1, :] = jnp.where(fits, owner * CAP + rank, 0)
    info_ref[1:2, :] = jnp.where(live, obs_block, nowhere)
    info_ref[2:3, :] = jnp.where(jnp.logical_and(live, delay > 0), obs_block, nowhere)
    info_ref[3:8, :] = jnp.zeros((5, n_tiles), jnp.int32)
    key = jnp.where(fits, owner * 128 + rank, FAR)
    key0 = jnp.where(fits0, owner * 128 + CAP + rank0, FAR)
    key_d = jnp.where(newest, rank_d.astype(jnp.int32), FAR)
    code_row = lax.broadcasted_iota(jnp.int32, (16, n_tiles), 0)
    codes = jnp.zeros((16, n_tiles), jnp.int32)
    slot0 = jnp.where(fits0, owner * CAP0 + rank0, 0)
    parts = (
        place, delay, jnp.bitwise_and(lane, 127), lax.shift_right_logical(lane, 7), slot0,
        jnp.bitwise_and(obs_block, 127), lax.shift_right_logical(obs_block, 7), jnp.ones_like(lane),
    )
    for i, part in enumerate(parts):
        codes = jnp.where(code_row == i, part, codes)
    codes = codes.astype(jnp.float32).astype(jnp.bfloat16)
    row = lax.broadcasted_iota(jnp.int32, (128, n_tiles), 0)
    out_lane = lax.broadcasted_iota(jnp.int32, (1, 128), 1)

    def find(hit):
        pick = jnp.where(hit, 1.0, 0.0).astype(jnp.bfloat16)
        return lax.dot_general(codes, pick, (((1,), (1,)), ((), ())), preferred_element_type=jnp.float32)

    def one_owner(o):
        found = find(jnp.logical_or(key - o * 128 == row, key0 - o * 128 == row))
        code = found[0:1, :] + found[1:2, :] * bd
        send_ref[o] = jnp.where(out_lane == 127, flag, code).astype(jnp.int32)

    each(n_obs, one_owner)
    recv_ref[me] = send_ref[me]
    entered()

    def send(k):
        return to_obs(k, n_obs, send_ref.at[lax.rem(me + k, n_obs)], recv_ref.at[me], send_sem, recv_sem)

    each(n_obs, lambda k: send(k).start(), 1)
    found = find(key_d == row)
    list_ref[0:1, :] = (found[2:3, :] + found[3:4, :] * 128.0).astype(jnp.int32)
    list_ref[1:2, :] = found[4:5, :].astype(jnp.int32)
    list_ref[2:3, :] = jnp.where(found[7:8, :] > 0.5, found[5:6, :] + found[6:7, :] * 128.0, 1.0 * nowhere).astype(jnp.int32)
    list_ref[3:8, :] = jnp.zeros((5, 128), jnp.int32)
    each(n_obs, lambda k: send(k).wait(), 1)


def step_kernel(
    n_src, n_obs, bd, req, info, lst, info_v, list_v, tiles_ref, hist_ref, inc_ref, near_ref,
    out_ref, flags_ref,
    tile, hist, inc, near, rows1, rows2, rows0, send1, send2, send0, mark,
    y_one, y_high, y_rest, y_new, pick1, pick2, pick0, part_old, part1, part2, recv1, recv2, drive,
    tile_sem, load_sem, fsend, frecv, send_sem1, recv_sem1, send_sem2, recv_sem2, send_sem0, recv_sem0,
    rsend1, rrecv1, rsend2, rrecv2,
):
    me_s, me_o = lax.axis_index("src"), lax.axis_index("obs")
    entered = greet(1, 1, n_src, n_obs)
    n_tiles = tiles_ref.shape[0]
    chunks = tile_sem.shape[0]
    chunk = n_tiles // chunks
    width = tiles_ref.shape[2]
    coefs = hist_ref.shape[1]
    blocks = n_src * bd
    load_hist = pltpu.make_async_copy(hist_ref, hist, load_sem.at[0])
    load_near = pltpu.make_async_copy(near_ref, near, load_sem.at[1])
    load_inc = pltpu.make_async_copy(inc_ref, inc, load_sem.at[2])

    def load_tiles(c):
        at = pl.ds(c * chunk, chunk)
        return pltpu.make_async_copy(tiles_ref.at[at], tile.at[at], tile_sem.at[c])

    load_hist.start()
    flag = req[0, 0, 127]
    for o in range(1, n_obs):
        flag = jnp.maximum(flag, req[o, 0, 127])
    mark[...] = jnp.full(mark.shape, flag, jnp.int32)
    flags_ref[me_s] = mark[...]

    def gather(table, out, o, slots, first, code_to_row):
        def eight(turn):
            for i in range(8):
                r = turn * 8 + i
                out[r] = table[code_to_row(req[o, 0, first + r])]

        each(slots // 8, eight)

    def send_flag(k):
        return to_src(k, n_src, mark, flags_ref.at[me_s], fsend, frecv)

    def send_rows(k, send, rows, cap, send_sem, recv_sem):
        return to_obs(k, n_obs, send.at[k], rows.at[pl.ds(me_o * cap, cap)], send_sem, recv_sem)

    def one_dest(k):
        gather(hist, send1.at[k], lax.rem(me_o + k, n_obs), CAP, 0, lambda c: c)

    def send_one(k):
        return send_rows(k, send1, rows1, CAP, send_sem1, recv_sem1)

    load_hist.wait()
    one_dest(1)
    load_inc.start()
    load_near.start()
    each(chunks, lambda c: load_tiles(c).start())
    entered()
    send_one(1).start()

    def gather_send(k):
        one_dest(k)
        send_one(k).start()

    each(n_obs, gather_send, 2)
    each(n_src, lambda k: send_flag(k).start(), 1)
    gather(hist, rows1.at[pl.ds(me_o * CAP, CAP)], me_o, CAP, 0, lambda c: c)

    older = lambda c: jnp.maximum(c - bd, 0)
    each(n_obs, lambda k: gather(hist, send2.at[k], lax.rem(me_o + k, n_obs), CAP, 0, older), 1)
    gather(hist, rows2.at[pl.ds(me_o * CAP, CAP)], me_o, CAP, 0, older)

    row = lax.broadcasted_iota(jnp.int32, (bd, n_tiles), 0)
    row0 = lax.broadcasted_iota(jnp.int32, (bd, CAPD), 0)

    def one_pick(j):
        at = pl.ds(j * bd, bd)
        ones = lambda hit: jnp.where(hit, 1.0, 0.0).astype(jnp.bfloat16)
        pick1[j] = ones(info_v[1:2, :] - j * bd == row)
        pick2[j] = ones(info_v[2:3, :] - j * bd == row)
        pick0[j] = ones(list_v[2:3, 0:CAPD] - j * bd == row0)

    each(n_src, one_pick)

    def two_products(x0, x1, t0, t1, y, count, at):
        x = jnp.concatenate([x0.astype(jnp.float32), x1.astype(jnp.float32)], axis=0).astype(jnp.bfloat16)
        both = jnp.dot(x, jnp.concatenate([t0, t1], axis=1), preferred_element_type=jnp.float32)
        y[pl.ds(at, coefs, stride=count), :] = both[:coefs, :width]
        y[pl.ds(at + 1, coefs, stride=count), :] = both[coefs:, width:]

    def products(rows):
        def one_chunk(c):
            for i in range(0, chunk, 2):
                t = c * chunk + i
                two_products(rows[info[0, t]], rows[info[0, t + 1]], tile[t], tile[t + 1], y_one, n_tiles, t)

        return one_chunk

    def split():
        for c in range(coefs):
            lanes = slice(c * width, (c + 1) * width)

            def some(i):
                at = pl.multiple_of(i * 64, 64)
                value = y_one[pl.ds(c * n_tiles + at, 64), :]
                high = value.astype(jnp.bfloat16)
                y_high[pl.ds(at, 64), lanes] = high
                y_rest[pl.ds(at, 64), lanes] = (value - high.astype(jnp.float32)).astype(jnp.bfloat16)

            each(n_tiles // 64, some)

    def add_up(pick):
        return jnp.dot(pick, y_high[...], preferred_element_type=jnp.float32) + jnp.dot(
            pick, y_rest[...], preferred_element_type=jnp.float32
        )

    def send_part(k, part, recv, send_sem, recv_sem):
        return to_src(k, n_src, part.at[lax.rem(me_s + k, n_src)], recv.at[me_s], send_sem, recv_sem)

    def solve(which, recv, part):
        total = part[me_s].astype(jnp.float32)
        for k in range(1, n_src):
            total = total + recv[lax.rem(me_s + k, n_src)].astype(jnp.float32)
        for c in range(coefs):
            drive[pl.ds(c * bd, bd), :] = total[:, c * width : (c + 1) * width]

        def pairs(turn):
            for i in range(4):
                b = turn * 8 + 2 * i
                x0 = inc[which, b] - drive[pl.ds(b, coefs, stride=bd), :]
                x1 = inc[which, b + 1] - drive[pl.ds(b + 1, coefs, stride=bd), :]
                x = jnp.concatenate([x0, x1], axis=0).astype(jnp.bfloat16)
                both = jnp.dot(
                    x, jnp.concatenate([near[b], near[b + 1]], axis=1), preferred_element_type=jnp.float32
                )
                out_ref[which, b] = both[:coefs, :width].astype(jnp.bfloat16)
                out_ref[which, b + 1] = both[coefs:, width:].astype(jnp.bfloat16)

        each(bd // 8, pairs)

    send_two = lambda k: send_rows(k, send2, rows2, CAP, send_sem2, recv_sem2)
    each(chunks, lambda c: load_tiles(c).wait())
    each(n_obs, lambda k: send_one(k).wait(), 1)
    each(n_obs, lambda k: send_two(k).start(), 1)
    each(chunks, products(rows1))
    split()
    part_one = lambda k: send_part(k, part1, recv1, rsend1, rrecv1)

    def sum_send_one(k):
        j = lax.rem(me_s + k, n_src)
        part1[j] = add_up(pick1[j]).astype(jnp.bfloat16)
        part_one(k).start()

    each(n_src, sum_send_one, 1)
    part1[me_s] = add_up(pick1[me_s]).astype(jnp.bfloat16)
    load_inc.wait()
    load_near.wait()
    each(n_src, lambda k: part_one(k).wait(), 1)
    solve(0, recv1, part1)

    newest = out_ref.at[0]
    placed = lambda c: jnp.bitwise_and(c, bd - 1)
    send_new = lambda k: send_rows(k, send0, rows0, CAP0, send_sem0, recv_sem0)

    def gather_send_new(k):
        gather(newest, send0.at[k], lax.rem(me_o + k, n_obs), CAP0, CAP, placed)
        send_new(k).start()

    each(n_obs, gather_send_new, 1)
    gather(newest, rows0.at[pl.ds(me_o * CAP0, CAP0)], me_o, CAP0, CAP, placed)
    each(n_obs, lambda k: send_two(k).wait(), 1)
    each(chunks, products(rows2))
    split()

    def sum_old(j):
        part_old[j] = add_up(pick2[j])

    each(n_src, sum_old)
    each(n_obs, lambda k: send_new(k).wait(), 1)

    def new_products(turn):
        for i in range(0, 8, 2):
            r = turn * 8 + i
            two_products(
                rows0[lst[1, r]], rows0[lst[1, r + 1]], tile[lst[0, r]], tile[lst[0, r + 1]], y_new, CAPD, r
            )

    each(CAPD // 8, new_products)
    value = jnp.concatenate([y_new[c * CAPD : (c + 1) * CAPD, :] for c in range(coefs)], axis=1)
    high = value.astype(jnp.bfloat16)
    rest = (value - high.astype(jnp.float32)).astype(jnp.bfloat16)
    part_two = lambda k: send_part(k, part2, recv2, rsend2, rrecv2)

    def sum_two(j):
        added = jnp.dot(pick0[j], high, preferred_element_type=jnp.float32) + jnp.dot(
            pick0[j], rest, preferred_element_type=jnp.float32
        )
        part2[j] = (part_old[j] + added).astype(jnp.bfloat16)

    def sum_send_two(k):
        sum_two(lax.rem(me_s + k, n_src))
        part_two(k).start()

    each(n_src, sum_send_two, 1)
    sum_two(me_s)
    each(n_src, lambda k: part_two(k).wait(), 1)
    solve(1, recv2, part2)
    each(n_src, lambda k: send_flag(k).wait(), 1)


def dense_path(tile_rows, index_rows, live_count, history, incident, near_inverse, n_src, n_obs):
    bd, width = near_inverse.shape[:2]
    slots, coefs = history.shape[:2]
    n_tiles = tile_rows.shape[0]
    group = min(64, n_tiles)

    def gather_obs(block):
        ring = [(i, (i + 1) % n_obs) for i in range(n_obs)]
        me = lax.axis_index("obs")
        whole = jnp.zeros((n_obs,) + block.shape, block.dtype)

        def hop(k, carry):
            whole, moving = carry
            whole = lax.dynamic_update_index_in_dim(whole, moving, lax.rem(me - k + n_obs, n_obs), 0)
            return whole, lax.ppermute(moving, "obs", ring)

        return lax.fori_loop(0, n_obs, hop, (whole, block))[0]

    def sum_src(value):
        ring = [(i, (i + 1) % n_src) for i in range(n_src)]

        def hop(k, carry):
            total, moving = carry
            moving = lax.ppermute(moving, "src", ring)
            return total + moving, moving

        return lax.fori_loop(0, n_src - 1, hop, (value, value))[0]

    def accumulate(chooser):
        def one_group(turn, partial):
            start = turn * group
            tile_part = lax.dynamic_slice_in_dim(tile_rows, start, group, 0)
            index_part = lax.dynamic_slice_in_dim(index_rows, start, group, 1)
            products = jnp.einsum(
                "gck,gki->gci", chooser(index_part), tile_part, preferred_element_type=jnp.float32
            )
            alive = start + jnp.arange(group, dtype=jnp.int32) < live_count
            products = jnp.where(alive[:, None, None], products, 0.0)
            return partial.at[index_part[0]].add(products)

        initial = jnp.zeros((bd * n_src, coefs, width), jnp.float32)
        return lax.fori_loop(0, n_tiles // group, one_group, initial)

    def settle(partial, drive):
        own = lax.dynamic_slice_in_dim(sum_src(partial), lax.axis_index("src") * bd, bd, 0)
        right = (drive - own).astype(jnp.bfloat16)
        solved = jnp.einsum("bck,bki->bci", right, near_inverse, preferred_element_type=jnp.float32)
        return solved.astype(jnp.bfloat16)

    past = gather_obs(history)

    def pick(block, index_part, slot):
        return past[index_part[1] // bd, slot, index_part[1] % bd]

    past = past.reshape(n_obs, slots, coefs, bd, width).transpose(0, 1, 3, 2, 4)
    first = settle(accumulate(lambda ip: pick(past, ip, ip[2])), incident[0])
    newest = gather_obs(first)

    def second_rows(ip):
        older = pick(past, ip, jnp.maximum(ip[2] - 1, 0))
        newer = newest[ip[1] // bd, ip[1] % bd]
        return jnp.where((ip[2] == 0)[:, None, None], newer, older)

    second = settle(accumulate(second_rows), incident[1])
    return jnp.stack([first, second])


def solution(mesh):
    n_src, n_obs = mesh.shape["src"], mesh.shape["obs"]
    vmem = pl.BlockSpec(memory_space=pltpu.VMEM)
    smem = pl.BlockSpec(memory_space=pltpu.SMEM)
    anywhere = pl.BlockSpec(memory_space=pl.ANY)
    dma = pltpu.SemaphoreType.DMA
    f32, bf16, i32 = jnp.float32, jnp.bfloat16, jnp.int32

    def params(i):
        return pltpu.CompilerParams(collective_id=i, has_side_effects=True)

    def on_device(tiles, tile_index, tile_count, history, incident, near_inverse):
        n_tiles, width = tiles.shape[2], tiles.shape[4]
        bd = near_inverse.shape[0]
        slots, coefs = history.shape[:2]
        tile_rows = tiles.reshape(n_tiles, width, width)
        index_rows = tile_index.transpose(0, 2, 1, 3).reshape(3, 1, n_tiles)
        hist = history.reshape(slots, coefs, bd, width).transpose(0, 2, 1, 3).reshape(slots * bd, coefs, width)
        drive = incident.reshape(2, coefs, bd, width).transpose(0, 2, 1, 3)

        requests, info, newest = pl.pallas_call(
            functools.partial(request_kernel, n_src, n_obs, bd),
            name="requests",
            out_shape=(
                jax.ShapeDtypeStruct((n_obs, 1, 128), i32),
                jax.ShapeDtypeStruct((8, n_tiles), i32),
                jax.ShapeDtypeStruct((8, 128), i32),
            ),
            in_specs=[vmem, smem],
            out_specs=(vmem, vmem, vmem),
            scratch_shapes=[pltpu.VMEM((n_obs, 1, 128), i32), dma((n_obs,)), dma((n_obs,))],
            compiler_params=params(0),
        )(index_rows, tile_count)

        def rows(cap):
            return pltpu.VMEM((n_obs * cap, coefs, width), bf16)

        def sends(cap):
            return pltpu.VMEM((n_obs, cap, coefs, width), bf16)

        def parts(kind):
            return pltpu.VMEM((n_src, bd, coefs * width), kind)

        chunks = max(1, n_tiles // 32)
        both, flags = pl.pallas_call(
            functools.partial(step_kernel, n_src, n_obs, bd),
            name="step",
            out_shape=(
                jax.ShapeDtypeStruct((2, bd, coefs, width), bf16),
                jax.ShapeDtypeStruct((n_src, 1, 128), i32),
            ),
            in_specs=[smem, smem, smem, vmem, vmem, anywhere, anywhere, anywhere, anywhere],
            out_specs=(vmem, vmem),
            scratch_shapes=[
                pltpu.VMEM((n_tiles, width, width), bf16),
                pltpu.VMEM(hist.shape, bf16),
                pltpu.VMEM(drive.shape, f32),
                pltpu.VMEM((bd, width, width), bf16),
                rows(CAP), rows(CAP), rows(CAP0), sends(CAP), sends(CAP), sends(CAP0),
                pltpu.VMEM((1, 128), i32),
                pltpu.VMEM((coefs * n_tiles, width), f32),
                pltpu.VMEM((n_tiles, coefs * width), bf16),
                pltpu.VMEM((n_tiles, coefs * width), bf16),
                pltpu.VMEM((coefs * CAPD, width), f32),
                pltpu.VMEM((n_src, bd, n_tiles), bf16),
                pltpu.VMEM((n_src, bd, n_tiles), bf16),
                pltpu.VMEM((n_src, bd, CAPD), bf16),
                parts(f32), parts(bf16), parts(bf16), parts(bf16), parts(bf16),
                pltpu.VMEM((coefs * bd, width), f32),
                dma((chunks,)), dma((3,)),
                dma((n_src,)), dma((n_src,)),
                dma((n_obs,)), dma((n_obs,)), dma((n_obs,)), dma((n_obs,)), dma((n_obs,)), dma((n_obs,)),
                dma((n_src,)), dma((n_src,)), dma((n_src,)), dma((n_src,)),
            ],
            compiler_params=params(1),
        )(requests, info, newest, info, newest, tile_rows, hist, drive, near_inverse)
        crowded = jnp.max(flags) > 0

        both = lax.cond(
            crowded,
            lambda kept: dense_path(
                tile_rows, tile_index.reshape(3, n_tiles), tile_count.reshape(()), history, drive, near_inverse,
                n_src, n_obs,
            ),
            lambda kept: kept,
            both,
        )
        return both.transpose(0, 2, 1, 3).reshape(2, coefs, bd * width)

    in_specs = (
        P("src", "obs", None, None, None),
        P("src", "obs", None, None),
        P("src", "obs"),
        P(None, None, ("src", "obs")),
        P(None, None, ("src", "obs")),
        P(("src", "obs"), None, None),
    )
    out_specs = P(None, None, ("src", "obs"))
    return jax.shard_map(on_device, mesh=mesh, in_specs=in_specs, out_specs=out_specs, check_vma=False)
```

```python
import functools

import jax
import jax.numpy as jnp
from jax import lax
from jax.experimental import pallas as pl
from jax.experimental.pallas import tpu as pltpu
from jax.sharding import PartitionSpec as P

MESH = pl.DeviceIdType.MESH
CAP = 60
CAP0 = 12
CAPD = 64
FAR = -(1 << 20)
AT0 = 64


def greet(src_peers, obs_peers, n_src, n_obs):
    me_s, me_o = lax.axis_index("src"), lax.axis_index("obs")
    barrier = pltpu.get_barrier_semaphore()
    if src_peers:
        for k in range(1, n_src):
            pl.semaphore_signal(
                barrier, inc=1, device_id=(lax.rem(me_s + k, n_src), me_o), device_id_type=MESH
            )
    if obs_peers:
        for k in range(1, n_obs):
            pl.semaphore_signal(
                barrier, inc=1, device_id=(me_s, lax.rem(me_o + k, n_obs)), device_id_type=MESH
            )
    total = (n_src - 1) * src_peers + (n_obs - 1) * obs_peers
    return lambda: pl.semaphore_wait(barrier, total)


def to_obs(k, n_obs, src_ref, dst_ref, send_sem, recv_sem):
    me_s, me_o = lax.axis_index("src"), lax.axis_index("obs")
    return pltpu.make_async_remote_copy(
        src_ref=src_ref, dst_ref=dst_ref, send_sem=send_sem.at[k], recv_sem=recv_sem.at[k],
        device_id=(me_s, lax.rem(me_o + k, n_obs)), device_id_type=MESH,
    )


def to_src(k, n_src, src_ref, dst_ref, send_sem, recv_sem):
    me_s, me_o = lax.axis_index("src"), lax.axis_index("obs")
    return pltpu.make_async_remote_copy(
        src_ref=src_ref, dst_ref=dst_ref, send_sem=send_sem.at[k], recv_sem=recv_sem.at[k],
        device_id=(lax.rem(me_s + k, n_src), me_o), device_id_type=MESH,
    )


def each(count, body, start=0):
    lax.fori_loop(start, count, lambda i, carry: (body(i), carry)[1], 0)


def build_requests(n_src, n_obs, bd, rows, idx_ref, cnt_ref, send_ref, info_ref, list_ref):
    n_tiles = idx_ref.shape[2]
    shift = bd.bit_length() - 1
    lane = lax.broadcasted_iota(jnp.int32, (1, n_tiles), 1)
    live = lane < cnt_ref[0, 0]
    obs_block, source, delay = idx_ref[0], idx_ref[1], idx_ref[2]
    owner = lax.shift_right_logical(source, shift)
    place = jnp.bitwise_and(source, bd - 1)
    owner_row = lax.broadcasted_iota(jnp.int32, (n_obs, n_tiles), 0)
    mine = jnp.where(jnp.logical_and(owner == owner_row, live), 1.0, 0.0)
    mine0 = jnp.where(delay == 0, mine, 0.0)
    before = jnp.where(
        lax.broadcasted_iota(jnp.int32, (n_tiles, n_tiles), 0)
        < lax.broadcasted_iota(jnp.int32, (n_tiles, n_tiles), 1),
        1.0, 0.0,
    ).astype(jnp.bfloat16)
    both = jnp.concatenate([mine, mine0], axis=0).astype(jnp.bfloat16)
    order = jnp.dot(both, before, preferred_element_type=jnp.float32)
    rank = jnp.sum(order[:n_obs] * mine, axis=0, keepdims=True)
    rank0 = jnp.sum(order[n_obs:] * mine0, axis=0, keepdims=True)
    rank_d = jnp.sum(order[n_obs:], axis=0, keepdims=True)
    newest = jnp.logical_and(live, delay == 0)
    over = jnp.where(live, jnp.where(rank >= CAP, 1.0, 0.0), 0.0) + jnp.where(
        newest, jnp.where(rank0 >= CAP0, 1.0, 0.0) + jnp.where(rank_d >= CAPD, 1.0, 0.0), 0.0
    )
    flag = jnp.where(jnp.max(over, axis=1, keepdims=True) > 0.0, 1.0, 0.0)
    rank = rank.astype(jnp.int32)
    rank0 = rank0.astype(jnp.int32)
    fits = jnp.logical_and(live, rank < CAP)
    fits0 = jnp.logical_and(newest, rank0 < CAP0)
    nowhere = n_src * bd
    info_ref[0:1, :] = jnp.clip(jnp.where(fits, owner * CAP + rank, 0), 0, n_obs * CAP - 1)
    info_ref[1:2, :] = jnp.where(live, obs_block, nowhere)
    info_ref[2:3, :] = jnp.where(jnp.logical_and(live, delay > 0), obs_block, nowhere)
    info_ref[3:8, :] = jnp.zeros((5, n_tiles), jnp.int32)
    row = lax.broadcasted_iota(jnp.int32, (128, n_tiles), 0)
    ones = lambda hit: jnp.where(hit, 1.0, 0.0).astype(jnp.bfloat16)
    key = jnp.where(fits, rank, FAR)
    key0 = jnp.where(fits0, rank0 + AT0, FAR)
    coded = jnp.concatenate([mine * place.astype(jnp.float32), mine * delay.astype(jnp.float32)], axis=0)

    def find(codes, hit):
        return lax.dot_general(
            codes.astype(jnp.bfloat16), ones(hit), (((1,), (1,)), ((), ())), preferred_element_type=jnp.float32
        )

    found = find(coded, jnp.logical_or(key == row, key0 == row))
    code = found[:n_obs] + found[n_obs:] * bd
    out_lane = lax.broadcasted_iota(jnp.int32, (n_obs, 128), 1)
    code = jnp.clip(jnp.where(out_lane == 127, flag, code).astype(jnp.int32), 0, rows - 1)
    for o in range(n_obs):
        send_ref[o] = code[o : o + 1]

    def build_list():
        key_d = jnp.where(newest, rank_d.astype(jnp.int32), FAR)
        code_row = lax.broadcasted_iota(jnp.int32, (16, n_tiles), 0)
        codes = jnp.zeros((16, n_tiles), jnp.int32)
        slot0 = jnp.where(fits0, owner * CAP0 + rank0, 0)
        parts = (
            jnp.bitwise_and(lane, 127), lax.shift_right_logical(lane, 7), slot0,
            jnp.bitwise_and(obs_block, 127), lax.shift_right_logical(obs_block, 7), jnp.ones_like(lane),
        )
        for i, part in enumerate(parts):
            codes = jnp.where(code_row == i, part, codes)
        found = find(codes.astype(jnp.float32), key_d == row)
        list_ref[0:1, :] = jnp.clip((found[0:1, :] + found[1:2, :] * 128.0).astype(jnp.int32), 0, n_tiles - 1)
        list_ref[1:2, :] = jnp.clip(found[2:3, :].astype(jnp.int32), 0, n_obs * CAP0 - 1)
        block = jnp.where(found[5:6, :] > 0.5, found[3:4, :] + found[4:5, :] * 128.0, 1.0 * nowhere)
        list_ref[2:3, :] = block.astype(jnp.int32)
        list_ref[3:8, :] = jnp.zeros((5, 128), jnp.int32)

    return build_list


def step_kernel(
    n_src, n_obs, bd, cnt_ref, idx_ref, tiles_ref, hist_ref, inc_ref, near_ref,
    out_ref, crowded_ref,
    ask, asked, info_v, list_v, req, info, lst, flags,
    tile, hist, inc, near, rows1, rows2, rows0, send1, send2, send0, mark,
    y_one, y_all, y_new, pick1, pick2, pick0, part_old, part1, part2, recv1, recv2, drive,
    tile_sem, load_sem, ask_send, ask_recv, fsend, frecv, send_sem1, recv_sem1, send_sem2, recv_sem2,
    send_sem0, recv_sem0, rsend1, rrecv1, rsend2, rrecv2,
):
    me_s, me_o = lax.axis_index("src"), lax.axis_index("obs")
    entered = greet(1, 1, n_src, n_obs)
    n_tiles = tiles_ref.shape[0]
    chunks = tile_sem.shape[0]
    chunk = n_tiles // chunks
    width = tiles_ref.shape[2]
    coefs = hist_ref.shape[1]
    load_hist = pltpu.make_async_copy(hist_ref, hist, load_sem.at[0])
    load_near = pltpu.make_async_copy(near_ref, near, load_sem.at[1])
    load_inc = pltpu.make_async_copy(inc_ref, inc, load_sem.at[2])

    def load_tiles(c):
        at = pl.ds(c * chunk, chunk)
        return pltpu.make_async_copy(tiles_ref.at[at], tile.at[at], tile_sem.at[c])

    load_hist.start()
    build_list = build_requests(n_src, n_obs, bd, hist_ref.shape[0], idx_ref, cnt_ref, ask, info_v, list_v)
    asked[me_o] = ask[me_o]

    def send_ask(k):
        return to_obs(k, n_obs, ask.at[lax.rem(me_o + k, n_obs)], asked.at[me_o], ask_send, ask_recv)

    entered()
    each(n_obs, lambda k: send_ask(k).start(), 1)
    build_list()
    info_down = pltpu.make_async_copy(info_v, info, load_sem.at[3])
    list_down = pltpu.make_async_copy(list_v, lst, load_sem.at[4])
    info_down.start()
    list_down.start()
    ones = lambda hit: jnp.where(hit, 1.0, 0.0).astype(jnp.bfloat16)
    row = lax.broadcasted_iota(jnp.int32, (bd, n_tiles), 0)
    row0 = lax.broadcasted_iota(jnp.int32, (bd, CAPD), 0)

    def one_pick(k):
        first = lax.rem(me_s + k + 1, n_src) * bd
        at = pl.ds(pl.multiple_of(k * bd, bd), bd)
        pick1[at, :] = ones(info_v[1:2, :] - first == row)
        pick2[at, :] = ones(info_v[2:3, :] - first == row)
        pick0[at, :] = ones(list_v[2:3, 0:CAPD] - first == row0)

    each(n_src, one_pick)
    each(n_obs, lambda k: send_ask(k).wait(), 1)
    req_down = pltpu.make_async_copy(asked, req, load_sem.at[5])
    req_down.start()
    worst = jnp.max(asked[...].astype(jnp.float32), axis=0)
    worst = jnp.where(lax.broadcasted_iota(jnp.int32, worst.shape, 1) == 127, worst, 0.0)
    mark[...] = jnp.broadcast_to(jnp.max(worst, axis=1, keepdims=True), mark.shape)
    flags[me_s] = mark[...]

    def gather(table, out, o, slots, first, code_to_row):
        def twelve(turn):
            for i in range(12):
                r = turn * 12 + i
                out[r] = table[code_to_row(req[o, 0, first + r])]

        each(slots // 12, twelve)

    def send_flag(k):
        return to_src(k, n_src, mark, flags.at[me_s], fsend, frecv)

    def send_rows(k, send, rows, cap, send_sem, recv_sem):
        return to_obs(k, n_obs, send.at[k], rows.at[pl.ds(me_o * cap, cap)], send_sem, recv_sem)

    def one_dest(k):
        gather(hist, send1.at[k], lax.rem(me_o + k, n_obs), CAP, 0, lambda c: c)

    def send_one(k):
        return send_rows(k, send1, rows1, CAP, send_sem1, recv_sem1)

    load_hist.wait()
    req_down.wait()

    def gather_send(k):
        one_dest(k)
        send_one(k).start()

    each(n_obs, gather_send, 1)
    each(chunks, lambda c: load_tiles(c).start())
    load_inc.start()
    load_near.start()
    each(n_src, lambda k: send_flag(k).start(), 1)
    gather(hist, rows1.at[pl.ds(me_o * CAP, CAP)], me_o, CAP, 0, lambda c: c)

    older = lambda c: jnp.maximum(c - bd, 0)
    each(n_obs, lambda k: gather(hist, send2.at[k], lax.rem(me_o + k, n_obs), CAP, 0, older), 1)
    gather(hist, rows2.at[pl.ds(me_o * CAP, CAP)], me_o, CAP, 0, older)

    def two_products(x0, x1, t0, t1, y, count, at):
        x = jnp.concatenate([x0.astype(jnp.float32), x1.astype(jnp.float32)], axis=0).astype(jnp.bfloat16)
        both = jnp.dot(x, jnp.concatenate([t0, t1], axis=1), preferred_element_type=jnp.float32)
        y[pl.ds(at, coefs, stride=count), :] = both[:coefs, :width]
        y[pl.ds(at + 1, coefs, stride=count), :] = both[coefs:, width:]

    def products(rows):
        def one_chunk(c):
            for i in range(0, chunk, 2):
                t = c * chunk + i
                two_products(rows[info[0, t]], rows[info[0, t + 1]], tile[t], tile[t + 1], y_one, n_tiles, t)

        return one_chunk

    def pack():
        for c in range(coefs):
            lanes = slice(c * width, (c + 1) * width)

            def some(i):
                at = pl.multiple_of(i * 64, 64)
                y_all[pl.ds(at, 64), lanes] = y_one[pl.ds(c * n_tiles + at, 64), :].astype(jnp.bfloat16)

            each(n_tiles // 64, some)

    def send_part(k, part, recv, send_sem, recv_sem):
        return to_src(k, n_src, part.at[pl.ds((k - 1) * bd, bd)], recv.at[me_s], send_sem, recv_sem)

    group = n_src // 2
    half = lambda g: slice(g * group * bd, (g + 1) * group * bd)

    def solve(which, recv, part):
        total = part[(n_src - 1) * bd :, :].astype(jnp.float32)
        for k in range(1, n_src):
            total = total + recv[lax.rem(me_s + k, n_src)].astype(jnp.float32)
        for c in range(coefs):
            drive[pl.ds(c * bd, bd), :] = total[:, c * width : (c + 1) * width]

        def pairs(turn):
            for i in range(4):
                b = turn * 8 + 2 * i
                x0 = inc[which, b] - drive[pl.ds(b, coefs, stride=bd), :]
                x1 = inc[which, b + 1] - drive[pl.ds(b + 1, coefs, stride=bd), :]
                x = jnp.concatenate([x0, x1], axis=0).astype(jnp.bfloat16)
                both = jnp.dot(
                    x, jnp.concatenate([near[b], near[b + 1]], axis=1), preferred_element_type=jnp.float32
                )
                out_ref[which, b] = both[:coefs, :width].astype(jnp.bfloat16)
                out_ref[which, b + 1] = both[coefs:, width:].astype(jnp.bfloat16)

        each(bd // 8, pairs)

    send_two = lambda k: send_rows(k, send2, rows2, CAP, send_sem2, recv_sem2)
    each(chunks, lambda c: load_tiles(c).wait())
    info_down.wait()
    each(n_obs, lambda k: send_one(k).wait(), 1)
    each(n_obs, lambda k: send_two(k).start(), 1)
    each(chunks, products(rows1))
    pack()
    part_one = lambda k: send_part(k, part1, recv1, rsend1, rrecv1)
    for g in range(2):
        part1[half(g), :] = jnp.dot(
            pick1[half(g), :], y_all[...], preferred_element_type=jnp.float32
        ).astype(jnp.bfloat16)
        each(min(group * (g + 1) + 1, n_src), lambda k: part_one(k).start(), group * g + 1)
    load_inc.wait()
    load_near.wait()
    each(n_src, lambda k: part_one(k).wait(), 1)
    each(n_src, lambda k: send_flag(k).wait(), 1)
    solve(0, recv1, part1)

    newest = out_ref.at[0]
    placed = lambda c: jnp.bitwise_and(c, bd - 1)
    send_new = lambda k: send_rows(k, send0, rows0, CAP0, send_sem0, recv_sem0)

    def gather_send_new(k):
        gather(newest, send0.at[k], lax.rem(me_o + k, n_obs), CAP0, AT0, placed)
        send_new(k).start()

    each(n_obs, gather_send_new, 1)
    gather(newest, rows0.at[pl.ds(me_o * CAP0, CAP0)], me_o, CAP0, AT0, placed)
    each(n_obs, lambda k: send_two(k).wait(), 1)
    each(chunks, products(rows2))
    pack()
    for g in range(2):
        part_old[half(g), :] = jnp.dot(pick2[half(g), :], y_all[...], preferred_element_type=jnp.float32)
    list_down.wait()
    each(n_obs, lambda k: send_new(k).wait(), 1)

    def new_products(turn):
        for i in range(0, 8, 2):
            r = turn * 8 + i
            two_products(
                rows0[lst[1, r]], rows0[lst[1, r + 1]], tile[lst[0, r]], tile[lst[0, r + 1]], y_new, CAPD, r
            )

    each(CAPD // 8, new_products)
    value = jnp.concatenate([y_new[c * CAPD : (c + 1) * CAPD, :] for c in range(coefs)], axis=1)
    value = value.astype(jnp.bfloat16)
    part_two = lambda k: send_part(k, part2, recv2, rsend2, rrecv2)
    for g in range(2):
        added = jnp.dot(pick0[half(g), :], value, preferred_element_type=jnp.float32)
        part2[half(g), :] = (part_old[half(g), :] + added).astype(jnp.bfloat16)
        each(min(group * (g + 1) + 1, n_src), lambda k: part_two(k).start(), group * g + 1)
    each(n_src, lambda k: part_two(k).wait(), 1)
    solve(1, recv2, part2)
    crowded_ref[0, 0] = jnp.max(flags[...])


def dense_path(tile_rows, index_rows, live_count, history, incident, near_inverse, n_src, n_obs):
    bd, width = near_inverse.shape[:2]
    slots, coefs = history.shape[:2]
    n_tiles = tile_rows.shape[0]
    group = min(64, n_tiles)

    def gather_obs(block):
        ring = [(i, (i + 1) % n_obs) for i in range(n_obs)]
        me = lax.axis_index("obs")
        whole = jnp.zeros((n_obs,) + block.shape, block.dtype)

        def hop(k, carry):
            whole, moving = carry
            whole = lax.dynamic_update_index_in_dim(whole, moving, lax.rem(me - k + n_obs, n_obs), 0)
            return whole, lax.ppermute(moving, "obs", ring)

        return lax.fori_loop(0, n_obs, hop, (whole, block))[0]

    def sum_src(value):
        ring = [(i, (i + 1) % n_src) for i in range(n_src)]

        def hop(k, carry):
            total, moving = carry
            moving = lax.ppermute(moving, "src", ring)
            return total + moving, moving

        return lax.fori_loop(0, n_src - 1, hop, (value, value))[0]

    def accumulate(chooser):
        def one_group(turn, partial):
            start = turn * group
            tile_part = lax.dynamic_slice_in_dim(tile_rows, start, group, 0)
            index_part = lax.dynamic_slice_in_dim(index_rows, start, group, 1)
            products = jnp.einsum(
                "gck,gki->gci", chooser(index_part), tile_part, preferred_element_type=jnp.float32
            )
            alive = start + jnp.arange(group, dtype=jnp.int32) < live_count
            products = jnp.where(alive[:, None, None], products, 0.0)
            return partial.at[index_part[0]].add(products)

        initial = jnp.zeros((bd * n_src, coefs, width), jnp.float32)
        return lax.fori_loop(0, n_tiles // group, one_group, initial)

    def settle(partial, drive):
        own = lax.dynamic_slice_in_dim(sum_src(partial), lax.axis_index("src") * bd, bd, 0)
        right = (drive - own).astype(jnp.bfloat16)
        solved = jnp.einsum("bck,bki->bci", right, near_inverse, preferred_element_type=jnp.float32)
        return solved.astype(jnp.bfloat16)

    past = gather_obs(history)

    def pick(block, index_part, slot):
        return past[index_part[1] // bd, slot, index_part[1] % bd]

    past = past.reshape(n_obs, slots, coefs, bd, width).transpose(0, 1, 3, 2, 4)
    first = settle(accumulate(lambda ip: pick(past, ip, ip[2])), incident[0])
    newest = gather_obs(first)

    def second_rows(ip):
        older = pick(past, ip, jnp.maximum(ip[2] - 1, 0))
        newer = newest[ip[1] // bd, ip[1] % bd]
        return jnp.where((ip[2] == 0)[:, None, None], newer, older)

    second = settle(accumulate(second_rows), incident[1])
    return jnp.stack([first, second])


def solution(mesh):
    n_src, n_obs = mesh.shape["src"], mesh.shape["obs"]
    vmem = pl.BlockSpec(memory_space=pltpu.VMEM)
    smem = pl.BlockSpec(memory_space=pltpu.SMEM)
    hbm = pl.BlockSpec(memory_space=pltpu.HBM)
    dma = pltpu.SemaphoreType.DMA
    f32, bf16, i32 = jnp.float32, jnp.bfloat16, jnp.int32

    def params(i):
        return pltpu.CompilerParams(collective_id=i, has_side_effects=True)

    def on_device(tiles, tile_index, tile_count, history, incident, near_inverse):
        n_tiles, width = tiles.shape[2], tiles.shape[4]
        bd = near_inverse.shape[0]
        slots, coefs = history.shape[:2]
        tile_rows = tiles.reshape(n_tiles, width, width)
        index_rows = tile_index.transpose(0, 2, 1, 3).reshape(3, 1, n_tiles)
        hist = history.reshape(slots, coefs, bd, width).transpose(0, 2, 1, 3).reshape(slots * bd, coefs, width)
        drive = incident.reshape(2, coefs, bd, width).transpose(0, 2, 1, 3)

        def rows(cap):
            return pltpu.VMEM((n_obs * cap, coefs, width), bf16)

        def sends(cap):
            return pltpu.VMEM((n_obs, cap, coefs, width), bf16)

        def parts(kind):
            return pltpu.VMEM((n_src * bd, coefs * width), kind)

        arrived = pltpu.VMEM((n_src, bd, coefs * width), bf16)

        chunks = max(1, n_tiles // 32)
        both, crowded = pl.pallas_call(
            functools.partial(step_kernel, n_src, n_obs, bd),
            name="step",
            out_shape=(
                jax.ShapeDtypeStruct((2, bd, coefs, width), bf16),
                jax.ShapeDtypeStruct((1, 1), f32),
            ),
            in_specs=[smem, vmem, hbm, hbm, hbm, hbm],
            out_specs=(vmem, smem),
            scratch_shapes=[
                pltpu.VMEM((n_obs, 1, 128), i32), pltpu.VMEM((n_obs, 1, 128), i32),
                pltpu.VMEM((8, n_tiles), i32), pltpu.VMEM((8, 128), i32),
                pltpu.SMEM((n_obs, 1, 128), i32), pltpu.SMEM((8, n_tiles), i32), pltpu.SMEM((8, 128), i32),
                pltpu.VMEM((n_src, 1, 128), f32),
                pltpu.VMEM((n_tiles, width, width), bf16),
                pltpu.VMEM(hist.shape, bf16),
                pltpu.VMEM(drive.shape, f32),
                pltpu.VMEM((bd, width, width), bf16),
                rows(CAP), rows(CAP), rows(CAP0), sends(CAP), sends(CAP), sends(CAP0),
                pltpu.VMEM((1, 128), f32),
                pltpu.VMEM((coefs * n_tiles, width), f32),
                pltpu.VMEM((n_tiles, coefs * width), bf16),
                pltpu.VMEM((coefs * CAPD, width), f32),
                pltpu.VMEM((n_src * bd, n_tiles), bf16),
                pltpu.VMEM((n_src * bd, n_tiles), bf16),
                pltpu.VMEM((n_src * bd, CAPD), bf16),
                parts(f32), parts(bf16), parts(bf16), arrived, arrived,
                pltpu.VMEM((coefs * bd, width), f32),
                dma((chunks,)), dma((6,)), dma((n_obs,)), dma((n_obs,)),
                dma((n_src,)), dma((n_src,)),
                dma((n_obs,)), dma((n_obs,)), dma((n_obs,)), dma((n_obs,)), dma((n_obs,)), dma((n_obs,)),
                dma((n_src,)), dma((n_src,)), dma((n_src,)), dma((n_src,)),
            ],
            compiler_params=params(0),
        )(tile_count, index_rows, tile_rows, hist, drive, near_inverse)

        both = lax.cond(
            crowded[0, 0] > 0.0,
            lambda kept: dense_path(
                tile_rows, tile_index.reshape(3, n_tiles), tile_count.reshape(()), history, drive, near_inverse,
                n_src, n_obs,
            ),
            lambda kept: kept,
            both,
        )
        return both.transpose(0, 2, 1, 3).reshape(2, coefs, bd * width)

    in_specs = (
        P("src", "obs", None, None, None),
        P("src", "obs", None, None),
        P("src", "obs"),
        P(None, None, ("src", "obs")),
        P(None, None, ("src", "obs")),
        P(("src", "obs"), None, None),
    )
    out_specs = P(None, None, ("src", "obs"))
    return jax.shard_map(on_device, mesh=mesh, in_specs=in_specs, out_specs=out_specs, check_vma=False)
```

```python
import functools

import jax
import jax.numpy as jnp
from jax import lax
from jax.experimental import pallas as pl
from jax.experimental.pallas import tpu as pltpu
from jax.sharding import PartitionSpec as P

MESH = pl.DeviceIdType.MESH
CAP = 60
CAP0 = 12
CAPD = 64
FAR = -(1 << 20)
ORDER = (10, 11, 8, 9, 6, 14, 7, 15, 4, 12, 5, 13, 2, 3, 1)
STAGED = (False, False)
AT0 = 64


def greet(src_peers, obs_peers, n_src, n_obs):
    me_s, me_o = lax.axis_index("src"), lax.axis_index("obs")
    barrier = pltpu.get_barrier_semaphore()
    if src_peers:
        for k in range(1, n_src):
            pl.semaphore_signal(
                barrier, inc=1, device_id=(lax.rem(me_s + k, n_src), me_o), device_id_type=MESH
            )
    if obs_peers:
        for k in range(1, n_obs):
            pl.semaphore_signal(
                barrier, inc=1, device_id=(me_s, obs_peer(k, n_obs)), device_id_type=MESH
            )
    total = (n_src - 1) * src_peers + (n_obs - 1) * obs_peers
    return lambda: pl.semaphore_wait(barrier, total)


def obs_peer(k, n_obs):
    me = lax.axis_index("obs")
    x = lax.rem(me // 4 + k // 4, n_obs // 4)
    z = lax.rem(lax.rem(me // 2, 2) + lax.rem(k // 2, 2), 2)
    core = lax.rem(lax.rem(me, 2) + lax.rem(k, 2), 2)
    return x * 4 + z * 2 + core


def to_obs(k, n_obs, src_ref, dst_ref, send_sem, recv_sem):
    return pltpu.make_async_remote_copy(
        src_ref=src_ref, dst_ref=dst_ref, send_sem=send_sem, recv_sem=recv_sem,
        device_id=(lax.axis_index("src"), obs_peer(k, n_obs)), device_id_type=MESH,
    )


def to_src(peer, src_ref, dst_ref, send_sem, recv_sem):
    return pltpu.make_async_remote_copy(
        src_ref=src_ref, dst_ref=dst_ref, send_sem=send_sem, recv_sem=recv_sem,
        device_id=(peer, lax.axis_index("obs")), device_id_type=MESH,
    )


def take(ref, sem):
    pltpu.make_async_copy(ref, ref, sem).wait()


def each(count, body, start=0):
    lax.fori_loop(start, count, lambda i, carry: (body(i), carry)[1], 0)


def build_requests(n_src, n_obs, bd, rows, idx_ref, cnt_ref, send_ref, info_ref, list_ref):
    n_tiles = idx_ref.shape[2]
    shift = bd.bit_length() - 1
    lane = lax.broadcasted_iota(jnp.int32, (1, n_tiles), 1)
    live = lane < cnt_ref[...]
    obs_block, source, delay = idx_ref[0], idx_ref[1], idx_ref[2]
    owner = lax.shift_right_logical(source, shift)
    place = jnp.bitwise_and(source, bd - 1)
    owner_row = lax.broadcasted_iota(jnp.int32, (n_obs, n_tiles), 0)
    mine = jnp.where(jnp.logical_and(owner == owner_row, live), 1.0, 0.0)
    mine0 = jnp.where(delay == 0, mine, 0.0)
    before = jnp.where(
        lax.broadcasted_iota(jnp.int32, (n_tiles, n_tiles), 0)
        < lax.broadcasted_iota(jnp.int32, (n_tiles, n_tiles), 1),
        1.0, 0.0,
    ).astype(jnp.bfloat16)
    both = jnp.concatenate([mine, mine0], axis=0).astype(jnp.bfloat16)
    order = jnp.dot(both, before, preferred_element_type=jnp.float32)
    rank = jnp.sum(order[:n_obs] * mine, axis=0, keepdims=True)
    rank0 = jnp.sum(order[n_obs:] * mine0, axis=0, keepdims=True)
    rank_d = jnp.sum(order[n_obs:], axis=0, keepdims=True)
    newest = jnp.logical_and(live, delay == 0)
    over = jnp.where(live, jnp.where(rank >= CAP, 1.0, 0.0), 0.0) + jnp.where(
        newest, jnp.where(rank0 >= CAP0, 1.0, 0.0) + jnp.where(rank_d >= CAPD, 1.0, 0.0), 0.0
    )
    flag = jnp.where(jnp.max(over, axis=1, keepdims=True) > 0.0, 1.0, 0.0)
    rank = rank.astype(jnp.int32)
    rank0 = rank0.astype(jnp.int32)
    fits = jnp.logical_and(live, rank < CAP)
    fits0 = jnp.logical_and(newest, rank0 < CAP0)
    nowhere = n_src * bd
    info_ref[0:1, :] = jnp.clip(jnp.where(fits, owner * CAP + rank, 0), 0, n_obs * CAP - 1)
    info_ref[1:2, :] = jnp.where(live, obs_block, nowhere)
    info_ref[2:3, :] = jnp.where(jnp.logical_and(live, delay > 0), obs_block, nowhere)
    info_ref[3:8, :] = jnp.zeros((5, n_tiles), jnp.int32)
    row = lax.broadcasted_iota(jnp.int32, (128, n_tiles), 0)
    ones = lambda hit: jnp.where(hit, 1.0, 0.0).astype(jnp.bfloat16)
    key = jnp.where(fits, rank, FAR)
    key0 = jnp.where(fits0, rank0 + AT0, FAR)
    coded = jnp.concatenate([mine * place.astype(jnp.float32), mine * delay.astype(jnp.float32)], axis=0)

    def find(codes, hit):
        return lax.dot_general(
            codes.astype(jnp.bfloat16), ones(hit), (((1,), (1,)), ((), ())), preferred_element_type=jnp.float32
        )

    found = find(coded, jnp.logical_or(key == row, key0 == row))
    code = found[:n_obs] + found[n_obs:] * bd
    out_lane = lax.broadcasted_iota(jnp.int32, (n_obs, 128), 1)
    code = jnp.clip(jnp.where(out_lane == 127, flag, code).astype(jnp.int32), 0, rows - 1)
    for o in range(n_obs):
        send_ref[o] = code[o : o + 1]

    def build_list():
        key_d = jnp.where(newest, rank_d.astype(jnp.int32), FAR)
        code_row = lax.broadcasted_iota(jnp.int32, (16, n_tiles), 0)
        codes = jnp.zeros((16, n_tiles), jnp.int32)
        slot0 = jnp.where(fits0, owner * CAP0 + rank0, 0)
        parts = (
            jnp.bitwise_and(lane, 127), lax.shift_right_logical(lane, 7), slot0,
            jnp.bitwise_and(obs_block, 127), lax.shift_right_logical(obs_block, 7), jnp.ones_like(lane),
        )
        for i, part in enumerate(parts):
            codes = jnp.where(code_row == i, part, codes)
        found = find(codes.astype(jnp.float32), key_d == row)
        list_ref[0:1, :] = jnp.clip((found[0:1, :] + found[1:2, :] * 128.0).astype(jnp.int32), 0, n_tiles - 1)
        list_ref[1:2, :] = jnp.clip(found[2:3, :].astype(jnp.int32), 0, n_obs * CAP0 - 1)
        block = jnp.where(found[5:6, :] > 0.5, found[3:4, :] + found[4:5, :] * 128.0, 1.0 * nowhere)
        list_ref[2:3, :] = block.astype(jnp.int32)
        list_ref[3:8, :] = jnp.zeros((5, 128), jnp.int32)

    return build_list


def step_kernel(
    n_src, n_obs, bd, cnt_ref, idx_ref, tiles_ref, hist_ref, inc_ref, near_ref,
    out_ref, crowded_ref,
    ask, asked, info_v, list_v, req, info, lst, flags,
    tile, hist, inc, near, rows1, rows2, rows0, send1, send2, send0, mark,
    y_one, y_all, y_new, pick1, pick2, pick0, part_old, part1, part2, recv1, recv2, far_out, far_in, drive,
    tile_sem, load_sem, ask_sem, flag_sem, sem1, sem2, sem0, part_sem1, part_sem2, far_sem1, far_sem2,
):
    me_s, me_o = lax.axis_index("src"), lax.axis_index("obs")
    order = ORDER if n_obs == len(ORDER) + 1 else range(1, n_obs)
    entered = greet(1, 1, n_src, n_obs)
    n_tiles = tiles_ref.shape[0]
    chunk = min(32, n_tiles)
    chunks = n_tiles // chunk
    width = tiles_ref.shape[2]
    coefs = hist_ref.shape[1]
    load_hist = pltpu.make_async_copy(hist_ref, hist, load_sem.at[0])
    load_near = pltpu.make_async_copy(near_ref, near, load_sem.at[1])
    load_inc = pltpu.make_async_copy(inc_ref, inc, load_sem.at[2])

    def load_tiles(c):
        at = pl.ds(c * chunk, chunk)
        return pltpu.make_async_copy(tiles_ref.at[at], tile.at[at], tile_sem)

    load_hist.start()
    build_list = build_requests(n_src, n_obs, bd, hist_ref.shape[0], idx_ref, cnt_ref, ask, info_v, list_v)
    asked[me_o] = ask[me_o]

    def send_ask(k):
        return to_obs(k, n_obs, ask.at[obs_peer(k, n_obs)], asked.at[me_o], ask_sem.at[0], ask_sem.at[1])

    entered()
    each(n_obs, lambda k: send_ask(k).start(), 1)
    build_list()
    info_down = pltpu.make_async_copy(info_v, info, load_sem.at[3])
    list_down = pltpu.make_async_copy(list_v, lst, load_sem.at[4])
    info_down.start()
    list_down.start()
    ones = lambda hit: jnp.where(hit, 1.0, 0.0).astype(jnp.bfloat16)
    row = lax.broadcasted_iota(jnp.int32, (bd, n_tiles), 0)
    row0 = lax.broadcasted_iota(jnp.int32, (bd, CAPD), 0)

    n_y = n_src // 2
    me_z, me_y = me_s // n_y, lax.rem(me_s, n_y)

    def place_of(k):
        return lax.rem(me_z + 1 - k // n_y, 2) * n_y + lax.rem(me_y + 1 + lax.rem(k, n_y), n_y)

    def one_pick(k):
        first = place_of(k) * bd
        at = pl.ds(pl.multiple_of(k * bd, bd), bd)
        pick1[at, :] = ones(info_v[1:2, :] - first == row)
        pick2[at, :] = ones(info_v[2:3, :] - first == row)
        pick0[at, :] = ones(list_v[2:3, 0:CAPD] - first == row0)

    each(n_src, one_pick)
    others = pl.ds(0, n_obs - 1)
    take(asked.at[others], ask_sem.at[1])
    take(ask.at[others], ask_sem.at[0])
    req_down = pltpu.make_async_copy(asked, req, load_sem.at[5])
    req_down.start()
    worst = jnp.max(asked[...].astype(jnp.float32), axis=0)
    worst = jnp.where(lax.broadcasted_iota(jnp.int32, worst.shape, 1) == 127, worst, 0.0)
    mark[...] = jnp.broadcast_to(jnp.max(worst, axis=1, keepdims=True), mark.shape)
    flags[me_s] = mark[...]

    def gather(table, out, o, slots, first, code_to_row):
        def twelve(turn):
            for i in range(12):
                r = turn * 12 + i
                out[r] = table[code_to_row(req[o, 0, first + r])]

        each(slots // 12, twelve)

    def send_flag(k):
        return to_src(lax.rem(me_s + k, n_src), mark, flags.at[me_s], flag_sem.at[0], flag_sem.at[1])

    def send_rows(k, send, rows, cap, sem):
        return to_obs(k, n_obs, send.at[k], rows.at[pl.ds(me_o * cap, cap)], sem.at[0], sem.at[1])

    def take_rows(send, rows, cap, sem):
        take(rows.at[pl.ds(0, (n_obs - 1) * cap)], sem.at[1])
        take(send.at[pl.ds(1, n_obs - 1)], sem.at[0])

    def one_dest(k):
        gather(hist, send1.at[k], obs_peer(k, n_obs), CAP, 0, lambda c: c)

    def send_one(k):
        return send_rows(k, send1, rows1, CAP, sem1)

    load_hist.wait()
    req_down.wait()

    def gather_send(k):
        one_dest(k)
        send_one(k).start()

    for k in order:
        gather_send(k)
    each(chunks, lambda c: load_tiles(c).start())
    load_inc.start()
    load_near.start()
    each(n_src, lambda k: send_flag(k).start(), 1)
    gather(hist, rows1.at[pl.ds(me_o * CAP, CAP)], me_o, CAP, 0, lambda c: c)

    older = lambda c: jnp.maximum(c - bd, 0)
    def gather_send_two(k):
        gather(hist, send2.at[k], obs_peer(k, n_obs), CAP, 0, older)
        send_rows(k, send2, rows2, CAP, sem2).start()

    for k in order:
        gather_send_two(k)
    gather(hist, rows2.at[pl.ds(me_o * CAP, CAP)], me_o, CAP, 0, older)

    def two_products(x0, x1, t0, t1, y, count, at):
        x = jnp.concatenate([x0.astype(jnp.float32), x1.astype(jnp.float32)], axis=0).astype(jnp.bfloat16)
        both = jnp.dot(x, jnp.concatenate([t0, t1], axis=1), preferred_element_type=jnp.float32)
        y[pl.ds(at, coefs, stride=count), :] = both[:coefs, :width]
        y[pl.ds(at + 1, coefs, stride=count), :] = both[coefs:, width:]

    def products(rows):
        def one_chunk(c):
            for i in range(0, chunk, 2):
                t = c * chunk + i
                two_products(rows[info[0, t]], rows[info[0, t + 1]], tile[t], tile[t + 1], y_one, n_tiles, t)

        return one_chunk

    def pack():
        for c in range(coefs):
            lanes = slice(c * width, (c + 1) * width)

            def some(i):
                at = pl.multiple_of(i * 64, 64)
                y_all[pl.ds(at, 64), lanes] = y_one[pl.ds(c * n_tiles + at, 64), :].astype(jnp.bfloat16)

            each(n_tiles // 64, some)

    def start_half(g, staged, part, recv, sem):
        for i in range(n_y - staged if g == 0 else n_y - 1):
            k = g * n_y + i
            peer = me_z * n_y + lax.rem(me_y + 1 + i, n_y) if staged else place_of(k)
            to_src(peer, part.at[pl.ds(k * bd, bd)], recv.at[k], sem.at[0], sem.at[1 + g]).start()

    def finish(staged, part, recv, sem, far_sem):
        def half_sum(g, count):
            if count:
                take(recv.at[pl.ds(g * n_y, count)], sem.at[1 + g])
            total = part[(g * n_y + n_y - 1) * bd : (g + 1) * n_y * bd, :].astype(jnp.float32)
            for i in range(n_y - 1):
                total = total + recv[g * n_y + i].astype(jnp.float32)
            return total

        sent = n_src - 2 if staged else n_src - 1
        if staged:
            far_out[...] = half_sum(0, n_y - 1).astype(jnp.bfloat16)
            peer = lax.rem(me_z + 1, 2) * n_y + me_y
            far = to_src(peer, far_out, far_in, far_sem.at[0], far_sem.at[1])
            far.start()
            total = half_sum(1, n_y - 1)
            far.wait()
            total = total + far_in[...].astype(jnp.float32)
        else:
            take(recv.at[pl.ds(0, n_y)], sem.at[1])
            total = half_sum(1, n_y - 1)
            for k in range(n_y):
                total = total + recv[k].astype(jnp.float32)
        if sent:
            take(recv.at[pl.ds(0, sent)], sem.at[0])
        return total

    group = n_src // 2
    half = lambda g: slice(g * group * bd, (g + 1) * group * bd)

    def solve(which, total):
        for c in range(coefs):
            drive[pl.ds(c * bd, bd), :] = total[:, c * width : (c + 1) * width]

        def pairs(turn):
            for i in range(4):
                b = turn * 8 + 2 * i
                x0 = inc[which, b] - drive[pl.ds(b, coefs, stride=bd), :]
                x1 = inc[which, b + 1] - drive[pl.ds(b + 1, coefs, stride=bd), :]
                x = jnp.concatenate([x0, x1], axis=0).astype(jnp.bfloat16)
                both = jnp.dot(
                    x, jnp.concatenate([near[b], near[b + 1]], axis=1), preferred_element_type=jnp.float32
                )
                out_ref[which, b] = both[:coefs, :width].astype(jnp.bfloat16)
                out_ref[which, b + 1] = both[coefs:, width:].astype(jnp.bfloat16)

        each(bd // 8, pairs)

    take(tile, tile_sem)
    info_down.wait()
    take_rows(send1, rows1, CAP, sem1)
    each(chunks, products(rows1))
    pack()
    for g in range(2):
        part1[half(g), :] = jnp.dot(
            pick1[half(g), :], y_all[...], preferred_element_type=jnp.float32
        ).astype(jnp.bfloat16)
        start_half(g, STAGED[0], part1, recv1, part_sem1)
    load_inc.wait()
    load_near.wait()
    for side in range(2):
        take(flags.at[pl.ds(0, n_src - 1)], flag_sem.at[side])
    solve(0, finish(STAGED[0], part1, recv1, part_sem1, far_sem1))

    newest = out_ref.at[0]
    placed = lambda c: jnp.bitwise_and(c, bd - 1)
    send_new = lambda k: send_rows(k, send0, rows0, CAP0, sem0)

    def gather_send_new(k):
        gather(newest, send0.at[k], obs_peer(k, n_obs), CAP0, AT0, placed)
        send_new(k).start()

    each(n_obs, gather_send_new, 1)
    gather(newest, rows0.at[pl.ds(me_o * CAP0, CAP0)], me_o, CAP0, AT0, placed)
    take_rows(send2, rows2, CAP, sem2)
    each(chunks, products(rows2))
    pack()
    for g in range(2):
        part_old[half(g), :] = jnp.dot(pick2[half(g), :], y_all[...], preferred_element_type=jnp.float32)
    list_down.wait()
    take_rows(send0, rows0, CAP0, sem0)

    def new_products(turn):
        for i in range(0, 8, 2):
            r = turn * 8 + i
            two_products(
                rows0[lst[1, r]], rows0[lst[1, r + 1]], tile[lst[0, r]], tile[lst[0, r + 1]], y_new, CAPD, r
            )

    each(CAPD // 8, new_products)
    value = jnp.concatenate([y_new[c * CAPD : (c + 1) * CAPD, :] for c in range(coefs)], axis=1)
    value = value.astype(jnp.bfloat16)
    for g in range(2):
        added = jnp.dot(pick0[half(g), :], value, preferred_element_type=jnp.float32)
        part2[half(g), :] = (part_old[half(g), :] + added).astype(jnp.bfloat16)
        start_half(g, STAGED[1], part2, recv2, part_sem2)
    solve(1, finish(STAGED[1], part2, recv2, part_sem2, far_sem2))
    crowded_ref[0, 0] = jnp.max(flags[...])


def dense_path(tile_rows, index_rows, live_count, history, incident, near_inverse, n_src, n_obs):
    bd, width = near_inverse.shape[:2]
    slots, coefs = history.shape[:2]
    n_tiles = tile_rows.shape[0]
    group = min(64, n_tiles)

    def gather_obs(block):
        ring = [(i, (i + 1) % n_obs) for i in range(n_obs)]
        me = lax.axis_index("obs")
        whole = jnp.zeros((n_obs,) + block.shape, block.dtype)
        whole = lax.dynamic_update_index_in_dim(whole, block, me, 0)

        def hop(k, carry):
            whole, moving = carry
            whole = lax.dynamic_update_index_in_dim(whole, moving, lax.rem(me - k + n_obs, n_obs), 0)
            return whole, lax.ppermute(moving, "obs", ring)

        return lax.fori_loop(1, n_obs, hop, (whole, lax.ppermute(block, "obs", ring)))[0]

    def sum_src(value):
        ring = [(i, (i + 1) % n_src) for i in range(n_src)]

        def hop(k, carry):
            total, moving = carry
            moving = lax.ppermute(moving, "src", ring)
            return total + moving, moving

        return lax.fori_loop(0, n_src - 1, hop, (value, value))[0]

    def accumulate(chooser):
        def one_group(turn, partial):
            start = turn * group
            tile_part = lax.dynamic_slice_in_dim(tile_rows, start, group, 0)
            index_part = lax.dynamic_slice_in_dim(index_rows, start, group, 1)
            products = jnp.einsum(
                "gck,gki->gci", chooser(index_part), tile_part, preferred_element_type=jnp.float32
            )
            alive = start + jnp.arange(group, dtype=jnp.int32) < live_count
            products = jnp.where(alive[:, None, None], products, 0.0)
            return partial.at[index_part[0]].add(products)

        initial = jnp.zeros((bd * n_src, coefs, width), jnp.float32)
        return lax.fori_loop(0, n_tiles // group, one_group, initial)

    def settle(partial, drive):
        own = lax.dynamic_slice_in_dim(sum_src(partial), lax.axis_index("src") * bd, bd, 0)
        right = (drive - own).astype(jnp.bfloat16)
        solved = jnp.einsum("bck,bki->bci", right, near_inverse, preferred_element_type=jnp.float32)
        return solved.astype(jnp.bfloat16)

    past = gather_obs(history)

    def pick(block, index_part, slot):
        return past[index_part[1] // bd, slot, index_part[1] % bd]

    past = past.reshape(n_obs, slots, coefs, bd, width).transpose(0, 1, 3, 2, 4)
    first = settle(accumulate(lambda ip: pick(past, ip, ip[2])), incident[0])
    newest = gather_obs(first)

    def second_rows(ip):
        older = pick(past, ip, jnp.maximum(ip[2] - 1, 0))
        newer = newest[ip[1] // bd, ip[1] % bd]
        return jnp.where((ip[2] == 0)[:, None, None], newer, older)

    second = settle(accumulate(second_rows), incident[1])
    return jnp.stack([first, second])


def solution(mesh):
    n_src, n_obs = mesh.shape["src"], mesh.shape["obs"]
    vmem = pl.BlockSpec(memory_space=pltpu.VMEM)
    smem = pl.BlockSpec(memory_space=pltpu.SMEM)
    hbm = pl.BlockSpec(memory_space=pltpu.HBM)
    dma = pltpu.SemaphoreType.DMA
    f32, bf16, i32 = jnp.float32, jnp.bfloat16, jnp.int32

    def params(i):
        return pltpu.CompilerParams(collective_id=i, has_side_effects=True)

    def on_device(tiles, tile_index, tile_count, history, incident, near_inverse):
        n_tiles, width = tiles.shape[2], tiles.shape[4]
        bd = near_inverse.shape[0]
        slots, coefs = history.shape[:2]
        tile_rows = tiles.reshape(n_tiles, width, width)
        index_rows = tile_index.transpose(0, 2, 1, 3).reshape(3, 1, n_tiles)
        hist = history.reshape(slots, coefs, bd, width).transpose(0, 2, 1, 3).reshape(slots * bd, coefs, width)
        drive = incident.reshape(2, coefs, bd, width).transpose(0, 2, 1, 3)

        def rows(cap):
            return pltpu.VMEM((n_obs * cap, coefs, width), bf16)

        def sends(cap):
            return pltpu.VMEM((n_obs, cap, coefs, width), bf16)

        def parts(kind):
            return pltpu.VMEM((n_src * bd, coefs * width), kind)

        arrived = pltpu.VMEM((n_src, bd, coefs * width), bf16)

        both, crowded = pl.pallas_call(
            functools.partial(step_kernel, n_src, n_obs, bd),
            name="step",
            out_shape=(
                jax.ShapeDtypeStruct((2, bd, coefs, width), bf16),
                jax.ShapeDtypeStruct((1, 1), f32),
            ),
            in_specs=[vmem, vmem, hbm, hbm, hbm, hbm],
            out_specs=(vmem, smem),
            scratch_shapes=[
                pltpu.VMEM((n_obs, 1, 128), i32), pltpu.VMEM((n_obs, 1, 128), i32),
                pltpu.VMEM((8, n_tiles), i32), pltpu.VMEM((8, 128), i32),
                pltpu.SMEM((n_obs, 1, 128), i32), pltpu.SMEM((8, n_tiles), i32), pltpu.SMEM((8, 128), i32),
                pltpu.VMEM((n_src, 1, 128), f32),
                pltpu.VMEM((n_tiles, width, width), bf16),
                pltpu.VMEM(hist.shape, bf16),
                pltpu.VMEM(drive.shape, f32),
                pltpu.VMEM((bd, width, width), bf16),
                rows(CAP), rows(CAP), rows(CAP0), sends(CAP), sends(CAP), sends(CAP0),
                pltpu.VMEM((1, 128), f32),
                pltpu.VMEM((coefs * n_tiles, width), f32),
                pltpu.VMEM((n_tiles, coefs * width), bf16),
                pltpu.VMEM((coefs * CAPD, width), f32),
                pltpu.VMEM((n_src * bd, n_tiles), bf16),
                pltpu.VMEM((n_src * bd, n_tiles), bf16),
                pltpu.VMEM((n_src * bd, CAPD), bf16),
                parts(f32), parts(bf16), parts(bf16), arrived, arrived,
                pltpu.VMEM((bd, coefs * width), bf16), pltpu.VMEM((bd, coefs * width), bf16),
                pltpu.VMEM((coefs * bd, width), f32),
                dma, dma((6,)), dma((2,)), dma((2,)), dma((2,)), dma((2,)), dma((2,)), dma((3,)), dma((3,)), dma((2,)), dma((2,)),
            ],
            compiler_params=params(0),
        )(tile_count, index_rows, tile_rows, hist, drive, near_inverse)

        both = lax.cond(
            crowded[0, 0] > 0.0,
            lambda kept: dense_path(
                tile_rows, tile_index.reshape(3, n_tiles), tile_count.reshape(()), history, drive, near_inverse,
                n_src, n_obs,
            ),
            lambda kept: kept,
            both,
        )
        return both.transpose(0, 2, 1, 3).reshape(2, coefs, bd * width)

    in_specs = (
        P("src", "obs", None, None, None),
        P("src", "obs", None, None),
        P("src", "obs"),
        P(None, None, ("src", "obs")),
        P(None, None, ("src", "obs")),
        P(("src", "obs"), None, None),
    )
    out_specs = P(None, None, ("src", "obs"))
    return jax.shard_map(on_device, mesh=mesh, in_specs=in_specs, out_specs=out_specs, check_vma=False)
```

```python
import functools

import jax
import jax.numpy as jnp
from jax import lax
from jax.experimental import pallas as pl
from jax.experimental.pallas import tpu as pltpu
from jax.sharding import PartitionSpec as P

MESH = pl.DeviceIdType.MESH
CAP = 60
CAP0 = 12
CAPD = 64
FAR = -(1 << 20)
ORDER = (10, 11, 6, 14, 7, 15, 2, 3, 8, 9, 4, 12, 5, 13, 1)
STAGED = (False, False)
AT0 = 64


def greet(src_peers, obs_peers, n_src, n_obs):
    me_s, me_o = lax.axis_index("src"), lax.axis_index("obs")
    barrier = pltpu.get_barrier_semaphore()
    if src_peers:
        for k in range(1, n_src):
            pl.semaphore_signal(
                barrier, inc=1, device_id=(lax.rem(me_s + k, n_src), me_o), device_id_type=MESH
            )
    if obs_peers:
        for k in range(1, n_obs):
            pl.semaphore_signal(
                barrier, inc=1, device_id=(me_s, obs_peer(k, n_obs)), device_id_type=MESH
            )
    total = (n_src - 1) * src_peers + (n_obs - 1) * obs_peers
    return lambda: pl.semaphore_wait(barrier, total)


def obs_peer(k, n_obs):
    me = lax.axis_index("obs")
    x = lax.rem(me // 4 + k // 4, n_obs // 4)
    z = lax.rem(lax.rem(me // 2, 2) + lax.rem(k // 2, 2), 2)
    core = lax.rem(lax.rem(me, 2) + lax.rem(k, 2), 2)
    return x * 4 + z * 2 + core


def to_obs(k, n_obs, src_ref, dst_ref, send_sem, recv_sem):
    return pltpu.make_async_remote_copy(
        src_ref=src_ref, dst_ref=dst_ref, send_sem=send_sem, recv_sem=recv_sem,
        device_id=(lax.axis_index("src"), obs_peer(k, n_obs)), device_id_type=MESH,
    )


def to_src(peer, src_ref, dst_ref, send_sem, recv_sem):
    return pltpu.make_async_remote_copy(
        src_ref=src_ref, dst_ref=dst_ref, send_sem=send_sem, recv_sem=recv_sem,
        device_id=(peer, lax.axis_index("obs")), device_id_type=MESH,
    )


def take(ref, sem):
    pltpu.make_async_copy(ref, ref, sem).wait()


def each(count, body, start=0):
    lax.fori_loop(start, count, lambda i, carry: (body(i), carry)[1], 0)


def build_requests(n_src, n_obs, bd, rows, idx_ref, cnt_ref, send_ref, info_ref, list_ref):
    n_tiles = idx_ref.shape[2]
    shift = bd.bit_length() - 1
    lane = lax.broadcasted_iota(jnp.int32, (1, n_tiles), 1)
    live = lane < cnt_ref[...]
    obs_block, source, delay = idx_ref[0], idx_ref[1], idx_ref[2]
    owner = lax.shift_right_logical(source, shift)
    place = jnp.bitwise_and(source, bd - 1)
    owner_row = lax.broadcasted_iota(jnp.int32, (n_obs, n_tiles), 0)
    mine = jnp.where(jnp.logical_and(owner == owner_row, live), 1.0, 0.0)
    mine0 = jnp.where(delay == 0, mine, 0.0)
    before = jnp.where(
        lax.broadcasted_iota(jnp.int32, (n_tiles, n_tiles), 0)
        < lax.broadcasted_iota(jnp.int32, (n_tiles, n_tiles), 1),
        1.0, 0.0,
    ).astype(jnp.bfloat16)
    both = jnp.concatenate([mine, mine0], axis=0).astype(jnp.bfloat16)
    order = jnp.dot(both, before, preferred_element_type=jnp.float32)
    rank = jnp.sum(order[:n_obs] * mine, axis=0, keepdims=True)
    rank0 = jnp.sum(order[n_obs:] * mine0, axis=0, keepdims=True)
    rank_d = jnp.sum(order[n_obs:], axis=0, keepdims=True)
    newest = jnp.logical_and(live, delay == 0)
    over = jnp.where(live, jnp.where(rank >= CAP, 1.0, 0.0), 0.0) + jnp.where(
        newest, jnp.where(rank0 >= CAP0, 1.0, 0.0) + jnp.where(rank_d >= CAPD, 1.0, 0.0), 0.0
    )
    flag = jnp.where(jnp.max(over, axis=1, keepdims=True) > 0.0, 1.0, 0.0)
    rank = rank.astype(jnp.int32)
    rank0 = rank0.astype(jnp.int32)
    fits = jnp.logical_and(live, rank < CAP)
    fits0 = jnp.logical_and(newest, rank0 < CAP0)
    nowhere = n_src * bd
    info_ref[0:1, :] = jnp.clip(jnp.where(fits, owner * CAP + rank, 0), 0, n_obs * CAP - 1)
    info_ref[1:2, :] = jnp.where(live, obs_block, nowhere)
    info_ref[2:3, :] = jnp.where(jnp.logical_and(live, delay > 0), obs_block, nowhere)
    info_ref[3:8, :] = jnp.zeros((5, n_tiles), jnp.int32)
    row = lax.broadcasted_iota(jnp.int32, (128, n_tiles), 0)
    ones = lambda hit: jnp.where(hit, 1.0, 0.0).astype(jnp.bfloat16)
    key = jnp.where(fits, rank, FAR)
    key0 = jnp.where(fits0, rank0 + AT0, FAR)
    coded = jnp.concatenate([mine * place.astype(jnp.float32), mine * delay.astype(jnp.float32)], axis=0)

    def find(codes, hit):
        return lax.dot_general(
            codes.astype(jnp.bfloat16), ones(hit), (((1,), (1,)), ((), ())), preferred_element_type=jnp.float32
        )

    found = find(coded, jnp.logical_or(key == row, key0 == row))
    code = found[:n_obs] + found[n_obs:] * bd
    out_lane = lax.broadcasted_iota(jnp.int32, (n_obs, 128), 1)
    code = jnp.clip(jnp.where(out_lane == 127, flag, code).astype(jnp.int32), 0, rows - 1)
    for o in range(n_obs):
        send_ref[o] = code[o : o + 1]

    def build_list():
        key_d = jnp.where(newest, rank_d.astype(jnp.int32), FAR)
        code_row = lax.broadcasted_iota(jnp.int32, (16, n_tiles), 0)
        codes = jnp.zeros((16, n_tiles), jnp.int32)
        slot0 = jnp.where(fits0, owner * CAP0 + rank0, 0)
        parts = (
            jnp.bitwise_and(lane, 127), lax.shift_right_logical(lane, 7), slot0,
            jnp.bitwise_and(obs_block, 127), lax.shift_right_logical(obs_block, 7), jnp.ones_like(lane),
        )
        for i, part in enumerate(parts):
            codes = jnp.where(code_row == i, part, codes)
        found = find(codes.astype(jnp.float32), key_d == row)
        list_ref[0:1, :] = jnp.clip((found[0:1, :] + found[1:2, :] * 128.0).astype(jnp.int32), 0, n_tiles - 1)
        list_ref[1:2, :] = jnp.clip(found[2:3, :].astype(jnp.int32), 0, n_obs * CAP0 - 1)
        block = jnp.where(found[5:6, :] > 0.5, found[3:4, :] + found[4:5, :] * 128.0, 1.0 * nowhere)
        list_ref[2:3, :] = block.astype(jnp.int32)
        list_ref[3:8, :] = jnp.zeros((5, 128), jnp.int32)

    return build_list


def step_kernel(
    n_src, n_obs, bd, cnt_ref, idx_ref, tiles_ref, hist_ref, inc_ref, near_ref,
    out_ref, crowded_ref,
    ask, asked, info_v, list_v, req, info, lst, flags,
    tile, hist, inc, near, rows1, rows2, rows0, send1, send2, send0, mark,
    y_one, y_all, y_new, pick1, pick2, pick0, part_old, part1, part2, recv1, recv2, far_out, far_in, drive,
    tile_sem, load_sem, ask_sem, flag_sem, sem1, sem2, sem0, part_sem1, part_sem2, far_sem1, far_sem2,
):
    me_s, me_o = lax.axis_index("src"), lax.axis_index("obs")
    order = ORDER if n_obs == len(ORDER) + 1 else range(1, n_obs)
    entered = greet(1, 1, n_src, n_obs)
    n_tiles = tiles_ref.shape[0]
    chunk = min(64, n_tiles)
    chunks = n_tiles // chunk
    width = tiles_ref.shape[2]
    coefs = hist_ref.shape[1]
    load_hist = pltpu.make_async_copy(hist_ref, hist, load_sem.at[0])
    load_near = pltpu.make_async_copy(near_ref, near, load_sem.at[1])
    load_inc = pltpu.make_async_copy(inc_ref, inc, load_sem.at[2])

    def load_tiles(c):
        at = pl.ds(c * chunk, chunk)
        return pltpu.make_async_copy(tiles_ref.at[at], tile.at[at], tile_sem)

    load_hist.start()
    build_list = build_requests(n_src, n_obs, bd, hist_ref.shape[0], idx_ref, cnt_ref, ask, info_v, list_v)
    asked[me_o] = ask[me_o]

    def send_ask(k):
        return to_obs(k, n_obs, ask.at[obs_peer(k, n_obs)], asked.at[me_o], ask_sem.at[0], ask_sem.at[1])

    entered()
    each(n_obs, lambda k: send_ask(k).start(), 1)
    build_list()
    info_down = pltpu.make_async_copy(info_v, info, load_sem.at[3])
    list_down = pltpu.make_async_copy(list_v, lst, load_sem.at[4])
    info_down.start()
    list_down.start()
    ones = lambda hit: jnp.where(hit, 1.0, 0.0).astype(jnp.bfloat16)
    row = lax.broadcasted_iota(jnp.int32, (bd, n_tiles), 0)
    row0 = lax.broadcasted_iota(jnp.int32, (bd, CAPD), 0)

    n_y = n_src // 2
    me_z, me_y = me_s // n_y, lax.rem(me_s, n_y)

    def place_of(k):
        return lax.rem(me_z + 1 - k // n_y, 2) * n_y + lax.rem(me_y + 1 + lax.rem(k, n_y), n_y)

    def one_pick(k):
        first = place_of(k) * bd
        at = pl.ds(pl.multiple_of(k * bd, bd), bd)
        pick1[at, :] = ones(info_v[1:2, :] - first == row)
        pick2[at, :] = ones(info_v[2:3, :] - first == row)
        pick0[at, :] = ones(list_v[2:3, 0:CAPD] - first == row0)

    each(n_src, one_pick)
    others = pl.ds(0, n_obs - 1)
    take(asked.at[others], ask_sem.at[1])
    take(ask.at[others], ask_sem.at[0])
    req_down = pltpu.make_async_copy(asked, req, load_sem.at[5])
    req_down.start()
    worst = jnp.max(asked[...].astype(jnp.float32), axis=0)
    worst = jnp.where(lax.broadcasted_iota(jnp.int32, worst.shape, 1) == 127, worst, 0.0)
    mark[...] = jnp.broadcast_to(jnp.max(worst, axis=1, keepdims=True), mark.shape)
    flags[me_s] = mark[...]

    def gather(table, out, o, slots, first, code_to_row):
        def twelve(turn):
            for i in range(12):
                r = turn * 12 + i
                out[r] = table[code_to_row(req[o, 0, first + r])]

        each(slots // 12, twelve)

    def send_flag(k):
        return to_src(lax.rem(me_s + k, n_src), mark, flags.at[me_s], flag_sem.at[0], flag_sem.at[1])

    def send_rows(k, send, rows, cap, sem):
        return to_obs(k, n_obs, send.at[k], rows.at[pl.ds(me_o * cap, cap)], sem.at[0], sem.at[1])

    def take_rows(send, rows, cap, sem):
        take(rows.at[pl.ds(0, (n_obs - 1) * cap)], sem.at[1])
        take(send.at[pl.ds(1, n_obs - 1)], sem.at[0])

    def one_dest(k):
        gather(hist, send1.at[k], obs_peer(k, n_obs), CAP, 0, lambda c: c)

    def send_one(k):
        return send_rows(k, send1, rows1, CAP, sem1)

    load_hist.wait()
    req_down.wait()

    def gather_send(k):
        one_dest(k)
        send_one(k).start()

    for k in order:
        gather_send(k)
    each(chunks, lambda c: load_tiles(c).start())
    load_inc.start()
    load_near.start()
    each(n_src, lambda k: send_flag(k).start(), 1)
    gather(hist, rows1.at[pl.ds(me_o * CAP, CAP)], me_o, CAP, 0, lambda c: c)

    older = lambda c: jnp.maximum(c - bd, 0)
    def gather_send_two(k):
        gather(hist, send2.at[k], obs_peer(k, n_obs), CAP, 0, older)
        send_rows(k, send2, rows2, CAP, sem2).start()

    for k in order:
        gather_send_two(k)
    gather(hist, rows2.at[pl.ds(me_o * CAP, CAP)], me_o, CAP, 0, older)

    def two_products(x0, x1, t0, t1, y, count, at):
        x = jnp.concatenate([x0.astype(jnp.float32), x1.astype(jnp.float32)], axis=0).astype(jnp.bfloat16)
        both = jnp.dot(x, jnp.concatenate([t0, t1], axis=1), preferred_element_type=jnp.float32)
        y[pl.ds(at, coefs, stride=count), :] = both[:coefs, :width]
        y[pl.ds(at + 1, coefs, stride=count), :] = both[coefs:, width:]

    def products(rows):
        def one_chunk(c):
            for i in range(0, chunk, 2):
                t = c * chunk + i
                two_products(rows[info[0, t]], rows[info[0, t + 1]], tile[t], tile[t + 1], y_one, n_tiles, t)

        return one_chunk

    def pack():
        for c in range(coefs):
            lanes = slice(c * width, (c + 1) * width)

            def some(i):
                at = pl.multiple_of(i * 64, 64)
                y_all[pl.ds(at, 64), lanes] = y_one[pl.ds(c * n_tiles + at, 64), :].astype(jnp.bfloat16)

            each(n_tiles // 64, some)

    def start_half(g, staged, part, recv, sem):
        for i in range(n_y - staged if g == 0 else n_y - 1):
            k = g * n_y + i
            peer = me_z * n_y + lax.rem(me_y + 1 + i, n_y) if staged else place_of(k)
            to_src(peer, part.at[pl.ds(k * bd, bd)], recv.at[k], sem.at[0], sem.at[1 + g]).start()

    def finish(staged, part, recv, sem, far_sem):
        def half_sum(g, count):
            if count:
                take(recv.at[pl.ds(g * n_y, count)], sem.at[1 + g])
            total = part[(g * n_y + n_y - 1) * bd : (g + 1) * n_y * bd, :].astype(jnp.float32)
            for i in range(n_y - 1):
                total = total + recv[g * n_y + i].astype(jnp.float32)
            return total

        sent = n_src - 2 if staged else n_src - 1
        if staged:
            far_out[...] = half_sum(0, n_y - 1).astype(jnp.bfloat16)
            peer = lax.rem(me_z + 1, 2) * n_y + me_y
            far = to_src(peer, far_out, far_in, far_sem.at[0], far_sem.at[1])
            far.start()
            total = half_sum(1, n_y - 1)
            far.wait()
            total = total + far_in[...].astype(jnp.float32)
        else:
            take(recv.at[pl.ds(0, n_y)], sem.at[1])
            total = half_sum(1, n_y - 1)
            for k in range(n_y):
                total = total + recv[k].astype(jnp.float32)
        if sent:
            take(recv.at[pl.ds(0, sent)], sem.at[0])
        return total

    group = n_src // 2
    half = lambda g: slice(g * group * bd, (g + 1) * group * bd)

    def solve(which, total):
        for c in range(coefs):
            drive[pl.ds(c * bd, bd), :] = total[:, c * width : (c + 1) * width]

        some = min(32, bd)

        def pairs(turn):
            for i in range(some // 2):
                b = turn * some + 2 * i
                x0 = inc[which, b] - drive[pl.ds(b, coefs, stride=bd), :]
                x1 = inc[which, b + 1] - drive[pl.ds(b + 1, coefs, stride=bd), :]
                x = jnp.concatenate([x0, x1], axis=0).astype(jnp.bfloat16)
                both = jnp.dot(
                    x, jnp.concatenate([near[b], near[b + 1]], axis=1), preferred_element_type=jnp.float32
                )
                out_ref[which, b] = both[:coefs, :width].astype(jnp.bfloat16)
                out_ref[which, b + 1] = both[coefs:, width:].astype(jnp.bfloat16)

        each(bd // some, pairs)

    take(tile, tile_sem)
    info_down.wait()
    take_rows(send1, rows1, CAP, sem1)
    each(chunks, products(rows1))
    pack()
    for g in range(2):
        part1[half(g), :] = jnp.dot(
            pick1[half(g), :], y_all[...], preferred_element_type=jnp.float32
        ).astype(jnp.bfloat16)
        start_half(g, STAGED[0], part1, recv1, part_sem1)
    load_inc.wait()
    load_near.wait()
    for side in range(2):
        take(flags.at[pl.ds(0, n_src - 1)], flag_sem.at[side])
    solve(0, finish(STAGED[0], part1, recv1, part_sem1, far_sem1))

    newest = out_ref.at[0]
    placed = lambda c: jnp.bitwise_and(c, bd - 1)
    send_new = lambda k: send_rows(k, send0, rows0, CAP0, sem0)

    def gather_send_new(k):
        gather(newest, send0.at[k], obs_peer(k, n_obs), CAP0, AT0, placed)
        send_new(k).start()

    for k in order:
        gather_send_new(k)
    gather(newest, rows0.at[pl.ds(me_o * CAP0, CAP0)], me_o, CAP0, AT0, placed)
    take_rows(send2, rows2, CAP, sem2)
    each(chunks, products(rows2))
    pack()
    for g in range(2):
        part_old[half(g), :] = jnp.dot(pick2[half(g), :], y_all[...], preferred_element_type=jnp.float32)
    list_down.wait()
    take_rows(send0, rows0, CAP0, sem0)

    def new_products(turn):
        for i in range(0, 32, 2):
            r = turn * 32 + i
            two_products(
                rows0[lst[1, r]], rows0[lst[1, r + 1]], tile[lst[0, r]], tile[lst[0, r + 1]], y_new, CAPD, r
            )

    each(CAPD // 32, new_products)
    value = jnp.concatenate([y_new[c * CAPD : (c + 1) * CAPD, :] for c in range(coefs)], axis=1)
    value = value.astype(jnp.bfloat16)
    for g in range(2):
        added = jnp.dot(pick0[half(g), :], value, preferred_element_type=jnp.float32)
        part2[half(g), :] = (part_old[half(g), :] + added).astype(jnp.bfloat16)
        start_half(g, STAGED[1], part2, recv2, part_sem2)
    solve(1, finish(STAGED[1], part2, recv2, part_sem2, far_sem2))
    crowded_ref[0, 0] = jnp.max(flags[...])


def dense_path(tile_rows, index_rows, live_count, history, incident, near_inverse, n_src, n_obs):
    bd, width = near_inverse.shape[:2]
    slots, coefs = history.shape[:2]
    n_tiles = tile_rows.shape[0]
    group = min(64, n_tiles)

    def gather_obs(block):
        ring = [(i, (i + 1) % n_obs) for i in range(n_obs)]
        me = lax.axis_index("obs")
        whole = jnp.zeros((n_obs,) + block.shape, block.dtype)
        whole = lax.dynamic_update_index_in_dim(whole, block, me, 0)

        def hop(k, carry):
            whole, moving = carry
            whole = lax.dynamic_update_index_in_dim(whole, moving, lax.rem(me - k + n_obs, n_obs), 0)
            return whole, lax.ppermute(moving, "obs", ring)

        return lax.fori_loop(1, n_obs, hop, (whole, lax.ppermute(block, "obs", ring)))[0]

    def sum_src(value):
        ring = [(i, (i + 1) % n_src) for i in range(n_src)]

        def hop(k, carry):
            total, moving = carry
            moving = lax.ppermute(moving, "src", ring)
            return total + moving, moving

        return lax.fori_loop(0, n_src - 1, hop, (value, value))[0]

    def accumulate(chooser):
        def one_group(turn, partial):
            start = turn * group
            tile_part = lax.dynamic_slice_in_dim(tile_rows, start, group, 0)
            index_part = lax.dynamic_slice_in_dim(index_rows, start, group, 1)
            products = jnp.einsum(
                "gck,gki->gci", chooser(index_part), tile_part, preferred_element_type=jnp.float32
            )
            alive = start + jnp.arange(group, dtype=jnp.int32) < live_count
            products = jnp.where(alive[:, None, None], products, 0.0)
            return partial.at[index_part[0]].add(products)

        initial = jnp.zeros((bd * n_src, coefs, width), jnp.float32)
        return lax.fori_loop(0, n_tiles // group, one_group, initial)

    def settle(partial, drive):
        own = lax.dynamic_slice_in_dim(sum_src(partial), lax.axis_index("src") * bd, bd, 0)
        right = (drive - own).astype(jnp.bfloat16)
        solved = jnp.einsum("bck,bki->bci", right, near_inverse, preferred_element_type=jnp.float32)
        return solved.astype(jnp.bfloat16)

    past = gather_obs(history)

    def pick(block, index_part, slot):
        return past[index_part[1] // bd, slot, index_part[1] % bd]

    past = past.reshape(n_obs, slots, coefs, bd, width).transpose(0, 1, 3, 2, 4)
    first = settle(accumulate(lambda ip: pick(past, ip, ip[2])), incident[0])
    newest = gather_obs(first)

    def second_rows(ip):
        older = pick(past, ip, jnp.maximum(ip[2] - 1, 0))
        newer = newest[ip[1] // bd, ip[1] % bd]
        return jnp.where((ip[2] == 0)[:, None, None], newer, older)

    second = settle(accumulate(second_rows), incident[1])
    return jnp.stack([first, second])


def solution(mesh):
    n_src, n_obs = mesh.shape["src"], mesh.shape["obs"]
    vmem = pl.BlockSpec(memory_space=pltpu.VMEM)
    smem = pl.BlockSpec(memory_space=pltpu.SMEM)
    hbm = pl.BlockSpec(memory_space=pltpu.HBM)
    dma = pltpu.SemaphoreType.DMA
    f32, bf16, i32 = jnp.float32, jnp.bfloat16, jnp.int32

    def params(i):
        return pltpu.CompilerParams(collective_id=i, has_side_effects=True)

    def on_device(tiles, tile_index, tile_count, history, incident, near_inverse):
        n_tiles, width = tiles.shape[2], tiles.shape[4]
        bd = near_inverse.shape[0]
        slots, coefs = history.shape[:2]
        tile_rows = tiles.reshape(n_tiles, width, width)
        index_rows = tile_index.transpose(0, 2, 1, 3).reshape(3, 1, n_tiles)
        hist = history.reshape(slots, coefs, bd, width).transpose(0, 2, 1, 3).reshape(slots * bd, coefs, width)
        drive = incident.reshape(2, coefs, bd, width).transpose(0, 2, 1, 3)

        def rows(cap):
            return pltpu.VMEM((n_obs * cap, coefs, width), bf16)

        def sends(cap):
            return pltpu.VMEM((n_obs, cap, coefs, width), bf16)

        def parts(kind):
            return pltpu.VMEM((n_src * bd, coefs * width), kind)

        arrived = pltpu.VMEM((n_src, bd, coefs * width), bf16)

        both, crowded = pl.pallas_call(
            functools.partial(step_kernel, n_src, n_obs, bd),
            name="step",
            out_shape=(
                jax.ShapeDtypeStruct((2, bd, coefs, width), bf16),
                jax.ShapeDtypeStruct((1, 1), f32),
            ),
            in_specs=[vmem, vmem, hbm, hbm, hbm, hbm],
            out_specs=(vmem, smem),
            scratch_shapes=[
                pltpu.VMEM((n_obs, 1, 128), i32), pltpu.VMEM((n_obs, 1, 128), i32),
                pltpu.VMEM((8, n_tiles), i32), pltpu.VMEM((8, 128), i32),
                pltpu.SMEM((n_obs, 1, 128), i32), pltpu.SMEM((8, n_tiles), i32), pltpu.SMEM((8, 128), i32),
                pltpu.VMEM((n_src, 1, 128), f32),
                pltpu.VMEM((n_tiles, width, width), bf16),
                pltpu.VMEM(hist.shape, bf16),
                pltpu.VMEM(drive.shape, f32),
                pltpu.VMEM((bd, width, width), bf16),
                rows(CAP), rows(CAP), rows(CAP0), sends(CAP), sends(CAP), sends(CAP0),
                pltpu.VMEM((1, 128), f32),
                pltpu.VMEM((coefs * n_tiles, width), f32),
                pltpu.VMEM((n_tiles, coefs * width), bf16),
                pltpu.VMEM((coefs * CAPD, width), f32),
                pltpu.VMEM((n_src * bd, n_tiles), bf16),
                pltpu.VMEM((n_src * bd, n_tiles), bf16),
                pltpu.VMEM((n_src * bd, CAPD), bf16),
                parts(f32), parts(bf16), parts(bf16), arrived, arrived,
                pltpu.VMEM((bd, coefs * width), bf16), pltpu.VMEM((bd, coefs * width), bf16),
                pltpu.VMEM((coefs * bd, width), f32),
                dma, dma((6,)), dma((2,)), dma((2,)), dma((2,)), dma((2,)), dma((2,)), dma((3,)), dma((3,)), dma((2,)), dma((2,)),
            ],
            compiler_params=params(0),
        )(tile_count, index_rows, tile_rows, hist, drive, near_inverse)

        both = lax.cond(
            crowded[0, 0] > 0.0,
            lambda kept: dense_path(
                tile_rows, tile_index.reshape(3, n_tiles), tile_count.reshape(()), history, drive, near_inverse,
                n_src, n_obs,
            ),
            lambda kept: kept,
            both,
        )
        return both.transpose(0, 2, 1, 3).reshape(2, coefs, bd * width)

    in_specs = (
        P("src", "obs", None, None, None),
        P("src", "obs", None, None),
        P("src", "obs"),
        P(None, None, ("src", "obs")),
        P(None, None, ("src", "obs")),
        P(("src", "obs"), None, None),
    )
    out_specs = P(None, None, ("src", "obs"))
    return jax.shard_map(on_device, mesh=mesh, in_specs=in_specs, out_specs=out_specs, check_vma=False)
```

```python
import functools

import jax
import jax.numpy as jnp
from jax import lax
from jax.experimental import pallas as pl
from jax.experimental.pallas import tpu as pltpu
from jax.sharding import PartitionSpec as P

MESH = pl.DeviceIdType.MESH
CAP = 60
CAP0 = 12
CAPD = 64
FAR = -(1 << 20)
ORDER = (6, 14, 7, 15, 10, 11, 2, 3, 8, 9, 4, 12, 5, 13, 1)
STAGED = (True, False)
AT0 = 64


def greet(src_peers, obs_peers, n_src, n_obs):
    me_s, me_o = lax.axis_index("src"), lax.axis_index("obs")
    barrier = pltpu.get_barrier_semaphore()
    if src_peers:
        for k in range(1, n_src):
            pl.semaphore_signal(
                barrier, inc=1, device_id=(lax.rem(me_s + k, n_src), me_o), device_id_type=MESH
            )
    if obs_peers:
        for k in range(1, n_obs):
            pl.semaphore_signal(
                barrier, inc=1, device_id=(me_s, obs_peer(k, n_obs)), device_id_type=MESH
            )
    total = (n_src - 1) * src_peers + (n_obs - 1) * obs_peers
    return lambda: pl.semaphore_wait(barrier, total)


def obs_peer(k, n_obs):
    me = lax.axis_index("obs")
    x = lax.rem(me // 4 + k // 4, n_obs // 4)
    z = lax.rem(lax.rem(me // 2, 2) + lax.rem(k // 2, 2), 2)
    core = lax.rem(lax.rem(me, 2) + lax.rem(k, 2), 2)
    return x * 4 + z * 2 + core


def to_obs(k, n_obs, src_ref, dst_ref, send_sem, recv_sem):
    return pltpu.make_async_remote_copy(
        src_ref=src_ref, dst_ref=dst_ref, send_sem=send_sem, recv_sem=recv_sem,
        device_id=(lax.axis_index("src"), obs_peer(k, n_obs)), device_id_type=MESH,
    )


def to_src(peer, src_ref, dst_ref, send_sem, recv_sem):
    return pltpu.make_async_remote_copy(
        src_ref=src_ref, dst_ref=dst_ref, send_sem=send_sem, recv_sem=recv_sem,
        device_id=(peer, lax.axis_index("obs")), device_id_type=MESH,
    )


def take(ref, sem):
    pltpu.make_async_copy(ref, ref, sem).wait()


def each(count, body, start=0):
    lax.fori_loop(start, count, lambda i, carry: (body(i), carry)[1], 0)


def build_requests(n_src, n_obs, bd, rows, idx_ref, cnt_ref, send_ref, info_ref, list_ref):
    n_tiles = idx_ref.shape[2]
    shift = bd.bit_length() - 1
    lane = lax.broadcasted_iota(jnp.int32, (1, n_tiles), 1)
    live = lane < cnt_ref[...]
    obs_block, source, delay = idx_ref[0], idx_ref[1], idx_ref[2]
    owner = lax.shift_right_logical(source, shift)
    place = jnp.bitwise_and(source, bd - 1)
    owner_row = lax.broadcasted_iota(jnp.int32, (n_obs, n_tiles), 0)
    mine = jnp.where(jnp.logical_and(owner == owner_row, live), 1.0, 0.0)
    mine0 = jnp.where(delay == 0, mine, 0.0)
    before = jnp.where(
        lax.broadcasted_iota(jnp.int32, (n_tiles, n_tiles), 0)
        < lax.broadcasted_iota(jnp.int32, (n_tiles, n_tiles), 1),
        1.0, 0.0,
    ).astype(jnp.bfloat16)
    both = jnp.concatenate([mine, mine0], axis=0).astype(jnp.bfloat16)
    order = jnp.dot(both, before, preferred_element_type=jnp.float32)
    rank = jnp.sum(order[:n_obs] * mine, axis=0, keepdims=True)
    rank0 = jnp.sum(order[n_obs:] * mine0, axis=0, keepdims=True)
    rank_d = jnp.sum(order[n_obs:], axis=0, keepdims=True)
    newest = jnp.logical_and(live, delay == 0)
    over = jnp.where(live, jnp.where(rank >= CAP, 1.0, 0.0), 0.0) + jnp.where(
        newest, jnp.where(rank0 >= CAP0, 1.0, 0.0) + jnp.where(rank_d >= CAPD, 1.0, 0.0), 0.0
    )
    flag = jnp.where(jnp.max(over, axis=1, keepdims=True) > 0.0, 1.0, 0.0)
    rank = rank.astype(jnp.int32)
    rank0 = rank0.astype(jnp.int32)
    fits = jnp.logical_and(live, rank < CAP)
    fits0 = jnp.logical_and(newest, rank0 < CAP0)
    nowhere = n_src * bd
    info_ref[0:1, :] = jnp.clip(jnp.where(fits, owner * CAP + rank, 0), 0, n_obs * CAP - 1)
    info_ref[1:2, :] = jnp.where(live, obs_block, nowhere)
    info_ref[2:3, :] = jnp.where(jnp.logical_and(live, delay > 0), obs_block, nowhere)
    info_ref[3:8, :] = jnp.zeros((5, n_tiles), jnp.int32)
    row = lax.broadcasted_iota(jnp.int32, (128, n_tiles), 0)
    ones = lambda hit: jnp.where(hit, 1.0, 0.0).astype(jnp.bfloat16)
    key = jnp.where(fits, rank, FAR)
    key0 = jnp.where(fits0, rank0 + AT0, FAR)
    coded = jnp.concatenate([mine * place.astype(jnp.float32), mine * delay.astype(jnp.float32)], axis=0)

    def find(codes, hit):
        return lax.dot_general(
            codes.astype(jnp.bfloat16), ones(hit), (((1,), (1,)), ((), ())), preferred_element_type=jnp.float32
        )

    found = find(coded, jnp.logical_or(key == row, key0 == row))
    code = found[:n_obs] + found[n_obs:] * bd
    out_lane = lax.broadcasted_iota(jnp.int32, (n_obs, 128), 1)
    code = jnp.clip(jnp.where(out_lane == 127, flag, code).astype(jnp.int32), 0, rows - 1)
    for o in range(n_obs):
        send_ref[o] = code[o : o + 1]

    def build_list():
        key_d = jnp.where(newest, rank_d.astype(jnp.int32), FAR)
        code_row = lax.broadcasted_iota(jnp.int32, (16, n_tiles), 0)
        codes = jnp.zeros((16, n_tiles), jnp.int32)
        slot0 = jnp.where(fits0, owner * CAP0 + rank0, 0)
        parts = (
            jnp.bitwise_and(lane, 127), lax.shift_right_logical(lane, 7), slot0,
            jnp.bitwise_and(obs_block, 127), lax.shift_right_logical(obs_block, 7), jnp.ones_like(lane),
        )
        for i, part in enumerate(parts):
            codes = jnp.where(code_row == i, part, codes)
        found = find(codes.astype(jnp.float32), key_d == row)
        list_ref[0:1, :] = jnp.clip((found[0:1, :] + found[1:2, :] * 128.0).astype(jnp.int32), 0, n_tiles - 1)
        list_ref[1:2, :] = jnp.clip(found[2:3, :].astype(jnp.int32), 0, n_obs * CAP0 - 1)
        block = jnp.where(found[5:6, :] > 0.5, found[3:4, :] + found[4:5, :] * 128.0, 1.0 * nowhere)
        list_ref[2:3, :] = block.astype(jnp.int32)
        list_ref[3:8, :] = jnp.zeros((5, 128), jnp.int32)

    return build_list


def step_kernel(
    n_src, n_obs, bd, cnt_ref, idx_ref, tiles_ref, hist_ref, inc_ref, near_ref,
    out_ref, crowded_ref,
    ask, asked, info_v, list_v, req, info, lst, flags,
    tile, hist, inc, near, rows1, rows2, rows0, send1, send2, send0, mark,
    y_one, y_all, y_new, pick1, pick2, pick0, part_old, part1, part2, recv1, recv2, far_out, far_in, drive,
    tile_sem, load_sem, ask_sem, flag_sem, sem1, sem2, sem0, part_sem1, part_sem2, far_sem1, far_sem2,
):
    me_s, me_o = lax.axis_index("src"), lax.axis_index("obs")
    order = ORDER if n_obs == len(ORDER) + 1 else range(1, n_obs)
    entered = greet(1, 1, n_src, n_obs)
    n_tiles = tiles_ref.shape[0]
    chunk = min(64, n_tiles)
    chunks = n_tiles // chunk
    width = tiles_ref.shape[2]
    coefs = hist_ref.shape[1]
    load_hist = pltpu.make_async_copy(hist_ref, hist, load_sem.at[0])
    load_near = pltpu.make_async_copy(near_ref, near, load_sem.at[1])
    load_inc = pltpu.make_async_copy(inc_ref, inc, load_sem.at[2])

    def load_tiles(c):
        at = pl.ds(c * chunk, chunk)
        return pltpu.make_async_copy(tiles_ref.at[at], tile.at[at], tile_sem)

    load_hist.start()
    build_list = build_requests(n_src, n_obs, bd, hist_ref.shape[0], idx_ref, cnt_ref, ask, info_v, list_v)
    asked[me_o] = ask[me_o]

    def send_ask(k):
        return to_obs(k, n_obs, ask.at[obs_peer(k, n_obs)], asked.at[me_o], ask_sem.at[0], ask_sem.at[1])

    entered()
    for k in order:
        send_ask(k).start()
    build_list()
    info_down = pltpu.make_async_copy(info_v, info, load_sem.at[3])
    list_down = pltpu.make_async_copy(list_v, lst, load_sem.at[4])
    info_down.start()
    list_down.start()
    ones = lambda hit: jnp.where(hit, 1.0, 0.0).astype(jnp.bfloat16)
    row = lax.broadcasted_iota(jnp.int32, (bd, n_tiles), 0)
    row0 = lax.broadcasted_iota(jnp.int32, (bd, CAPD), 0)

    n_y = n_src // 2
    me_z, me_y = me_s // n_y, lax.rem(me_s, n_y)

    def place_of(k):
        return lax.rem(me_z + 1 - k // n_y, 2) * n_y + lax.rem(me_y + 1 + lax.rem(k, n_y), n_y)

    def one_pick(k):
        first = place_of(k) * bd
        at = pl.ds(pl.multiple_of(k * bd, bd), bd)
        pick1[at, :] = ones(info_v[1:2, :] - first == row)
        pick2[at, :] = ones(info_v[2:3, :] - first == row)
        pick0[at, :] = ones(list_v[2:3, 0:CAPD] - first == row0)

    each(n_src, one_pick)
    others = pl.ds(0, n_obs - 1)
    take(asked.at[others], ask_sem.at[1])
    take(ask.at[others], ask_sem.at[0])
    req_down = pltpu.make_async_copy(asked, req, load_sem.at[5])
    req_down.start()
    worst = jnp.max(asked[...].astype(jnp.float32), axis=0)
    worst = jnp.where(lax.broadcasted_iota(jnp.int32, worst.shape, 1) == 127, worst, 0.0)
    mark[...] = jnp.broadcast_to(jnp.max(worst, axis=1, keepdims=True), mark.shape)
    flags[me_s] = mark[...]

    def gather(table, out, o, slots, first, code_to_row):
        def twelve(turn):
            for i in range(12):
                r = turn * 12 + i
                out[r] = table[code_to_row(req[o, 0, first + r])]

        each(slots // 12, twelve)

    def send_flag(k):
        return to_src(lax.rem(me_s + k, n_src), mark, flags.at[me_s], flag_sem.at[0], flag_sem.at[1])

    def send_rows(k, send, rows, cap, sem):
        return to_obs(k, n_obs, send.at[k], rows.at[pl.ds(me_o * cap, cap)], sem.at[0], sem.at[1])

    def take_rows(send, rows, cap, sem):
        take(rows.at[pl.ds(0, (n_obs - 1) * cap)], sem.at[1])
        take(send.at[pl.ds(1, n_obs - 1)], sem.at[0])

    def one_dest(k):
        gather(hist, send1.at[k], obs_peer(k, n_obs), CAP, 0, lambda c: c)

    def send_one(k):
        return send_rows(k, send1, rows1, CAP, sem1)

    load_hist.wait()
    req_down.wait()

    def gather_send(k):
        one_dest(k)
        send_one(k).start()

    for k in order:
        gather_send(k)
    each(chunks, lambda c: load_tiles(c).start())
    load_inc.start()
    load_near.start()
    each(n_src, lambda k: send_flag(k).start(), 1)
    gather(hist, rows1.at[pl.ds(me_o * CAP, CAP)], me_o, CAP, 0, lambda c: c)

    older = lambda c: jnp.maximum(c - bd, 0)
    def gather_send_two(k):
        gather(hist, send2.at[k], obs_peer(k, n_obs), CAP, 0, older)
        send_rows(k, send2, rows2, CAP, sem2).start()

    for k in order:
        gather_send_two(k)
    gather(hist, rows2.at[pl.ds(me_o * CAP, CAP)], me_o, CAP, 0, older)

    def two_products(x0, x1, t0, t1, y, count, at):
        x = jnp.concatenate([x0.astype(jnp.float32), x1.astype(jnp.float32)], axis=0).astype(jnp.bfloat16)
        both = jnp.dot(x, jnp.concatenate([t0, t1], axis=1), preferred_element_type=jnp.float32)
        y[pl.ds(at, coefs, stride=count), :] = both[:coefs, :width]
        y[pl.ds(at + 1, coefs, stride=count), :] = both[coefs:, width:]

    def products(rows):
        def one_chunk(c):
            for i in range(0, chunk, 2):
                t = c * chunk + i
                two_products(rows[info[0, t]], rows[info[0, t + 1]], tile[t], tile[t + 1], y_one, n_tiles, t)

        return one_chunk

    def pack():
        for c in range(coefs):
            lanes = slice(c * width, (c + 1) * width)

            def some(i):
                at = pl.multiple_of(i * 64, 64)
                y_all[pl.ds(at, 64), lanes] = y_one[pl.ds(c * n_tiles + at, 64), :].astype(jnp.bfloat16)

            each(n_tiles // 64, some)

    def start_half(g, staged, part, recv, sem):
        for i in range(n_y - staged if g == 0 else n_y - 1):
            k = g * n_y + i
            peer = me_z * n_y + lax.rem(me_y + 1 + i, n_y) if staged else place_of(k)
            to_src(peer, part.at[pl.ds(k * bd, bd)], recv.at[k], sem.at[0], sem.at[1 + g]).start()

    def finish(staged, part, recv, sem, far_sem):
        def half_sum(g, count):
            if count:
                take(recv.at[pl.ds(g * n_y, count)], sem.at[1 + g])
            total = part[(g * n_y + n_y - 1) * bd : (g + 1) * n_y * bd, :].astype(jnp.float32)
            for i in range(n_y - 1):
                total = total + recv[g * n_y + i].astype(jnp.float32)
            return total

        sent = n_src - 2 if staged else n_src - 1
        if staged:
            far_out[...] = half_sum(0, n_y - 1).astype(jnp.bfloat16)
            peer = lax.rem(me_z + 1, 2) * n_y + me_y
            far = to_src(peer, far_out, far_in, far_sem.at[0], far_sem.at[1])
            far.start()
            total = half_sum(1, n_y - 1)
            far.wait()
            total = total + far_in[...].astype(jnp.float32)
        else:
            take(recv.at[pl.ds(0, n_y)], sem.at[1])
            total = half_sum(1, n_y - 1)
            for k in range(n_y):
                total = total + recv[k].astype(jnp.float32)
        if sent:
            take(recv.at[pl.ds(0, sent)], sem.at[0])
        return total

    group = n_src // 2
    half = lambda g: slice(g * group * bd, (g + 1) * group * bd)

    def solve(which, total):
        for c in range(coefs):
            drive[pl.ds(c * bd, bd), :] = total[:, c * width : (c + 1) * width]

        some = min(32, bd)

        def pairs(turn):
            for i in range(some // 2):
                b = turn * some + 2 * i
                x0 = inc[which, b] - drive[pl.ds(b, coefs, stride=bd), :]
                x1 = inc[which, b + 1] - drive[pl.ds(b + 1, coefs, stride=bd), :]
                x = jnp.concatenate([x0, x1], axis=0).astype(jnp.bfloat16)
                both = jnp.dot(
                    x, jnp.concatenate([near[b], near[b + 1]], axis=1), preferred_element_type=jnp.float32
                )
                out_ref[which, b] = both[:coefs, :width].astype(jnp.bfloat16)
                out_ref[which, b + 1] = both[coefs:, width:].astype(jnp.bfloat16)

        each(bd // some, pairs)

    take(tile, tile_sem)
    info_down.wait()
    take_rows(send1, rows1, CAP, sem1)
    each(chunks, products(rows1))
    pack()
    for g in range(2):
        part1[half(g), :] = jnp.dot(
            pick1[half(g), :], y_all[...], preferred_element_type=jnp.float32
        ).astype(jnp.bfloat16)
        start_half(g, STAGED[0], part1, recv1, part_sem1)
    load_inc.wait()
    load_near.wait()
    for side in range(2):
        take(flags.at[pl.ds(0, n_src - 1)], flag_sem.at[side])
    solve(0, finish(STAGED[0], part1, recv1, part_sem1, far_sem1))

    newest = out_ref.at[0]
    placed = lambda c: jnp.bitwise_and(c, bd - 1)
    send_new = lambda k: send_rows(k, send0, rows0, CAP0, sem0)

    def gather_send_new(k):
        gather(newest, send0.at[k], obs_peer(k, n_obs), CAP0, AT0, placed)
        send_new(k).start()

    for k in order:
        gather_send_new(k)
    gather(newest, rows0.at[pl.ds(me_o * CAP0, CAP0)], me_o, CAP0, AT0, placed)
    take_rows(send2, rows2, CAP, sem2)
    each(chunks, products(rows2))
    pack()
    for g in range(2):
        part_old[half(g), :] = jnp.dot(pick2[half(g), :], y_all[...], preferred_element_type=jnp.float32)
    list_down.wait()
    take_rows(send0, rows0, CAP0, sem0)

    def new_products(turn):
        for i in range(0, 32, 2):
            r = turn * 32 + i
            two_products(
                rows0[lst[1, r]], rows0[lst[1, r + 1]], tile[lst[0, r]], tile[lst[0, r + 1]], y_new, CAPD, r
            )

    each(CAPD // 32, new_products)
    value = jnp.concatenate([y_new[c * CAPD : (c + 1) * CAPD, :] for c in range(coefs)], axis=1)
    value = value.astype(jnp.bfloat16)
    for g in range(2):
        added = jnp.dot(pick0[half(g), :], value, preferred_element_type=jnp.float32)
        part2[half(g), :] = (part_old[half(g), :] + added).astype(jnp.bfloat16)
        start_half(g, STAGED[1], part2, recv2, part_sem2)
    solve(1, finish(STAGED[1], part2, recv2, part_sem2, far_sem2))
    crowded_ref[0, 0] = jnp.max(flags[...])


def dense_path(tile_rows, index_rows, live_count, history, incident, near_inverse, n_src, n_obs):
    bd, width = near_inverse.shape[:2]
    slots, coefs = history.shape[:2]
    n_tiles = tile_rows.shape[0]
    group = min(64, n_tiles)

    def gather_obs(block):
        ring = [(i, (i + 1) % n_obs) for i in range(n_obs)]
        me = lax.axis_index("obs")
        whole = jnp.zeros((n_obs,) + block.shape, block.dtype)
        whole = lax.dynamic_update_index_in_dim(whole, block, me, 0)

        def hop(k, carry):
            whole, moving = carry
            whole = lax.dynamic_update_index_in_dim(whole, moving, lax.rem(me - k + n_obs, n_obs), 0)
            return whole, lax.ppermute(moving, "obs", ring)

        return lax.fori_loop(1, n_obs, hop, (whole, lax.ppermute(block, "obs", ring)))[0]

    def sum_src(value):
        ring = [(i, (i + 1) % n_src) for i in range(n_src)]

        def hop(k, carry):
            total, moving = carry
            moving = lax.ppermute(moving, "src", ring)
            return total + moving, moving

        return lax.fori_loop(0, n_src - 1, hop, (value, value))[0]

    def accumulate(chooser):
        def one_group(turn, partial):
            start = turn * group
            tile_part = lax.dynamic_slice_in_dim(tile_rows, start, group, 0)
            index_part = lax.dynamic_slice_in_dim(index_rows, start, group, 1)
            products = jnp.einsum(
                "gck,gki->gci", chooser(index_part), tile_part, preferred_element_type=jnp.float32
            )
            alive = start + jnp.arange(group, dtype=jnp.int32) < live_count
            products = jnp.where(alive[:, None, None], products, 0.0)
            return partial.at[index_part[0]].add(products)

        initial = jnp.zeros((bd * n_src, coefs, width), jnp.float32)
        return lax.fori_loop(0, n_tiles // group, one_group, initial)

    def settle(partial, drive):
        own = lax.dynamic_slice_in_dim(sum_src(partial), lax.axis_index("src") * bd, bd, 0)
        right = (drive - own).astype(jnp.bfloat16)
        solved = jnp.einsum("bck,bki->bci", right, near_inverse, preferred_element_type=jnp.float32)
        return solved.astype(jnp.bfloat16)

    past = gather_obs(history)

    def pick(block, index_part, slot):
        return past[index_part[1] // bd, slot, index_part[1] % bd]

    past = past.reshape(n_obs, slots, coefs, bd, width).transpose(0, 1, 3, 2, 4)
    first = settle(accumulate(lambda ip: pick(past, ip, ip[2])), incident[0])
    newest = gather_obs(first)

    def second_rows(ip):
        older = pick(past, ip, jnp.maximum(ip[2] - 1, 0))
        newer = newest[ip[1] // bd, ip[1] % bd]
        return jnp.where((ip[2] == 0)[:, None, None], newer, older)

    second = settle(accumulate(second_rows), incident[1])
    return jnp.stack([first, second])


def solution(mesh):
    n_src, n_obs = mesh.shape["src"], mesh.shape["obs"]
    vmem = pl.BlockSpec(memory_space=pltpu.VMEM)
    smem = pl.BlockSpec(memory_space=pltpu.SMEM)
    hbm = pl.BlockSpec(memory_space=pltpu.HBM)
    dma = pltpu.SemaphoreType.DMA
    f32, bf16, i32 = jnp.float32, jnp.bfloat16, jnp.int32

    def params(i):
        return pltpu.CompilerParams(collective_id=i, has_side_effects=True)

    def on_device(tiles, tile_index, tile_count, history, incident, near_inverse):
        n_tiles, width = tiles.shape[2], tiles.shape[4]
        bd = near_inverse.shape[0]
        slots, coefs = history.shape[:2]
        tile_rows = tiles.reshape(n_tiles, width, width)
        index_rows = tile_index.transpose(0, 2, 1, 3).reshape(3, 1, n_tiles)
        hist = history.reshape(slots, coefs, bd, width).transpose(0, 2, 1, 3).reshape(slots * bd, coefs, width)
        drive = incident.reshape(2, coefs, bd, width).transpose(0, 2, 1, 3)

        def rows(cap):
            return pltpu.VMEM((n_obs * cap, coefs, width), bf16)

        def sends(cap):
            return pltpu.VMEM((n_obs, cap, coefs, width), bf16)

        def parts(kind):
            return pltpu.VMEM((n_src * bd, coefs * width), kind)

        arrived = pltpu.VMEM((n_src, bd, coefs * width), bf16)

        both, crowded = pl.pallas_call(
            functools.partial(step_kernel, n_src, n_obs, bd),
            name="step",
            out_shape=(
                jax.ShapeDtypeStruct((2, bd, coefs, width), bf16),
                jax.ShapeDtypeStruct((1, 1), f32),
            ),
            in_specs=[vmem, vmem, hbm, hbm, hbm, hbm],
            out_specs=(vmem, smem),
            scratch_shapes=[
                pltpu.VMEM((n_obs, 1, 128), i32), pltpu.VMEM((n_obs, 1, 128), i32),
                pltpu.VMEM((8, n_tiles), i32), pltpu.VMEM((8, 128), i32),
                pltpu.SMEM((n_obs, 1, 128), i32), pltpu.SMEM((8, n_tiles), i32), pltpu.SMEM((8, 128), i32),
                pltpu.VMEM((n_src, 1, 128), f32),
                pltpu.VMEM((n_tiles, width, width), bf16),
                pltpu.VMEM(hist.shape, bf16),
                pltpu.VMEM(drive.shape, f32),
                pltpu.VMEM((bd, width, width), bf16),
                rows(CAP), rows(CAP), rows(CAP0), sends(CAP), sends(CAP), sends(CAP0),
                pltpu.VMEM((1, 128), f32),
                pltpu.VMEM((coefs * n_tiles, width), f32),
                pltpu.VMEM((n_tiles, coefs * width), bf16),
                pltpu.VMEM((coefs * CAPD, width), f32),
                pltpu.VMEM((n_src * bd, n_tiles), bf16),
                pltpu.VMEM((n_src * bd, n_tiles), bf16),
                pltpu.VMEM((n_src * bd, CAPD), bf16),
                parts(f32), parts(bf16), parts(bf16), arrived, arrived,
                pltpu.VMEM((bd, coefs * width), bf16), pltpu.VMEM((bd, coefs * width), bf16),
                pltpu.VMEM((coefs * bd, width), f32),
                dma, dma((6,)), dma((2,)), dma((2,)), dma((2,)), dma((2,)), dma((2,)), dma((3,)), dma((3,)), dma((2,)), dma((2,)),
            ],
            compiler_params=params(0),
        )(tile_count, index_rows, tile_rows, hist, drive, near_inverse)

        both = lax.cond(
            crowded[0, 0] > 0.0,
            lambda kept: dense_path(
                tile_rows, tile_index.reshape(3, n_tiles), tile_count.reshape(()), history, drive, near_inverse,
                n_src, n_obs,
            ),
            lambda kept: kept,
            both,
        )
        return both.transpose(0, 2, 1, 3).reshape(2, coefs, bd * width)

    in_specs = (
        P("src", "obs", None, None, None),
        P("src", "obs", None, None),
        P("src", "obs"),
        P(None, None, ("src", "obs")),
        P(None, None, ("src", "obs")),
        P(("src", "obs"), None, None),
    )
    out_specs = P(None, None, ("src", "obs"))
    return jax.shard_map(on_device, mesh=mesh, in_specs=in_specs, out_specs=out_specs, check_vma=False)
```

```python
import functools

import jax
import jax.numpy as jnp
from jax import lax
from jax.experimental import pallas as pl
from jax.experimental.pallas import tpu as pltpu
from jax.sharding import PartitionSpec as P

MESH = pl.DeviceIdType.MESH
CAP = 60
CAP0 = 12
CAPD = 64
FAR = -(1 << 20)
ORDER = (6, 14, 7, 15, 10, 11, 2, 3, 8, 9, 4, 12, 5, 13, 1)
STAGED = (True, False)
AT0 = 64


def greet(src_peers, obs_peers, n_src, n_obs):
    me_s, me_o = lax.axis_index("src"), lax.axis_index("obs")
    barrier = pltpu.get_barrier_semaphore()
    if obs_peers:
        for k in ORDER if n_obs == len(ORDER) + 1 else range(1, n_obs):
            pl.semaphore_signal(barrier, inc=1, device_id=(me_s, obs_peer(k, n_obs)), device_id_type=MESH)
    if src_peers:
        for k in range(1, n_src):
            pl.semaphore_signal(
                barrier, inc=1, device_id=(lax.rem(me_s + k, n_src), me_o), device_id_type=MESH
            )
    total = (n_src - 1) * src_peers + (n_obs - 1) * obs_peers
    return lambda: pl.semaphore_wait(barrier, total)


def obs_peer(k, n_obs):
    me = lax.axis_index("obs")
    x = lax.rem(me // 4 + k // 4, n_obs // 4)
    z = lax.rem(lax.rem(me // 2, 2) + lax.rem(k // 2, 2), 2)
    core = lax.rem(lax.rem(me, 2) + lax.rem(k, 2), 2)
    return x * 4 + z * 2 + core


def to_obs(k, n_obs, src_ref, dst_ref, send_sem, recv_sem):
    return pltpu.make_async_remote_copy(
        src_ref=src_ref, dst_ref=dst_ref, send_sem=send_sem, recv_sem=recv_sem,
        device_id=(lax.axis_index("src"), obs_peer(k, n_obs)), device_id_type=MESH,
    )


def to_src(peer, src_ref, dst_ref, send_sem, recv_sem):
    return pltpu.make_async_remote_copy(
        src_ref=src_ref, dst_ref=dst_ref, send_sem=send_sem, recv_sem=recv_sem,
        device_id=(peer, lax.axis_index("obs")), device_id_type=MESH,
    )


def take(ref, sem):
    pltpu.make_async_copy(ref, ref, sem).wait()


def each(count, body, start=0):
    lax.fori_loop(start, count, lambda i, carry: (body(i), carry)[1], 0)


def build_requests(n_src, n_obs, bd, rows, idx_ref, cnt_ref, send_ref, info_ref, list_ref):
    n_tiles = idx_ref.shape[2]
    shift = bd.bit_length() - 1
    lane = lax.broadcasted_iota(jnp.int32, (1, n_tiles), 1)
    live = lane < cnt_ref[...]
    obs_block, source, delay = idx_ref[0], idx_ref[1], idx_ref[2]
    owner = lax.shift_right_logical(source, shift)
    place = jnp.bitwise_and(source, bd - 1)
    owner_row = lax.broadcasted_iota(jnp.int32, (n_obs, n_tiles), 0)
    mine = jnp.where(jnp.logical_and(owner == owner_row, live), 1.0, 0.0)
    mine0 = jnp.where(delay == 0, mine, 0.0)
    before = jnp.where(
        lax.broadcasted_iota(jnp.int32, (n_tiles, n_tiles), 0)
        < lax.broadcasted_iota(jnp.int32, (n_tiles, n_tiles), 1),
        1.0, 0.0,
    ).astype(jnp.bfloat16)
    both = jnp.concatenate([mine, mine0], axis=0).astype(jnp.bfloat16)
    order = jnp.dot(both, before, preferred_element_type=jnp.float32)
    rank = jnp.sum(order[:n_obs] * mine, axis=0, keepdims=True)
    rank0 = jnp.sum(order[n_obs:] * mine0, axis=0, keepdims=True)
    rank_d = jnp.sum(order[n_obs:], axis=0, keepdims=True)
    newest = jnp.logical_and(live, delay == 0)
    over = jnp.where(live, jnp.where(rank >= CAP, 1.0, 0.0), 0.0) + jnp.where(
        newest, jnp.where(rank0 >= CAP0, 1.0, 0.0) + jnp.where(rank_d >= CAPD, 1.0, 0.0), 0.0
    )
    flag = jnp.where(jnp.max(over, axis=1, keepdims=True) > 0.0, 1.0, 0.0)
    rank = rank.astype(jnp.int32)
    rank0 = rank0.astype(jnp.int32)
    fits = jnp.logical_and(live, rank < CAP)
    fits0 = jnp.logical_and(newest, rank0 < CAP0)
    nowhere = n_src * bd
    info_ref[0:1, :] = jnp.clip(jnp.where(fits, owner * CAP + rank, 0), 0, n_obs * CAP - 1)
    info_ref[1:2, :] = jnp.where(live, obs_block, nowhere)
    info_ref[2:3, :] = jnp.where(jnp.logical_and(live, delay > 0), obs_block, nowhere)
    info_ref[3:8, :] = jnp.zeros((5, n_tiles), jnp.int32)
    row = lax.broadcasted_iota(jnp.int32, (128, n_tiles), 0)
    ones = lambda hit: jnp.where(hit, 1.0, 0.0).astype(jnp.bfloat16)
    key = jnp.where(fits, rank, FAR)
    key0 = jnp.where(fits0, rank0 + AT0, FAR)
    coded = jnp.concatenate([mine * place.astype(jnp.float32), mine * delay.astype(jnp.float32)], axis=0)

    def find(codes, hit):
        return lax.dot_general(
            codes.astype(jnp.bfloat16), ones(hit), (((1,), (1,)), ((), ())), preferred_element_type=jnp.float32
        )

    found = find(coded, jnp.logical_or(key == row, key0 == row))
    code = found[:n_obs] + found[n_obs:] * bd
    out_lane = lax.broadcasted_iota(jnp.int32, (n_obs, 128), 1)
    code = jnp.clip(jnp.where(out_lane == 127, flag, code).astype(jnp.int32), 0, rows - 1)
    for o in range(n_obs):
        send_ref[o] = code[o : o + 1]

    def build_list():
        key_d = jnp.where(newest, rank_d.astype(jnp.int32), FAR)
        code_row = lax.broadcasted_iota(jnp.int32, (16, n_tiles), 0)
        codes = jnp.zeros((16, n_tiles), jnp.int32)
        slot0 = jnp.where(fits0, owner * CAP0 + rank0, 0)
        parts = (
            jnp.bitwise_and(lane, 127), lax.shift_right_logical(lane, 7), slot0,
            jnp.bitwise_and(obs_block, 127), lax.shift_right_logical(obs_block, 7), jnp.ones_like(lane),
        )
        for i, part in enumerate(parts):
            codes = jnp.where(code_row == i, part, codes)
        found = find(codes.astype(jnp.float32), key_d == row)
        list_ref[0:1, :] = jnp.clip((found[0:1, :] + found[1:2, :] * 128.0).astype(jnp.int32), 0, n_tiles - 1)
        list_ref[1:2, :] = jnp.clip(found[2:3, :].astype(jnp.int32), 0, n_obs * CAP0 - 1)
        block = jnp.where(found[5:6, :] > 0.5, found[3:4, :] + found[4:5, :] * 128.0, 1.0 * nowhere)
        list_ref[2:3, :] = block.astype(jnp.int32)
        list_ref[3:8, :] = jnp.zeros((5, 128), jnp.int32)

    return build_list


def step_kernel(
    n_src, n_obs, bd, cnt_hbm, idx_hbm, tiles_ref, hist_ref, inc_ref, near_ref,
    out_ref, crowded_ref,
    cnt_ref, idx_ref, ask, asked, info_v, list_v, req, info, lst, flags,
    tile, hist, inc, near, rows1, rows2, rows0, send1, send2, send0, mark,
    y_one, y_all, y_new, pick1, pick2, pick0, part_old, part1, part2, recv1, recv2, far_out, far_in, drive,
    tile_sem, load_sem, ask_sem, flag_sem, sem1, sem2, sem0, part_sem1, part_sem2, far_sem1, far_sem2,
):
    me_s, me_o = lax.axis_index("src"), lax.axis_index("obs")
    order = ORDER if n_obs == len(ORDER) + 1 else range(1, n_obs)
    load_cnt = pltpu.make_async_copy(cnt_hbm, cnt_ref, load_sem.at[6])
    load_idx = pltpu.make_async_copy(idx_hbm, idx_ref, load_sem.at[7])
    load_cnt.start()
    load_idx.start()
    entered = greet(1, 1, n_src, n_obs)
    n_tiles = tiles_ref.shape[0]
    chunk = min(64, n_tiles)
    chunks = n_tiles // chunk
    width = tiles_ref.shape[2]
    coefs = hist_ref.shape[1]
    load_hist = pltpu.make_async_copy(hist_ref, hist, load_sem.at[0])
    load_near = pltpu.make_async_copy(near_ref, near, load_sem.at[1])
    load_inc = pltpu.make_async_copy(inc_ref, inc, load_sem.at[2])

    def load_tiles(c):
        at = pl.ds(c * chunk, chunk)
        return pltpu.make_async_copy(tiles_ref.at[at], tile.at[at], tile_sem)

    load_hist.start()
    load_cnt.wait()
    load_idx.wait()
    build_list = build_requests(n_src, n_obs, bd, hist_ref.shape[0], idx_ref, cnt_ref, ask, info_v, list_v)
    asked[me_o] = ask[me_o]

    def send_ask(k):
        return to_obs(k, n_obs, ask.at[obs_peer(k, n_obs)], asked.at[me_o], ask_sem.at[0], ask_sem.at[1])

    entered()
    for k in order:
        send_ask(k).start()
    build_list()
    info_down = pltpu.make_async_copy(info_v, info, load_sem.at[3])
    list_down = pltpu.make_async_copy(list_v, lst, load_sem.at[4])
    info_down.start()
    list_down.start()
    ones = lambda hit: jnp.where(hit, 1.0, 0.0).astype(jnp.bfloat16)
    row = lax.broadcasted_iota(jnp.int32, (bd, n_tiles), 0)
    row0 = lax.broadcasted_iota(jnp.int32, (bd, CAPD), 0)

    n_y = n_src // 2
    me_z, me_y = me_s // n_y, lax.rem(me_s, n_y)

    def place_of(k):
        return lax.rem(me_z + 1 - k // n_y, 2) * n_y + lax.rem(me_y + 1 + lax.rem(k, n_y), n_y)

    def one_pick(k):
        first = place_of(k) * bd
        at = pl.ds(pl.multiple_of(k * bd, bd), bd)
        pick1[at, :] = ones(info_v[1:2, :] - first == row)
        pick2[at, :] = ones(info_v[2:3, :] - first == row)
        pick0[at, :] = ones(list_v[2:3, 0:CAPD] - first == row0)

    each(n_src, one_pick)
    others = pl.ds(0, n_obs - 1)
    take(asked.at[others], ask_sem.at[1])
    take(ask.at[others], ask_sem.at[0])
    req_down = pltpu.make_async_copy(asked, req, load_sem.at[5])
    req_down.start()
    worst = jnp.max(asked[...].astype(jnp.float32), axis=0)
    worst = jnp.where(lax.broadcasted_iota(jnp.int32, worst.shape, 1) == 127, worst, 0.0)
    mark[...] = jnp.broadcast_to(jnp.max(worst, axis=1, keepdims=True), mark.shape)
    flags[me_s] = mark[...]

    def gather(table, out, o, slots, first, code_to_row):
        def twelve(turn):
            for i in range(12):
                r = turn * 12 + i
                out[r] = table[code_to_row(req[o, 0, first + r])]

        each(slots // 12, twelve)

    def send_flag(k):
        return to_src(lax.rem(me_s + k, n_src), mark, flags.at[me_s], flag_sem.at[0], flag_sem.at[1])

    def send_rows(k, send, rows, cap, sem):
        return to_obs(k, n_obs, send.at[k], rows.at[pl.ds(me_o * cap, cap)], sem.at[0], sem.at[1])

    def take_rows(send, rows, cap, sem):
        take(rows.at[pl.ds(0, (n_obs - 1) * cap)], sem.at[1])
        take(send.at[pl.ds(1, n_obs - 1)], sem.at[0])

    def one_dest(k):
        gather(hist, send1.at[k], obs_peer(k, n_obs), CAP, 0, lambda c: c)

    def send_one(k):
        return send_rows(k, send1, rows1, CAP, sem1)

    load_hist.wait()
    req_down.wait()

    def gather_send(k):
        one_dest(k)
        send_one(k).start()

    for k in order:
        gather_send(k)
    each(chunks, lambda c: load_tiles(c).start())
    load_inc.start()
    load_near.start()
    each(n_src, lambda k: send_flag(k).start(), 1)
    gather(hist, rows1.at[pl.ds(me_o * CAP, CAP)], me_o, CAP, 0, lambda c: c)

    older = lambda c: jnp.maximum(c - bd, 0)
    def gather_send_two(k):
        gather(hist, send2.at[k], obs_peer(k, n_obs), CAP, 0, older)
        send_rows(k, send2, rows2, CAP, sem2).start()

    for k in order:
        gather_send_two(k)
    gather(hist, rows2.at[pl.ds(me_o * CAP, CAP)], me_o, CAP, 0, older)

    def two_products(x0, x1, t0, t1, y, count, at):
        x = jnp.concatenate([x0.astype(jnp.float32), x1.astype(jnp.float32)], axis=0).astype(jnp.bfloat16)
        both = jnp.dot(x, jnp.concatenate([t0, t1], axis=1), preferred_element_type=jnp.float32)
        y[pl.ds(at, coefs, stride=count), :] = both[:coefs, :width]
        y[pl.ds(at + 1, coefs, stride=count), :] = both[coefs:, width:]

    def products(rows):
        def one_chunk(c):
            for i in range(0, chunk, 2):
                t = c * chunk + i
                two_products(rows[info[0, t]], rows[info[0, t + 1]], tile[t], tile[t + 1], y_one, n_tiles, t)

        return one_chunk

    def pack():
        for c in range(coefs):
            lanes = slice(c * width, (c + 1) * width)

            def some(i):
                at = pl.multiple_of(i * 64, 64)
                y_all[pl.ds(at, 64), lanes] = y_one[pl.ds(c * n_tiles + at, 64), :].astype(jnp.bfloat16)

            each(n_tiles // 64, some)

    def start_half(g, staged, part, recv, sem):
        for i in range(n_y - staged if g == 0 else n_y - 1):
            k = g * n_y + i
            peer = me_z * n_y + lax.rem(me_y + 1 + i, n_y) if staged else place_of(k)
            to_src(peer, part.at[pl.ds(k * bd, bd)], recv.at[k], sem.at[0], sem.at[1 + g]).start()

    def finish(staged, part, recv, sem, far_sem):
        def half_sum(g, count):
            if count:
                take(recv.at[pl.ds(g * n_y, count)], sem.at[1 + g])
            total = part[(g * n_y + n_y - 1) * bd : (g + 1) * n_y * bd, :].astype(jnp.float32)
            for i in range(n_y - 1):
                total = total + recv[g * n_y + i].astype(jnp.float32)
            return total

        sent = n_src - 2 if staged else n_src - 1
        if staged:
            far_out[...] = half_sum(0, n_y - 1).astype(jnp.bfloat16)
            peer = lax.rem(me_z + 1, 2) * n_y + me_y
            far = to_src(peer, far_out, far_in, far_sem.at[0], far_sem.at[1])
            far.start()
            total = half_sum(1, n_y - 1)
            far.wait()
            total = total + far_in[...].astype(jnp.float32)
        else:
            take(recv.at[pl.ds(0, n_y)], sem.at[1])
            total = half_sum(1, n_y - 1)
            for k in range(n_y):
                total = total + recv[k].astype(jnp.float32)
        if sent:
            take(recv.at[pl.ds(0, sent)], sem.at[0])
        return total

    group = n_src // 2
    half = lambda g: slice(g * group * bd, (g + 1) * group * bd)

    def solve(which, total):
        for c in range(coefs):
            drive[pl.ds(c * bd, bd), :] = total[:, c * width : (c + 1) * width]

        some = min(32, bd)

        def pairs(turn):
            for i in range(some // 2):
                b = turn * some + 2 * i
                x0 = inc[which, b] - drive[pl.ds(b, coefs, stride=bd), :]
                x1 = inc[which, b + 1] - drive[pl.ds(b + 1, coefs, stride=bd), :]
                x = jnp.concatenate([x0, x1], axis=0).astype(jnp.bfloat16)
                both = jnp.dot(
                    x, jnp.concatenate([near[b], near[b + 1]], axis=1), preferred_element_type=jnp.float32
                )
                out_ref[which, b] = both[:coefs, :width].astype(jnp.bfloat16)
                out_ref[which, b + 1] = both[coefs:, width:].astype(jnp.bfloat16)

        each(bd // some, pairs)

    take(tile, tile_sem)
    info_down.wait()
    take_rows(send1, rows1, CAP, sem1)
    each(chunks, products(rows1))
    pack()
    for g in range(2):
        part1[half(g), :] = jnp.dot(
            pick1[half(g), :], y_all[...], preferred_element_type=jnp.float32
        ).astype(jnp.bfloat16)
        start_half(g, STAGED[0], part1, recv1, part_sem1)
    load_inc.wait()
    load_near.wait()
    for side in range(2):
        take(flags.at[pl.ds(0, n_src - 1)], flag_sem.at[side])
    solve(0, finish(STAGED[0], part1, recv1, part_sem1, far_sem1))

    newest = out_ref.at[0]
    placed = lambda c: jnp.bitwise_and(c, bd - 1)
    send_new = lambda k: send_rows(k, send0, rows0, CAP0, sem0)

    def gather_send_new(k):
        gather(newest, send0.at[k], obs_peer(k, n_obs), CAP0, AT0, placed)
        send_new(k).start()

    for k in order:
        gather_send_new(k)
    gather(newest, rows0.at[pl.ds(me_o * CAP0, CAP0)], me_o, CAP0, AT0, placed)
    take_rows(send2, rows2, CAP, sem2)
    each(chunks, products(rows2))
    pack()
    for g in range(2):
        part_old[half(g), :] = jnp.dot(pick2[half(g), :], y_all[...], preferred_element_type=jnp.float32)
    list_down.wait()
    take_rows(send0, rows0, CAP0, sem0)

    def new_products(turn):
        for i in range(0, 32, 2):
            r = turn * 32 + i
            two_products(
                rows0[lst[1, r]], rows0[lst[1, r + 1]], tile[lst[0, r]], tile[lst[0, r + 1]], y_new, CAPD, r
            )

    each(CAPD // 32, new_products)
    value = jnp.concatenate([y_new[c * CAPD : (c + 1) * CAPD, :] for c in range(coefs)], axis=1)
    value = value.astype(jnp.bfloat16)
    for g in range(2):
        added = jnp.dot(pick0[half(g), :], value, preferred_element_type=jnp.float32)
        part2[half(g), :] = (part_old[half(g), :] + added).astype(jnp.bfloat16)
        start_half(g, STAGED[1], part2, recv2, part_sem2)
    solve(1, finish(STAGED[1], part2, recv2, part_sem2, far_sem2))
    crowded_ref[0, 0] = jnp.max(flags[...])


def dense_path(tile_rows, index_rows, live_count, history, incident, near_inverse, n_src, n_obs):
    bd, width = near_inverse.shape[:2]
    slots, coefs = history.shape[:2]
    n_tiles = tile_rows.shape[0]
    group = min(64, n_tiles)

    def gather_obs(block):
        ring = [(i, (i + 1) % n_obs) for i in range(n_obs)]
        me = lax.axis_index("obs")
        whole = jnp.zeros((n_obs,) + block.shape, block.dtype)
        whole = lax.dynamic_update_index_in_dim(whole, block, me, 0)

        def hop(k, carry):
            whole, moving = carry
            whole = lax.dynamic_update_index_in_dim(whole, moving, lax.rem(me - k + n_obs, n_obs), 0)
            return whole, lax.ppermute(moving, "obs", ring)

        return lax.fori_loop(1, n_obs, hop, (whole, lax.ppermute(block, "obs", ring)))[0]

    def sum_src(value):
        ring = [(i, (i + 1) % n_src) for i in range(n_src)]

        def hop(k, carry):
            total, moving = carry
            moving = lax.ppermute(moving, "src", ring)
            return total + moving, moving

        return lax.fori_loop(0, n_src - 1, hop, (value, value))[0]

    def accumulate(chooser):
        def one_group(turn, partial):
            start = turn * group
            tile_part = lax.dynamic_slice_in_dim(tile_rows, start, group, 0)
            index_part = lax.dynamic_slice_in_dim(index_rows, start, group, 1)
            products = jnp.einsum(
                "gck,gki->gci", chooser(index_part), tile_part, preferred_element_type=jnp.float32
            )
            alive = start + jnp.arange(group, dtype=jnp.int32) < live_count
            products = jnp.where(alive[:, None, None], products, 0.0)
            return partial.at[index_part[0]].add(products)

        initial = jnp.zeros((bd * n_src, coefs, width), jnp.float32)
        return lax.fori_loop(0, n_tiles // group, one_group, initial)

    def settle(partial, drive):
        own = lax.dynamic_slice_in_dim(sum_src(partial), lax.axis_index("src") * bd, bd, 0)
        right = (drive - own).astype(jnp.bfloat16)
        solved = jnp.einsum("bck,bki->bci", right, near_inverse, preferred_element_type=jnp.float32)
        return solved.astype(jnp.bfloat16)

    past = gather_obs(history)

    def pick(block, index_part, slot):
        return past[index_part[1] // bd, slot, index_part[1] % bd]

    past = past.reshape(n_obs, slots, coefs, bd, width).transpose(0, 1, 3, 2, 4)
    first = settle(accumulate(lambda ip: pick(past, ip, ip[2])), incident[0])
    newest = gather_obs(first)

    def second_rows(ip):
        older = pick(past, ip, jnp.maximum(ip[2] - 1, 0))
        newer = newest[ip[1] // bd, ip[1] % bd]
        return jnp.where((ip[2] == 0)[:, None, None], newer, older)

    second = settle(accumulate(second_rows), incident[1])
    return jnp.stack([first, second])


def solution(mesh):
    n_src, n_obs = mesh.shape["src"], mesh.shape["obs"]
    vmem = pl.BlockSpec(memory_space=pltpu.VMEM)
    smem = pl.BlockSpec(memory_space=pltpu.SMEM)
    hbm = pl.BlockSpec(memory_space=pltpu.HBM)
    dma = pltpu.SemaphoreType.DMA
    f32, bf16, i32 = jnp.float32, jnp.bfloat16, jnp.int32

    def params(i):
        return pltpu.CompilerParams(collective_id=i, has_side_effects=True)

    def on_device(tiles, tile_index, tile_count, history, incident, near_inverse):
        n_tiles, width = tiles.shape[2], tiles.shape[4]
        bd = near_inverse.shape[0]
        slots, coefs = history.shape[:2]
        tile_rows = tiles.reshape(n_tiles, width, width)
        index_rows = tile_index.transpose(0, 2, 1, 3).reshape(3, 1, n_tiles)
        hist = history.reshape(slots, coefs, bd, width).transpose(0, 2, 1, 3).reshape(slots * bd, coefs, width)
        drive = incident.reshape(2, coefs, bd, width).transpose(0, 2, 1, 3)

        def rows(cap):
            return pltpu.VMEM((n_obs * cap, coefs, width), bf16)

        def sends(cap):
            return pltpu.VMEM((n_obs, cap, coefs, width), bf16)

        def parts(kind):
            return pltpu.VMEM((n_src * bd, coefs * width), kind)

        arrived = pltpu.VMEM((n_src, bd, coefs * width), bf16)

        both, crowded = pl.pallas_call(
            functools.partial(step_kernel, n_src, n_obs, bd),
            name="step",
            out_shape=(
                jax.ShapeDtypeStruct((2, bd, coefs, width), bf16),
                jax.ShapeDtypeStruct((1, 1), f32),
            ),
            in_specs=[hbm] * 6,
            out_specs=(vmem, smem),
            scratch_shapes=[
                pltpu.VMEM((1, 1), i32), pltpu.VMEM(index_rows.shape, i32),
                pltpu.VMEM((n_obs, 1, 128), i32), pltpu.VMEM((n_obs, 1, 128), i32),
                pltpu.VMEM((8, n_tiles), i32), pltpu.VMEM((8, 128), i32),
                pltpu.SMEM((n_obs, 1, 128), i32), pltpu.SMEM((8, n_tiles), i32), pltpu.SMEM((8, 128), i32),
                pltpu.VMEM((n_src, 1, 128), f32),
                pltpu.VMEM((n_tiles, width, width), bf16),
                pltpu.VMEM(hist.shape, bf16),
                pltpu.VMEM(drive.shape, f32),
                pltpu.VMEM((bd, width, width), bf16),
                rows(CAP), rows(CAP), rows(CAP0), sends(CAP), sends(CAP), sends(CAP0),
                pltpu.VMEM((1, 128), f32),
                pltpu.VMEM((coefs * n_tiles, width), f32),
                pltpu.VMEM((n_tiles, coefs * width), bf16),
                pltpu.VMEM((coefs * CAPD, width), f32),
                pltpu.VMEM((n_src * bd, n_tiles), bf16),
                pltpu.VMEM((n_src * bd, n_tiles), bf16),
                pltpu.VMEM((n_src * bd, CAPD), bf16),
                parts(f32), parts(bf16), parts(bf16), arrived, arrived,
                pltpu.VMEM((bd, coefs * width), bf16), pltpu.VMEM((bd, coefs * width), bf16),
                pltpu.VMEM((coefs * bd, width), f32),
                dma, dma((8,)), dma((2,)), dma((2,)), dma((2,)), dma((2,)), dma((2,)), dma((3,)), dma((3,)), dma((2,)), dma((2,)),
            ],
            compiler_params=params(0),
        )(tile_count, index_rows, tile_rows, hist, drive, near_inverse)

        both = lax.cond(
            crowded[0, 0] > 0.0,
            lambda kept: dense_path(
                tile_rows, tile_index.reshape(3, n_tiles), tile_count.reshape(()), history, drive, near_inverse,
                n_src, n_obs,
            ),
            lambda kept: kept,
            both,
        )
        return both.transpose(0, 2, 1, 3).reshape(2, coefs, bd * width)

    in_specs = (
        P("src", "obs", None, None, None),
        P("src", "obs", None, None),
        P("src", "obs"),
        P(None, None, ("src", "obs")),
        P(None, None, ("src", "obs")),
        P(("src", "obs"), None, None),
    )
    out_specs = P(None, None, ("src", "obs"))
    return jax.shard_map(on_device, mesh=mesh, in_specs=in_specs, out_specs=out_specs, check_vma=False)
```

```python
import functools

import jax
import jax.numpy as jnp
from jax import lax
from jax.experimental import pallas as pl
from jax.experimental.pallas import tpu as pltpu
from jax.sharding import PartitionSpec as P

MESH = pl.DeviceIdType.MESH
CAP = 60
CAP0 = 12
CAPD = 64
FAR = -(1 << 20)
ORDER = (6, 14, 7, 15, 10, 11, 2, 3, 8, 9, 4, 12, 5, 13, 1)
STAGED = (True, False)
AT0 = 64


def greet(src_peers, obs_peers, n_src, n_obs):
    me_s, me_o = lax.axis_index("src"), lax.axis_index("obs")
    barrier = pltpu.get_barrier_semaphore()
    if src_peers:
        for k in range(1, n_src):
            pl.semaphore_signal(
                barrier, inc=1, device_id=(lax.rem(me_s + k, n_src), me_o), device_id_type=MESH
            )
    if obs_peers:
        for k in range(1, n_obs):
            pl.semaphore_signal(
                barrier, inc=1, device_id=(me_s, obs_peer(k, n_obs)), device_id_type=MESH
            )
    total = (n_src - 1) * src_peers + (n_obs - 1) * obs_peers
    return lambda: pl.semaphore_wait(barrier, total)


def obs_peer(k, n_obs):
    me = lax.axis_index("obs")
    x = lax.rem(me // 4 + k // 4, n_obs // 4)
    z = lax.rem(lax.rem(me // 2, 2) + lax.rem(k // 2, 2), 2)
    core = lax.rem(lax.rem(me, 2) + lax.rem(k, 2), 2)
    return x * 4 + z * 2 + core


def to_obs(k, n_obs, src_ref, dst_ref, send_sem, recv_sem):
    return pltpu.make_async_remote_copy(
        src_ref=src_ref, dst_ref=dst_ref, send_sem=send_sem, recv_sem=recv_sem,
        device_id=(lax.axis_index("src"), obs_peer(k, n_obs)), device_id_type=MESH,
    )


def to_src(peer, src_ref, dst_ref, send_sem, recv_sem):
    return pltpu.make_async_remote_copy(
        src_ref=src_ref, dst_ref=dst_ref, send_sem=send_sem, recv_sem=recv_sem,
        device_id=(peer, lax.axis_index("obs")), device_id_type=MESH,
    )


def take(ref, sem):
    pltpu.make_async_copy(ref, ref, sem).wait()


def each(count, body, start=0):
    lax.fori_loop(start, count, lambda i, carry: (body(i), carry)[1], 0)


def build_requests(n_src, n_obs, bd, rows, idx_ref, cnt_ref, send_ref, info_ref, list_ref):
    n_tiles = idx_ref.shape[2]
    shift = bd.bit_length() - 1
    lane = lax.broadcasted_iota(jnp.int32, (1, n_tiles), 1)
    live = lane < cnt_ref[...]
    obs_block, source, delay = idx_ref[0], idx_ref[1], idx_ref[2]
    owner = lax.shift_right_logical(source, shift)
    place = jnp.bitwise_and(source, bd - 1)
    owner_row = lax.broadcasted_iota(jnp.int32, (n_obs, n_tiles), 0)
    mine = jnp.where(jnp.logical_and(owner == owner_row, live), 1.0, 0.0)
    mine0 = jnp.where(delay == 0, mine, 0.0)
    before = jnp.where(
        lax.broadcasted_iota(jnp.int32, (n_tiles, n_tiles), 0)
        < lax.broadcasted_iota(jnp.int32, (n_tiles, n_tiles), 1),
        1.0, 0.0,
    ).astype(jnp.bfloat16)
    both = jnp.concatenate([mine, mine0], axis=0).astype(jnp.bfloat16)
    order = jnp.dot(both, before, preferred_element_type=jnp.float32)
    rank = jnp.sum(order[:n_obs] * mine, axis=0, keepdims=True)
    rank0 = jnp.sum(order[n_obs:] * mine0, axis=0, keepdims=True)
    rank_d = jnp.sum(order[n_obs:], axis=0, keepdims=True)
    newest = jnp.logical_and(live, delay == 0)
    over = jnp.where(live, jnp.where(rank >= CAP, 1.0, 0.0), 0.0) + jnp.where(
        newest, jnp.where(rank0 >= CAP0, 1.0, 0.0) + jnp.where(rank_d >= CAPD, 1.0, 0.0), 0.0
    )
    flag = jnp.where(jnp.max(over, axis=1, keepdims=True) > 0.0, 1.0, 0.0)
    rank = rank.astype(jnp.int32)
    rank0 = rank0.astype(jnp.int32)
    fits = jnp.logical_and(live, rank < CAP)
    fits0 = jnp.logical_and(newest, rank0 < CAP0)
    nowhere = n_src * bd
    info_ref[0:1, :] = jnp.clip(jnp.where(fits, owner * CAP + rank, 0), 0, n_obs * CAP - 1)
    info_ref[1:2, :] = jnp.where(live, obs_block, nowhere)
    info_ref[2:3, :] = jnp.where(jnp.logical_and(live, delay > 0), obs_block, nowhere)
    info_ref[3:8, :] = jnp.zeros((5, n_tiles), jnp.int32)
    row = lax.broadcasted_iota(jnp.int32, (128, n_tiles), 0)
    ones = lambda hit: jnp.where(hit, 1.0, 0.0).astype(jnp.bfloat16)
    key = jnp.where(fits, rank, FAR)
    key0 = jnp.where(fits0, rank0 + AT0, FAR)
    coded = jnp.concatenate([mine * place.astype(jnp.float32), mine * delay.astype(jnp.float32)], axis=0)

    def find(codes, hit):
        return lax.dot_general(
            codes.astype(jnp.bfloat16), ones(hit), (((1,), (1,)), ((), ())), preferred_element_type=jnp.float32
        )

    found = find(coded, jnp.logical_or(key == row, key0 == row))
    code = found[:n_obs] + found[n_obs:] * bd
    out_lane = lax.broadcasted_iota(jnp.int32, (n_obs, 128), 1)
    code = jnp.clip(jnp.where(out_lane == 127, flag, code).astype(jnp.int32), 0, rows - 1)
    for o in range(n_obs):
        send_ref[o] = code[o : o + 1]

    def build_list():
        key_d = jnp.where(newest, rank_d.astype(jnp.int32), FAR)
        code_row = lax.broadcasted_iota(jnp.int32, (16, n_tiles), 0)
        codes = jnp.zeros((16, n_tiles), jnp.int32)
        slot0 = jnp.where(fits0, owner * CAP0 + rank0, 0)
        parts = (
            jnp.bitwise_and(lane, 127), lax.shift_right_logical(lane, 7), slot0,
            jnp.bitwise_and(obs_block, 127), lax.shift_right_logical(obs_block, 7), jnp.ones_like(lane),
        )
        for i, part in enumerate(parts):
            codes = jnp.where(code_row == i, part, codes)
        found = find(codes.astype(jnp.float32), key_d == row)
        list_ref[0:1, :] = jnp.clip((found[0:1, :] + found[1:2, :] * 128.0).astype(jnp.int32), 0, n_tiles - 1)
        list_ref[1:2, :] = jnp.clip(found[2:3, :].astype(jnp.int32), 0, n_obs * CAP0 - 1)
        block = jnp.where(found[5:6, :] > 0.5, found[3:4, :] + found[4:5, :] * 128.0, 1.0 * nowhere)
        list_ref[2:3, :] = block.astype(jnp.int32)
        list_ref[3:8, :] = jnp.zeros((5, 128), jnp.int32)

    return build_list


def step_kernel(
    n_src, n_obs, bd, cnt_ref, idx_ref, tiles_ref, hist_ref, inc_ref, near_ref,
    out_ref, crowded_ref,
    ask, asked, info_v, list_v, req, info, lst, flags,
    tile, hist, inc, near, rows1, rows2, rows0, send1, send2, send0, mark,
    y_one, y_all, y_new, pick1, pick2, pick0, part_old, part1, part2, recv1, recv2, far_out, far_in, drive,
    tile_sem, load_sem, ask_sem, flag_sem, sem1, sem2, sem0, part_sem1, part_sem2, far_sem1, far_sem2,
):
    me_s, me_o = lax.axis_index("src"), lax.axis_index("obs")
    order = ORDER if n_obs == len(ORDER) + 1 else range(1, n_obs)
    entered = greet(1, 1, n_src, n_obs)
    n_tiles = tiles_ref.shape[0]
    chunk = min(128, n_tiles)
    chunks = n_tiles // chunk
    width = tiles_ref.shape[2]
    coefs = hist_ref.shape[1]
    load_hist = pltpu.make_async_copy(hist_ref, hist, load_sem.at[0])
    load_near = pltpu.make_async_copy(near_ref, near, load_sem.at[1])
    load_inc = pltpu.make_async_copy(inc_ref, inc, load_sem.at[2])

    def load_tiles(c):
        at = pl.ds(c * chunk, chunk)
        return pltpu.make_async_copy(tiles_ref.at[at], tile.at[at], tile_sem)

    load_hist.start()
    build_list = build_requests(n_src, n_obs, bd, hist_ref.shape[0], idx_ref, cnt_ref, ask, info_v, list_v)
    asked[me_o] = ask[me_o]

    def send_ask(k):
        return to_obs(k, n_obs, ask.at[obs_peer(k, n_obs)], asked.at[me_o], ask_sem.at[0], ask_sem.at[1])

    entered()
    for k in order:
        send_ask(k).start()
    build_list()
    info_down = pltpu.make_async_copy(info_v, info, load_sem.at[3])
    list_down = pltpu.make_async_copy(list_v, lst, load_sem.at[4])
    info_down.start()
    list_down.start()
    ones = lambda hit: jnp.where(hit, 1.0, 0.0).astype(jnp.bfloat16)
    row = lax.broadcasted_iota(jnp.int32, (bd, n_tiles), 0)
    row0 = lax.broadcasted_iota(jnp.int32, (bd, CAPD), 0)

    n_y = n_src // 2
    me_z, me_y = me_s // n_y, lax.rem(me_s, n_y)

    def place_of(k):
        return lax.rem(me_z + 1 - k // n_y, 2) * n_y + lax.rem(me_y + 1 + lax.rem(k, n_y), n_y)

    def one_pick(k):
        first = place_of(k) * bd
        at = pl.ds(pl.multiple_of(k * bd, bd), bd)
        pick1[at, :] = ones(info_v[1:2, :] - first == row)
        pick2[at, :] = ones(info_v[2:3, :] - first == row)
        pick0[at, :] = ones(list_v[2:3, 0:CAPD] - first == row0)

    each(n_src, one_pick)
    others = pl.ds(0, n_obs - 1)
    take(asked.at[others], ask_sem.at[1])
    take(ask.at[others], ask_sem.at[0])
    req_down = pltpu.make_async_copy(asked, req, load_sem.at[5])
    req_down.start()
    worst = jnp.max(asked[...].astype(jnp.float32), axis=0)
    worst = jnp.where(lax.broadcasted_iota(jnp.int32, worst.shape, 1) == 127, worst, 0.0)
    mark[...] = jnp.broadcast_to(jnp.max(worst, axis=1, keepdims=True), mark.shape)
    flags[me_s] = mark[...]

    def gather(table, out, o, slots, first, code_to_row):
        def twelve(turn):
            for i in range(12):
                r = turn * 12 + i
                out[r] = table[code_to_row(req[o, 0, first + r])]

        each(slots // 12, twelve)

    def send_flag(k):
        return to_src(lax.rem(me_s + k, n_src), mark, flags.at[me_s], flag_sem.at[0], flag_sem.at[1])

    def send_rows(k, send, rows, cap, sem):
        return to_obs(k, n_obs, send.at[k], rows.at[pl.ds(me_o * cap, cap)], sem.at[0], sem.at[1])

    def take_rows(send, rows, cap, sem):
        take(rows.at[pl.ds(0, (n_obs - 1) * cap)], sem.at[1])
        take(send.at[pl.ds(1, n_obs - 1)], sem.at[0])

    def one_dest(k):
        gather(hist, send1.at[k], obs_peer(k, n_obs), CAP, 0, lambda c: c)

    def send_one(k):
        return send_rows(k, send1, rows1, CAP, sem1)

    load_hist.wait()
    req_down.wait()

    def gather_send(k):
        one_dest(k)
        send_one(k).start()

    for k in order:
        gather_send(k)
    each(chunks, lambda c: load_tiles(c).start())
    load_inc.start()
    load_near.start()
    each(n_src, lambda k: send_flag(k).start(), 1)
    gather(hist, rows1.at[pl.ds(me_o * CAP, CAP)], me_o, CAP, 0, lambda c: c)

    older = lambda c: jnp.maximum(c - bd, 0)
    def gather_send_two(k):
        gather(hist, send2.at[k], obs_peer(k, n_obs), CAP, 0, older)
        send_rows(k, send2, rows2, CAP, sem2).start()

    for k in order:
        gather_send_two(k)
    gather(hist, rows2.at[pl.ds(me_o * CAP, CAP)], me_o, CAP, 0, older)

    def two_products(x0, x1, t0, t1, y, count, at):
        x = jnp.concatenate([x0.astype(jnp.float32), x1.astype(jnp.float32)], axis=0).astype(jnp.bfloat16)
        both = jnp.dot(x, jnp.concatenate([t0, t1], axis=1), preferred_element_type=jnp.float32)
        y[pl.ds(at, coefs, stride=count), :] = both[:coefs, :width]
        y[pl.ds(at + 1, coefs, stride=count), :] = both[coefs:, width:]

    def products(rows):
        def one_chunk(c):
            for i in range(0, chunk, 2):
                t = c * chunk + i
                two_products(rows[info[0, t]], rows[info[0, t + 1]], tile[t], tile[t + 1], y_one, n_tiles, t)

        return one_chunk

    def pack():
        for c in range(coefs):
            lanes = slice(c * width, (c + 1) * width)

            def some(i):
                at = pl.multiple_of(i * 64, 64)
                y_all[pl.ds(at, 64), lanes] = y_one[pl.ds(c * n_tiles + at, 64), :].astype(jnp.bfloat16)

            each(n_tiles // 64, some)

    def start_half(g, staged, part, recv, sem):
        for i in range(n_y - staged if g == 0 else n_y - 1):
            k = g * n_y + i
            peer = me_z * n_y + lax.rem(me_y + 1 + i, n_y) if staged else place_of(k)
            to_src(peer, part.at[pl.ds(k * bd, bd)], recv.at[k], sem.at[0], sem.at[1 + g]).start()

    def finish(staged, part, recv, sem, far_sem):
        def half_sum(g, count):
            if count:
                take(recv.at[pl.ds(g * n_y, count)], sem.at[1 + g])
            total = part[(g * n_y + n_y - 1) * bd : (g + 1) * n_y * bd, :].astype(jnp.float32)
            for i in range(n_y - 1):
                total = total + recv[g * n_y + i].astype(jnp.float32)
            return total

        sent = n_src - 2 if staged else n_src - 1
        if staged:
            far_out[...] = half_sum(0, n_y - 1).astype(jnp.bfloat16)
            peer = lax.rem(me_z + 1, 2) * n_y + me_y
            far = to_src(peer, far_out, far_in, far_sem.at[0], far_sem.at[1])
            far.start()
            total = half_sum(1, n_y - 1)
            far.wait()
            total = total + far_in[...].astype(jnp.float32)
        else:
            take(recv.at[pl.ds(0, n_y)], sem.at[1])
            total = half_sum(1, n_y - 1)
            for k in range(n_y):
                total = total + recv[k].astype(jnp.float32)
        if sent:
            take(recv.at[pl.ds(0, sent)], sem.at[0])
        return total

    group = n_src // 2
    half = lambda g: slice(g * group * bd, (g + 1) * group * bd)

    def solve(which, total):
        for c in range(coefs):
            drive[pl.ds(c * bd, bd), :] = total[:, c * width : (c + 1) * width]

        some = min(64, bd)

        def pairs(turn):
            for i in range(some // 2):
                b = turn * some + 2 * i
                x0 = inc[which, b] - drive[pl.ds(b, coefs, stride=bd), :]
                x1 = inc[which, b + 1] - drive[pl.ds(b + 1, coefs, stride=bd), :]
                x = jnp.concatenate([x0, x1], axis=0).astype(jnp.bfloat16)
                both = jnp.dot(
                    x, jnp.concatenate([near[b], near[b + 1]], axis=1), preferred_element_type=jnp.float32
                )
                out_ref[which, b] = both[:coefs, :width].astype(jnp.bfloat16)
                out_ref[which, b + 1] = both[coefs:, width:].astype(jnp.bfloat16)

        each(bd // some, pairs)

    take(tile, tile_sem)
    info_down.wait()
    take_rows(send1, rows1, CAP, sem1)
    each(chunks, products(rows1))
    pack()
    for g in range(2):
        part1[half(g), :] = jnp.dot(
            pick1[half(g), :], y_all[...], preferred_element_type=jnp.float32
        ).astype(jnp.bfloat16)
        start_half(g, STAGED[0], part1, recv1, part_sem1)
    load_inc.wait()
    load_near.wait()
    for side in range(2):
        take(flags.at[pl.ds(0, n_src - 1)], flag_sem.at[side])
    solve(0, finish(STAGED[0], part1, recv1, part_sem1, far_sem1))

    newest = out_ref.at[0]
    placed = lambda c: jnp.bitwise_and(c, bd - 1)
    send_new = lambda k: send_rows(k, send0, rows0, CAP0, sem0)

    def gather_send_new(k):
        gather(newest, send0.at[k], obs_peer(k, n_obs), CAP0, AT0, placed)
        send_new(k).start()

    for k in order:
        gather_send_new(k)
    gather(newest, rows0.at[pl.ds(me_o * CAP0, CAP0)], me_o, CAP0, AT0, placed)
    take_rows(send2, rows2, CAP, sem2)
    each(chunks, products(rows2))
    pack()
    for g in range(2):
        part_old[half(g), :] = jnp.dot(pick2[half(g), :], y_all[...], preferred_element_type=jnp.float32)
    list_down.wait()
    take_rows(send0, rows0, CAP0, sem0)

    def new_products(turn):
        for i in range(0, 64, 2):
            r = turn * 64 + i
            two_products(
                rows0[lst[1, r]], rows0[lst[1, r + 1]], tile[lst[0, r]], tile[lst[0, r + 1]], y_new, CAPD, r
            )

    each(CAPD // 64, new_products)
    value = jnp.concatenate([y_new[c * CAPD : (c + 1) * CAPD, :] for c in range(coefs)], axis=1)
    value = value.astype(jnp.bfloat16)
    for g in range(2):
        added = jnp.dot(pick0[half(g), :], value, preferred_element_type=jnp.float32)
        part2[half(g), :] = (part_old[half(g), :] + added).astype(jnp.bfloat16)
        start_half(g, STAGED[1], part2, recv2, part_sem2)
    solve(1, finish(STAGED[1], part2, recv2, part_sem2, far_sem2))
    crowded_ref[0, 0] = jnp.max(flags[...])


def dense_path(tile_rows, index_rows, live_count, history, incident, near_inverse, n_src, n_obs):
    bd, width = near_inverse.shape[:2]
    slots, coefs = history.shape[:2]
    n_tiles = tile_rows.shape[0]
    group = min(64, n_tiles)

    def gather_obs(block):
        ring = [(i, (i + 1) % n_obs) for i in range(n_obs)]
        me = lax.axis_index("obs")
        whole = jnp.zeros((n_obs,) + block.shape, block.dtype)
        whole = lax.dynamic_update_index_in_dim(whole, block, me, 0)

        def hop(k, carry):
            whole, moving = carry
            whole = lax.dynamic_update_index_in_dim(whole, moving, lax.rem(me - k + n_obs, n_obs), 0)
            return whole, lax.ppermute(moving, "obs", ring)

        return lax.fori_loop(1, n_obs, hop, (whole, lax.ppermute(block, "obs", ring)))[0]

    def sum_src(value):
        ring = [(i, (i + 1) % n_src) for i in range(n_src)]

        def hop(k, carry):
            total, moving = carry
            moving = lax.ppermute(moving, "src", ring)
            return total + moving, moving

        return lax.fori_loop(0, n_src - 1, hop, (value, value))[0]

    def accumulate(chooser):
        def one_group(turn, partial):
            start = turn * group
            tile_part = lax.dynamic_slice_in_dim(tile_rows, start, group, 0)
            index_part = lax.dynamic_slice_in_dim(index_rows, start, group, 1)
            products = jnp.einsum(
                "gck,gki->gci", chooser(index_part), tile_part, preferred_element_type=jnp.float32
            )
            alive = start + jnp.arange(group, dtype=jnp.int32) < live_count
            products = jnp.where(alive[:, None, None], products, 0.0)
            return partial.at[index_part[0]].add(products)

        initial = jnp.zeros((bd * n_src, coefs, width), jnp.float32)
        return lax.fori_loop(0, n_tiles // group, one_group, initial)

    def settle(partial, drive):
        own = lax.dynamic_slice_in_dim(sum_src(partial), lax.axis_index("src") * bd, bd, 0)
        right = (drive - own).astype(jnp.bfloat16)
        solved = jnp.einsum("bck,bki->bci", right, near_inverse, preferred_element_type=jnp.float32)
        return solved.astype(jnp.bfloat16)

    past = gather_obs(history)

    def pick(block, index_part, slot):
        return past[index_part[1] // bd, slot, index_part[1] % bd]

    past = past.reshape(n_obs, slots, coefs, bd, width).transpose(0, 1, 3, 2, 4)
    first = settle(accumulate(lambda ip: pick(past, ip, ip[2])), incident[0])
    newest = gather_obs(first)

    def second_rows(ip):
        older = pick(past, ip, jnp.maximum(ip[2] - 1, 0))
        newer = newest[ip[1] // bd, ip[1] % bd]
        return jnp.where((ip[2] == 0)[:, None, None], newer, older)

    second = settle(accumulate(second_rows), incident[1])
    return jnp.stack([first, second])


def solution(mesh):
    n_src, n_obs = mesh.shape["src"], mesh.shape["obs"]
    vmem = pl.BlockSpec(memory_space=pltpu.VMEM)
    smem = pl.BlockSpec(memory_space=pltpu.SMEM)
    hbm = pl.BlockSpec(memory_space=pltpu.HBM)
    dma = pltpu.SemaphoreType.DMA
    f32, bf16, i32 = jnp.float32, jnp.bfloat16, jnp.int32

    def params(i):
        return pltpu.CompilerParams(collective_id=i, has_side_effects=True)

    def on_device(tiles, tile_index, tile_count, history, incident, near_inverse):
        n_tiles, width = tiles.shape[2], tiles.shape[4]
        bd = near_inverse.shape[0]
        slots, coefs = history.shape[:2]
        tile_rows = tiles.reshape(n_tiles, width, width)
        index_rows = tile_index.transpose(0, 2, 1, 3).reshape(3, 1, n_tiles)
        hist = history.reshape(slots, coefs, bd, width).transpose(0, 2, 1, 3).reshape(slots * bd, coefs, width)
        drive = incident.reshape(2, coefs, bd, width).transpose(0, 2, 1, 3)

        def rows(cap):
            return pltpu.VMEM((n_obs * cap, coefs, width), bf16)

        def sends(cap):
            return pltpu.VMEM((n_obs, cap, coefs, width), bf16)

        def parts(kind):
            return pltpu.VMEM((n_src * bd, coefs * width), kind)

        arrived = pltpu.VMEM((n_src, bd, coefs * width), bf16)

        both, crowded = pl.pallas_call(
            functools.partial(step_kernel, n_src, n_obs, bd),
            name="step",
            out_shape=(
                jax.ShapeDtypeStruct((2, bd, coefs, width), bf16),
                jax.ShapeDtypeStruct((1, 1), f32),
            ),
            in_specs=[vmem, vmem, hbm, hbm, hbm, hbm],
            out_specs=(vmem, smem),
            scratch_shapes=[
                pltpu.VMEM((n_obs, 1, 128), i32), pltpu.VMEM((n_obs, 1, 128), i32),
                pltpu.VMEM((8, n_tiles), i32), pltpu.VMEM((8, 128), i32),
                pltpu.SMEM((n_obs, 1, 128), i32), pltpu.SMEM((8, n_tiles), i32), pltpu.SMEM((8, 128), i32),
                pltpu.VMEM((n_src, 1, 128), f32),
                pltpu.VMEM((n_tiles, width, width), bf16),
                pltpu.VMEM(hist.shape, bf16),
                pltpu.VMEM(drive.shape, f32),
                pltpu.VMEM((bd, width, width), bf16),
                rows(CAP), rows(CAP), rows(CAP0), sends(CAP), sends(CAP), sends(CAP0),
                pltpu.VMEM((1, 128), f32),
                pltpu.VMEM((coefs * n_tiles, width), f32),
                pltpu.VMEM((n_tiles, coefs * width), bf16),
                pltpu.VMEM((coefs * CAPD, width), f32),
                pltpu.VMEM((n_src * bd, n_tiles), bf16),
                pltpu.VMEM((n_src * bd, n_tiles), bf16),
                pltpu.VMEM((n_src * bd, CAPD), bf16),
                parts(f32), parts(bf16), parts(bf16), arrived, arrived,
                pltpu.VMEM((bd, coefs * width), bf16), pltpu.VMEM((bd, coefs * width), bf16),
                pltpu.VMEM((coefs * bd, width), f32),
                dma, dma((6,)), dma((2,)), dma((2,)), dma((2,)), dma((2,)), dma((2,)), dma((3,)), dma((3,)), dma((2,)), dma((2,)),
            ],
            compiler_params=params(0),
        )(tile_count, index_rows, tile_rows, hist, drive, near_inverse)

        both = lax.cond(
            crowded[0, 0] > 0.0,
            lambda kept: dense_path(
                tile_rows, tile_index.reshape(3, n_tiles), tile_count.reshape(()), history, drive, near_inverse,
                n_src, n_obs,
            ),
            lambda kept: kept,
            both,
        )
        return both.transpose(0, 2, 1, 3).reshape(2, coefs, bd * width)

    in_specs = (
        P("src", "obs", None, None, None),
        P("src", "obs", None, None),
        P("src", "obs"),
        P(None, None, ("src", "obs")),
        P(None, None, ("src", "obs")),
        P(("src", "obs"), None, None),
    )
    out_specs = P(None, None, ("src", "obs"))
    return jax.shard_map(on_device, mesh=mesh, in_specs=in_specs, out_specs=out_specs, check_vma=False)
```
